32 devices in a mesh: seq: 8 (over y, x, core), tp: 4 (over z).
Axes of the slice: x: 2, y: 2, z: 4, core: 2. Of those that a mesh axis runs over, the one named last changes fastest.
Arguments:
- byte_states: bfloat16 [2048, 1024], P('seq'), may hold values from -6 to 6
- enc_gain: bfloat16 [1024], replicated, may hold values from 0.25 to 1.75
- enc_qkv: bfloat16 [3, 1024, 1024], P(None, None, 'tp')
- enc_proj_out: bfloat16 [1024, 1024], P('tp'), may hold values from -0.1875 to 0.1875
- starts: int32 [8, 64], P('seq'), may hold values from 0 to 2048, as said below
- counts: int32 [8], P('seq'), may hold values from 32 to 64, as said below
- lift: bfloat16 [1024, 4096], P(None, 'tp')
- cross_kv: bfloat16 [2, 1024, 4096], P(None, None, 'tp')
- latent_gain: bfloat16 [4096], replicated, may hold values from 0.25 to 1.75
- lat_qkv: bfloat16 [3, 4096, 2048], P(None, 'seq', 'tp')
- lat_proj_out: bfloat16 [2048, 4096], P('tp', 'seq'), may hold values from -0.75 to 0.75
Outputs:
- byte_out: bfloat16 [2048, 1024], P('seq')
- latent_out: bfloat16 [512, 4096], P('seq', 'tp')
The draws below stay inside these ranges and needn't reach their ends.
Inputs may be any that keep to these rules, and one draw needn't show every extreme that they name: `starts`: row s lists in increasing order the first byte (counted over all 2048 bytes) of each patch beginning in bytes s * 256 to (s + 1) * 256 - 1, then 2048 in unused places. Byte 0 begins a patch; every row's first patch begins fewer than 8 bytes into its block, and in some row exactly 7 bytes in. counts[s] is the number of patches listed in row s of starts; some row holds 64.
All inputs are finite; a program needn't handle non-finite values.
Results may differ from the reference program's by a relative error of at most 0.018.
Values may be sent and summed in bfloat16 or wider, within the bound.
A program may use at most 128 MiB of HBM per device.

```python
import math
import jax
import jax.numpy as jnp
from jax import lax

DE = 1024
EH = 64
D = 4096
HD = 128
HL = 16
WIN = 512
SPILL = 8
B_DEV = 256
BYTES = 2048
P_CAP = 64
C_MIN = 32
N_SEQ = 8


def patch_table(key):
    stream = jax.random.fold_in(key, 11)
    split_keys = jax.random.split(stream, 5)
    spill_row = jax.random.randint(split_keys[0], (), 1, N_SEQ)
    full_row = (spill_row + jax.random.randint(split_keys[1], (), 1, N_SEQ)) % N_SEQ
    spread = P_CAP - C_MIN
    first_draw = jax.random.randint(split_keys[2], (N_SEQ,), 0, spread + 1)
    second_draw = jax.random.randint(split_keys[3], (N_SEQ,), 0, spread + 1)
    amounts = P_CAP - first_draw * second_draw // spread
    row_ids = jnp.arange(N_SEQ, dtype=jnp.int32)
    amounts = jnp.where(row_ids == full_row, P_CAP, jnp.where(row_ids == spill_row, C_MIN, amounts))
    slot_ids = jnp.arange(P_CAP, dtype=jnp.int32)
    lower_edge = slot_ids[None, :] * B_DEV // amounts[:, None]
    upper_edge = (slot_ids[None, :] + 1) * B_DEV // amounts[:, None]
    span_sizes = jnp.maximum(upper_edge - lower_edge, 1)
    jitter = jax.random.randint(split_keys[4], (N_SEQ, P_CAP), 0, span_sizes)
    first_col = slot_ids[None, :] == 0
    jitter = jnp.where(first_col & (row_ids[:, None] == spill_row), span_sizes - 1, jitter)
    jitter = jnp.where(first_col & (row_ids[:, None] == 0), 0, jitter)
    start_table = jnp.where(slot_ids[None, :] < amounts[:, None], row_ids[:, None] * B_DEV + lower_edge + jitter, BYTES)
    return (start_table.astype(jnp.int32), amounts.astype(jnp.int32))


def draw_starts(key, part):
    return patch_table(key)[0]


def draw_counts(key, part):
    return patch_table(key)[1]


def weight_block(key, shape, fan_in):
    multiplier = 1.0 / math.sqrt(fan_in)
    return jax.random.truncated_normal(key, -4.0, 4.0, shape, jnp.float32) * multiplier


def draw_byte_states(key, part):
    independent = jax.random.normal(jax.random.fold_in(key, 21), (BYTES, DE), jnp.float32)
    values = independent
    return jnp.clip(values, -6.0, 6.0).astype(jnp.bfloat16)


def draw_enc_qkv(key, part):
    query_cols = weight_block(jax.random.fold_in(key, 31), (DE, DE), DE)
    key_cols = weight_block(jax.random.fold_in(key, 32), (DE, DE), DE)
    value_cols = weight_block(jax.random.fold_in(key, 33), (DE, DE), DE)
    return jnp.stack([query_cols, key_cols, value_cols]).astype(jnp.bfloat16)


def cross_tables(key):
    stream = jax.random.fold_in(key, 41)
    lift_cols = weight_block(jax.random.fold_in(stream, 1), (DE, D), DE)
    key_cols = weight_block(jax.random.fold_in(stream, 2), (DE, D), DE)
    value_cols = weight_block(jax.random.fold_in(stream, 3), (DE, D), DE)
    return (lift_cols, jnp.stack([key_cols, value_cols]))


def draw_lift(key, part):
    return cross_tables(key)[0].astype(jnp.bfloat16)


def draw_cross_kv(key, part):
    return cross_tables(key)[1].astype(jnp.bfloat16)


def draw_lat_qkv(key, part):
    query_cols = weight_block(jax.random.fold_in(key, 51), (D, HL * HD), D)
    key_cols = weight_block(jax.random.fold_in(key, 52), (D, HL * HD), D)
    value_cols = weight_block(jax.random.fold_in(key, 53), (D, HL * HD), D)
    return jnp.stack([query_cols, key_cols, value_cols]).astype(jnp.bfloat16)


def shard_levels(key, shape, pieces, low, high):
    loudness, own = 1.0, jax.random.fold_in(key, 6)
    for dim, blocks in pieces:
        heights = jnp.exp(jax.random.uniform(jax.random.fold_in(own, dim), (blocks,), jnp.float32, low / len(pieces), high / len(pieces)))
        loudness = loudness * jnp.repeat(heights, shape[dim] // blocks).reshape([-1 if axis == dim else 1 for axis in range(len(shape))])
    return loudness


def bell_draw(rng, shape, deviation, limit, cuts=(), held_as=jnp.bfloat16):
    result = jax.random.normal(rng, shape, jnp.float32) * deviation
    if len(cuts) > 0:
        result = shard_levels(rng, shape, cuts, -0.22, 0.18) * result
    return jnp.clip(result, min=-limit, max=limit).astype(held_as)


def setup_inputs(seed: int = 0) -> dict:
    splits = jax.random.split(jax.random.key(seed), 12)
    byte_states = draw_byte_states(jax.random.fold_in(splits[11], 71), 0)
    enc_gain = jnp.clip(1.0 + 0.15 * jax.random.normal(splits[1], (DE,), jnp.float32), 0.25, 1.75).astype(jnp.bfloat16)
    enc_qkv = draw_enc_qkv(jax.random.fold_in(splits[11], 71), 0)
    enc_proj_out = bell_draw(splits[3], (DE, DE), DE ** -0.5, 0.1875, ((0, 4),))
    starts = draw_starts(jax.random.fold_in(splits[11], 71), 0)
    counts = draw_counts(jax.random.fold_in(splits[11], 71), 0)
    lift = draw_lift(jax.random.fold_in(splits[11], 71), 0)
    cross_kv = draw_cross_kv(jax.random.fold_in(splits[11], 71), 0)
    latent_gain = jnp.clip(1.0 + 0.15 * jax.random.normal(splits[8], (D,), jnp.float32), 0.25, 1.75).astype(jnp.bfloat16)
    lat_qkv = draw_lat_qkv(jax.random.fold_in(splits[11], 71), 0)
    lat_proj_out = bell_draw(splits[10], (HL * HD, D), (HL * HD // 32) ** -0.5, 0.75, ((0, 4), (1, 8)))
    return dict(byte_states=byte_states, enc_gain=enc_gain, enc_qkv=enc_qkv, enc_proj_out=enc_proj_out, starts=starts, counts=counts, lift=lift, cross_kv=cross_kv, latent_gain=latent_gain, lat_qkv=lat_qkv, lat_proj_out=lat_proj_out)


epsilon = 1e-05
rope_base = 500000.0
far_position = 1 << 30

def rms_scale(values, gain_row):
    mean_square = lax.optimization_barrier(jnp.mean(values * values, axis=-1, keepdims=True))
    return values * lax.rsqrt(mean_square + epsilon) * gain_row

def masked_softmax(scores, allowed):
    scores = jnp.where(allowed, scores, -1e+30)
    largest = lax.optimization_barrier(jnp.max(scores, axis=-1, keepdims=True))
    raised = jnp.where(allowed, jnp.exp(scores - largest), 0.0)
    return raised / lax.optimization_barrier(jnp.sum(raised, axis=-1, keepdims=True))

def rotate(values, position):
    halfway = values.shape[-1] // 2
    frequency = jnp.power(rope_base, -2.0 * jnp.arange(halfway, dtype=jnp.float32) / values.shape[-1])
    angles = position.astype(jnp.float32)[:, None] * frequency[None, :]
    cosine = jnp.cos(angles)[:, None, :]
    sine_rows = jnp.sin(angles)[:, None, :]
    lower_half = values[..., :halfway]
    upper_half = values[..., halfway:]
    return jnp.concatenate([lower_half * cosine - upper_half * sine_rows, upper_half * cosine + lower_half * sine_rows], axis=-1)

def encoder_layer(byte_states, enc_gain, enc_qkv, enc_proj_out):
    states = byte_states.astype(jnp.float32)
    normed = rms_scale(states, enc_gain.astype(jnp.float32)).astype(jnp.bfloat16)
    projected = jnp.einsum('bd,idc->ibc', normed.astype(jnp.float32), enc_qkv.astype(jnp.float32)).astype(jnp.bfloat16)
    head_count = projected.shape[2] // EH
    padding = jnp.zeros((WIN, projected.shape[2]), jnp.bfloat16)
    key_rows = jnp.concatenate([padding, projected[1]], axis=0)
    value_rows = jnp.concatenate([padding, projected[2]], axis=0)

    def attend(block_id):
        opening = block_id * WIN
        queries = lax.dynamic_slice_in_dim(projected[0], opening, WIN, 0).reshape(WIN, head_count, EH).astype(jnp.float32)
        near_keys = lax.dynamic_slice_in_dim(key_rows, opening, 2 * WIN, 0).reshape(2 * WIN, head_count, EH).astype(jnp.float32)
        near_values = lax.dynamic_slice_in_dim(value_rows, opening, 2 * WIN, 0).reshape(2 * WIN, head_count, EH).astype(jnp.float32)
        scores = jnp.einsum('qhd,khd->hqk', queries, near_keys) * (1.0 / math.sqrt(EH))
        query_pos = opening + jnp.arange(WIN, dtype=jnp.int32)
        key_pos = opening - WIN + jnp.arange(2 * WIN, dtype=jnp.int32)
        allowed = (key_pos[None, :] <= query_pos[:, None]) & (key_pos[None, :] > query_pos[:, None] - WIN) & (key_pos[None, :] >= 0)
        weights = masked_softmax(scores, allowed[None]).astype(jnp.bfloat16)
        attended = jnp.einsum('hqk,khd->qhd', weights.astype(jnp.float32), near_values)
        return attended.reshape(WIN, head_count * EH).astype(jnp.bfloat16)
    attended = lax.map(attend, jnp.arange(BYTES // WIN, dtype=jnp.int32)).reshape(BYTES, -1)
    return (states + jnp.dot(attended, enc_proj_out, preferred_element_type=jnp.float32)).astype(jnp.bfloat16)

def patch_block(extended, first_byte, end_byte, in_use, anchor, lift, cross_kv):
    columns = anchor + jnp.arange(extended.shape[0], dtype=jnp.int32)
    inside = (columns[None, :] >= first_byte[:, None]) & (columns[None, :] < end_byte[:, None]) & in_use[:, None]
    member = inside.astype(jnp.bfloat16)
    totals = jnp.dot(member, extended, preferred_element_type=jnp.float32)
    lengths = jnp.maximum(lax.optimization_barrier(jnp.sum(inside.astype(jnp.float32), axis=1)), 1.0)
    pooled = (totals / lengths[:, None]).astype(jnp.bfloat16)
    lifted = jnp.dot(pooled, lift, preferred_element_type=jnp.float32)
    key_rows = jnp.dot(extended, cross_kv[0], preferred_element_type=jnp.float32).astype(jnp.bfloat16)
    value_rows = jnp.dot(extended, cross_kv[1], preferred_element_type=jnp.float32).astype(jnp.bfloat16)
    slot_total = first_byte.shape[0]
    head_count = lifted.shape[1] // HD
    queries = lifted.astype(jnp.bfloat16).reshape(slot_total, head_count, HD)
    scores = jnp.einsum('phd,khd->hpk', queries.astype(jnp.float32), key_rows.reshape(-1, head_count, HD).astype(jnp.float32)) * (1.0 / math.sqrt(HD))
    allowed = inside | (~in_use)[:, None] & (columns[None, :] == anchor)
    weights = masked_softmax(scores, allowed[None]).astype(jnp.bfloat16)
    crossed = jnp.einsum('hpk,khd->phd', weights.astype(jnp.float32), value_rows.reshape(-1, head_count, HD).astype(jnp.float32))
    crossed = crossed.reshape(slot_total, head_count * HD)
    return jnp.where(in_use[:, None], lifted + crossed, 0.0).astype(jnp.bfloat16)

def latent_layer(patch_rows, in_use, position, latent_gain, lat_qkv, lat_proj_out):
    states = patch_rows.astype(jnp.float32)
    normed = rms_scale(states, latent_gain.astype(jnp.float32)).astype(jnp.bfloat16)
    projected = jnp.einsum('pd,idc->ipc', normed.astype(jnp.float32), lat_qkv.astype(jnp.float32))
    row_total = patch_rows.shape[0]
    head_count = projected.shape[2] // HD
    queries = rotate(projected[0].reshape(row_total, head_count, HD), position).astype(jnp.bfloat16)
    key_rows = rotate(projected[1].reshape(row_total, head_count, HD), position).astype(jnp.bfloat16)
    value_rows = projected[2].reshape(row_total, head_count, HD).astype(jnp.bfloat16)
    key_pos = jnp.where(in_use, position, far_position)
    allowed = key_pos[None, :] <= position[:, None]

    def attend(head_rows):
        query_head, key_head, value_head = head_rows
        scores = jnp.dot(query_head, key_head.T, preferred_element_type=jnp.float32) * (1.0 / math.sqrt(HD))
        weights = masked_softmax(scores, allowed).astype(jnp.bfloat16)
        return jnp.dot(weights, value_head, preferred_element_type=jnp.float32).astype(jnp.bfloat16)
    attended = lax.map(attend, (queries.transpose(1, 0, 2), key_rows.transpose(1, 0, 2), value_rows.transpose(1, 0, 2)))
    attended = attended.transpose(1, 0, 2).reshape(row_total, head_count * HD)
    summed = states + jnp.dot(attended, lat_proj_out, preferred_element_type=jnp.float32)
    return jnp.where(in_use[:, None], summed, 0.0).astype(jnp.bfloat16)

def reference(byte_states, enc_gain, enc_qkv, enc_proj_out, starts, counts, lift, cross_kv, latent_gain, lat_qkv, lat_proj_out):
    encoded = encoder_layer(byte_states, enc_gain, enc_qkv, enc_proj_out)
    anchors = jnp.arange(N_SEQ, dtype=jnp.int32) * B_DEV
    first_local = starts[:, 0] - anchors
    next_first = jnp.concatenate([first_local[1:], jnp.zeros((1,), jnp.int32)])
    slot_ids = jnp.arange(P_CAP, dtype=jnp.int32)
    in_use = slot_ids[None, :] < counts[:, None]
    following = jnp.concatenate([starts[:, 1:], jnp.zeros((N_SEQ, 1), jnp.int32)], axis=1)
    patch_end = jnp.where(slot_ids[None, :] + 1 < counts[:, None], following, (anchors + B_DEV + next_first)[:, None])
    padded = jnp.concatenate([encoded, jnp.zeros((SPILL, DE), jnp.bfloat16)], axis=0)

    def one_shard(shard_items):
        anchor, first_byte, end_byte, shard_use = shard_items
        extended = lax.dynamic_slice_in_dim(padded, anchor, B_DEV + SPILL, 0)
        return patch_block(extended, first_byte, end_byte, shard_use, anchor, lift, cross_kv)
    patches = lax.map(one_shard, (anchors, starts, patch_end, in_use)).reshape(N_SEQ * P_CAP, -1)
    offsets = (jnp.cumsum(counts) - counts).astype(jnp.int32)
    position = (offsets[:, None] + slot_ids[None, :]).reshape(-1).astype(jnp.int32)
    latent = latent_layer(patches, in_use.reshape(-1), position, latent_gain, lat_qkv, lat_proj_out)
    return (encoded, latent)
```

```python
import math

import jax
import jax.numpy as jnp
from jax import lax
from jax.experimental import pallas as pl
from jax.experimental.pallas import tpu as pltpu
from jax.sharding import PartitionSpec as P

EH = 64
HD = 128
WIN = 512
SPILL = 8


epsilon = 1e-05
rope_base = 500000.0
far_position = 1 << 30


def from_behind(value, axis, steps):
    count = lax.axis_size(axis)
    leading, last = (max(0, -steps), min(count, count - steps))
    return lax.ppermute(value, axis, [(source, source + steps) for source in range(leading, last)])


def prefix(value, axis, join, neutral):
    count, mine = (lax.axis_size(axis), lax.axis_index(axis))
    pieces = lax.all_gather(value, axis)
    subtotal = jnp.full_like(value, 0) + jnp.asarray(neutral, value.dtype)

    def hop(position, subtotal):
        longer = join(subtotal, pieces[position])
        return jnp.where(position < mine, longer, subtotal)

    return lax.fori_loop(0, count - 1, hop, subtotal)


def shortened(value):

    def short(part):
        return part.astype(jnp.bfloat16) if part.dtype == jnp.float32 else part

    return jax.tree.map(short, value)


def rms_scale(values, gain_row):
    mean_square = jnp.mean(values * values, axis=-1, keepdims=True)
    return values * lax.rsqrt(mean_square + epsilon) * gain_row


def masked_softmax(scores, allowed):
    scores = jnp.where(allowed, scores, -1e30)
    largest = jnp.max(scores, axis=-1, keepdims=True)
    raised = jnp.where(allowed, jnp.exp(scores - largest), 0.0)
    return raised / jnp.sum(raised, axis=-1, keepdims=True)


def rotate(values, position):
    halfway = values.shape[-1] // 2
    frequency = jnp.power(
        rope_base, -2.0 * jnp.arange(halfway, dtype=jnp.float32) / values.shape[-1]
    )
    angles = position.astype(jnp.float32)[:, None] * frequency[None, :]
    cosine = jnp.cos(angles)[:, None, :]
    sine_rows = jnp.sin(angles)[:, None, :]
    lower_half = values[..., :halfway]
    upper_half = values[..., halfway:]
    return jnp.concatenate(
        [
            lower_half * cosine - upper_half * sine_rows,
            upper_half * cosine + lower_half * sine_rows,
        ],
        axis=-1,
    )


def patch_block(extended, first_byte, end_byte, in_use, anchor, lift, cross_kv):
    columns = anchor + jnp.arange(extended.shape[0], dtype=jnp.int32)
    inside = (
        (columns[None, :] >= first_byte[:, None])
        & (columns[None, :] < end_byte[:, None])
        & in_use[:, None]
    )
    member = inside.astype(jnp.bfloat16)
    totals = jnp.dot(member, extended, preferred_element_type=jnp.float32)
    lengths = jnp.maximum(jnp.sum(inside.astype(jnp.float32), axis=1), 1.0)
    pooled = (totals / lengths[:, None]).astype(jnp.bfloat16)
    lifted = jnp.dot(pooled, lift, preferred_element_type=jnp.float32)
    key_rows = jnp.dot(extended, cross_kv[0], preferred_element_type=jnp.float32).astype(
        jnp.bfloat16
    )
    value_rows = jnp.dot(extended, cross_kv[1], preferred_element_type=jnp.float32).astype(
        jnp.bfloat16
    )
    slot_total = first_byte.shape[0]
    head_count = lifted.shape[1] // HD
    queries = lifted.astype(jnp.bfloat16).reshape(slot_total, head_count, HD)
    scores = jnp.einsum(
        "phd,khd->hpk",
        queries,
        key_rows.reshape(-1, head_count, HD),
        preferred_element_type=jnp.float32,
    ) * (1.0 / math.sqrt(HD))
    allowed = inside | (~in_use)[:, None] & (columns[None, :] == anchor)
    weights = masked_softmax(scores, allowed[None]).astype(jnp.bfloat16)
    crossed = jnp.einsum(
        "hpk,khd->phd",
        weights,
        value_rows.reshape(-1, head_count, HD),
        preferred_element_type=jnp.float32,
    )
    crossed = crossed.reshape(slot_total, head_count * HD)
    return jnp.where(in_use[:, None], lifted + crossed, 0.0).astype(jnp.bfloat16)


def add_counts(earlier, later):
    return earlier + later


def gathered_shards(
    byte_states,
    enc_gain,
    enc_qkv,
    enc_proj_out,
    starts,
    counts,
    lift,
    cross_kv,
    latent_gain,
    lat_qkv,
    lat_proj_out,
):
    byte_rows = byte_states.shape[0]
    anchor = lax.axis_index("seq") * byte_rows
    states = byte_states.astype(jnp.float32)
    normed = rms_scale(states, enc_gain.astype(jnp.float32)).astype(jnp.bfloat16)
    projected = jnp.einsum(
        "bd,idc->ibc", normed, enc_qkv, preferred_element_type=jnp.float32
    ).astype(jnp.bfloat16)
    reach_blocks = max(WIN // byte_rows, 1)
    tail_rows = min(WIN, byte_rows)
    key_parts = []
    value_parts = []
    for distance in range(reach_blocks, 0, -1):
        moved_keys, moved_values = from_behind(
            (projected[1, byte_rows - tail_rows :], projected[2, byte_rows - tail_rows :]),
            "seq",
            distance,
        )
        key_parts.append(moved_keys)
        value_parts.append(moved_values)
    key_rows = jnp.concatenate(key_parts + [projected[1]], axis=0)
    value_rows = jnp.concatenate(value_parts + [projected[2]], axis=0)
    head_count = projected.shape[2] // EH
    scores = jnp.einsum(
        "qhd,khd->hqk",
        projected[0].reshape(byte_rows, head_count, EH),
        key_rows.reshape(-1, head_count, EH),
        preferred_element_type=jnp.float32,
    ) * (1.0 / math.sqrt(EH))
    query_pos = anchor + jnp.arange(byte_rows, dtype=jnp.int32)
    key_pos = anchor - WIN + jnp.arange(WIN + byte_rows, dtype=jnp.int32)
    allowed = (
        (key_pos[None, :] <= query_pos[:, None])
        & (key_pos[None, :] > query_pos[:, None] - WIN)
        & (key_pos[None, :] >= 0)
    )
    weights = masked_softmax(scores, allowed[None]).astype(jnp.bfloat16)
    attended = jnp.einsum(
        "hqk,khd->qhd",
        weights,
        value_rows.reshape(-1, head_count, EH),
        preferred_element_type=jnp.float32,
    )
    attended = attended.reshape(byte_rows, head_count * EH).astype(jnp.bfloat16)
    blended = lax.psum(jnp.dot(attended, enc_proj_out, preferred_element_type=jnp.float32), "tp")
    encoded = (states + blended).astype(jnp.bfloat16)
    patch_count = counts[0]
    local_starts = starts[0]
    first_local = (local_starts[0:1] - anchor).astype(jnp.bfloat16)
    next_rows, next_first = from_behind((encoded[:SPILL], first_local), "seq", -1)
    next_first = next_first.astype(jnp.int32)[0]
    extended = jnp.concatenate([encoded, next_rows], axis=0)
    slot_ids = jnp.arange(local_starts.shape[0], dtype=jnp.int32)
    in_use = slot_ids < patch_count
    following = jnp.concatenate([local_starts[1:], jnp.zeros((1,), jnp.int32)])
    patch_end = jnp.where(slot_ids + 1 < patch_count, following, anchor + byte_rows + next_first)
    patches = patch_block(extended, local_starts, patch_end, in_use, anchor, lift, cross_kv)
    offset = prefix(counts, "seq", add_counts, jnp.zeros((1,), jnp.int32))[0]
    position = offset + slot_ids
    slot_total = patches.shape[0]
    full_rows = lax.all_gather(patches, "tp", axis=1, tiled=True)
    normed_rows = rms_scale(full_rows.astype(jnp.float32), latent_gain.astype(jnp.float32)).astype(
        jnp.bfloat16
    )
    inner_width = lat_qkv.shape[2]
    projected = jnp.einsum(
        "pd,idc->ipc",
        normed_rows,
        lax.all_gather(lat_qkv, "seq", axis=1, tiled=True),
        preferred_element_type=jnp.float32,
    )
    heads_here = inner_width // HD
    queries = rotate(projected[0].reshape(slot_total, heads_here, HD), position).astype(
        jnp.bfloat16
    )
    latent_keys = (
        rotate(projected[1].reshape(slot_total, heads_here, HD), position)
        .astype(jnp.bfloat16)
        .reshape(slot_total, inner_width)
    )
    latent_values = projected[2].astype(jnp.bfloat16)
    latent_pos = jnp.where(in_use, position, far_position)
    largest = jnp.full((heads_here, slot_total), -1e30, jnp.float32)
    piece_keys = lax.all_gather(latent_keys, "seq", axis=0, tiled=True)
    piece_values = lax.all_gather(latent_values, "seq", axis=0, tiled=True)
    piece_pos = lax.all_gather(shortened(latent_pos), "seq", axis=0, tiled=True)
    rows_here = piece_keys.shape[0]
    piece_scores = jnp.einsum(
        "qhd,khd->hqk",
        queries,
        piece_keys.reshape(rows_here, heads_here, HD),
        preferred_element_type=jnp.float32,
    ) * (1.0 / math.sqrt(HD))
    permitted = (piece_pos[None, :] <= position[:, None])[None]
    piece_scores = jnp.where(permitted, piece_scores, -1e30)
    renewed = jnp.maximum(largest, jnp.max(piece_scores, axis=-1))
    raised = jnp.where(permitted, jnp.exp(piece_scores - renewed[..., None]), 0.0)
    weight_sum = jnp.sum(raised, axis=-1)
    weighted = jnp.einsum(
        "hqk,khd->hqd",
        raised.astype(jnp.bfloat16),
        piece_values.reshape(rows_here, heads_here, HD),
        preferred_element_type=jnp.float32,
    )
    largest, weight_sum, weighted = (renewed, weight_sum, weighted)
    latent_heads = (
        (weighted / weight_sum[..., None])
        .transpose(1, 0, 2)
        .reshape(slot_total, inner_width)
        .astype(jnp.bfloat16)
    )
    partials = jnp.dot(
        latent_heads,
        lax.all_gather(lat_proj_out, "seq", axis=1, tiled=True),
        preferred_element_type=jnp.float32,
    )
    reduced = lax.psum_scatter(partials, "tp", scatter_dimension=1, tiled=True)
    latent = jnp.where(in_use[:, None], patches.astype(jnp.float32) + reduced, 0.0).astype(
        jnp.bfloat16
    )
    return (encoded, latent)


MESH = pl.DeviceIdType.MESH
EDGE = 16


def greet(peers):
    barrier = pltpu.get_barrier_semaphore()
    for peer in peers:
        pl.semaphore_signal(barrier, inc=1, device_id=peer, device_id_type=MESH)
    pl.semaphore_wait(barrier, len(peers))


def exchange(values, out_shapes, plan, call_id):
    n_in, n_out = len(values), len(out_shapes)
    n_copies = 16

    def kernel(*refs):
        ins, outs = refs[:n_in], refs[n_in : n_in + n_out]
        send_sems, recv_sems = refs[n_in + n_out :]
        rounds = plan()
        greet([source for source, _, _ in rounds])
        copies = []
        for _, target, items in rounds:
            for in_id, in_view, out_id, out_view in items:
                copy = pltpu.make_async_remote_copy(
                    src_ref=in_view(ins[in_id]),
                    dst_ref=out_view(outs[out_id]),
                    send_sem=send_sems.at[len(copies)],
                    recv_sem=recv_sems.at[len(copies)],
                    device_id=target,
                    device_id_type=MESH,
                )
                copy.start()
                copies.append(copy)
        for copy in copies:
            copy.wait()

    return pl.pallas_call(
        kernel,
        out_shape=out_shapes,
        in_specs=[pl.BlockSpec(memory_space=pl.ANY)] * n_in,
        out_specs=[pl.BlockSpec(memory_space=pl.ANY)] * n_out,
        scratch_shapes=[
            pltpu.SemaphoreType.DMA((n_copies,)),
            pltpu.SemaphoreType.DMA((n_copies,)),
        ],
        compiler_params=pltpu.CompilerParams(collective_id=call_id, has_side_effects=True),
    )(*values)


def whole(ref):
    return ref


def slot(index):
    return lambda ref: ref.at[index]


def seq_peer(index):
    return {"seq": index}


def tp_peer(index):
    return {"tp": index}


def relay(value, count, spread, plane_first, call_id):
    block = value.shape[1:] if spread else value.shape

    def kernel(value_ref, out_ref, land, send_a, recv_a, send_b, recv_b, own_sem):
        s, t = lax.axis_index("seq"), lax.axis_index("tp")
        p, c = s // 2, lax.rem(s, 2)

        def plane(index):
            return {"seq": 2 * index + c}

        if plane_first:
            a, b, first, second = p, t, plane, tp_peer
        else:
            a, b, first, second = t, p, tp_peer, plane
        others_a = [lax.rem(a + k, count) for k in range(1, count)]
        others_b = [lax.rem(b + k, count) for k in range(1, count)]
        greet([first(i) for i in others_a] + [second(i) for i in others_b])
        hops = []
        for k in range(1, count):
            target = lax.rem(a + k, count)
            hop = pltpu.make_async_remote_copy(
                src_ref=value_ref.at[target] if spread else value_ref,
                dst_ref=land.at[k - 1],
                send_sem=send_a.at[k - 1],
                recv_sem=recv_a.at[k - 1],
                device_id=first(target),
                device_id_type=MESH,
            )
            hop.start()
            hops.append(hop)
        onward = []
        for k in range(count):
            origin = lax.rem(a + count - k, count)
            if k == 0:
                here = value_ref.at[a] if spread else value_ref
            else:
                hops[k - 1].wait_recv()
                here = land.at[k - 1]
            away = pltpu.make_async_remote_copy(
                src_ref=here,
                dst_ref=out_ref.at[b],
                send_sem=send_b.at[k],
                recv_sem=recv_b.at[b],
                device_id=second(origin),
                device_id_type=MESH,
            )
            stay = pltpu.make_async_copy(here, out_ref.at[b], own_sem)
            onward.append((origin, away, stay))

            @pl.when(origin != b)
            def _():
                away.start()

            @pl.when(origin == b)
            def _():
                stay.start()

        for q in range(count):

            @pl.when(b != q)
            def _():
                pltpu.make_async_remote_copy(
                    src_ref=land.at[0],
                    dst_ref=out_ref.at[q],
                    send_sem=send_b.at[q],
                    recv_sem=recv_b.at[q],
                    device_id=second(b),
                    device_id_type=MESH,
                ).wait_recv()

        for hop in hops:
            hop.wait_send()
        for origin, away, stay in onward:

            @pl.when(origin != b)
            def _():
                away.wait_send()

            @pl.when(origin == b)
            def _():
                stay.wait()

    return pl.pallas_call(
        kernel,
        out_shape=jax.ShapeDtypeStruct((count, *block), value.dtype),
        in_specs=[pl.BlockSpec(memory_space=pltpu.VMEM)],
        out_specs=pl.BlockSpec(memory_space=pl.ANY),
        scratch_shapes=[
            pltpu.VMEM((count - 1, *block), value.dtype),
            pltpu.SemaphoreType.DMA((count - 1,)),
            pltpu.SemaphoreType.DMA((count - 1,)),
            pltpu.SemaphoreType.DMA((count,)),
            pltpu.SemaphoreType.DMA((count,)),
            pltpu.SemaphoreType.DMA,
        ],
        compiler_params=pltpu.CompilerParams(collective_id=call_id, has_side_effects=True),
    )(value)


def like(shape, dtype=jnp.bfloat16):
    return jax.ShapeDtypeStruct(shape, dtype)


def halo(projected, byte_states, info):
    size = lax.axis_size("seq")
    rows, width = projected.shape[1:]
    reach = WIN // rows

    def plan():
        s = lax.axis_index("seq")
        rounds = []
        for k in range(1, size):
            items = []
            if k <= reach:
                items.append((0, lambda ref: ref.at[pl.ds(1, 2)], 0, slot(k - 1)))
            if k == size - 1:
                items.append((0, lambda ref: ref.at[:, pl.ds(0, EDGE)], 1, whole))
                items.append((1, lambda ref: ref.at[pl.ds(0, EDGE)], 2, whole))
            items.append((2, whole, 3, slot(k - 1)))
            rounds.append(
                (seq_peer(lax.rem(s + size - k, size)), seq_peer(lax.rem(s + k, size)), items)
            )
        return rounds

    return exchange(
        [projected, byte_states, info],
        [
            like((reach, 2, rows, width)),
            like((3, EDGE, width)),
            like((EDGE, byte_states.shape[1])),
            like((size - 1, 8, 128), jnp.int32),
        ],
        plan,
        1,
    )


def turn(values, axis_kind, send_views, out_shapes, call_id, count, by_source=False):
    def plan():
        s, t = lax.axis_index("seq"), lax.axis_index("tp")
        p, c = s // 2, lax.rem(s, 2)
        rounds = []
        for k in range(1, count):
            if axis_kind == "tp":
                me = t
                peer = tp_peer
            else:
                me = p
                peer = lambda i: {"seq": 2 * i + c}
            target = lax.rem(me + k, count)
            source = lax.rem(me + count - k, count)
            items = [
                (i, (lambda ref, v=view, to=target: v(ref, to)), i, slot(me if by_source else k - 1))
                for i, view in enumerate(send_views)
            ]
            rounds.append((peer(source), peer(target), items))
        return rounds

    return exchange(values, out_shapes, plan, call_id)


def swap_cores(value, call_id):
    def plan():
        s = lax.axis_index("seq")
        other = seq_peer(s + 1 - 2 * lax.rem(s, 2))
        return [(other, other, [(0, whole, 0, whole)])]

    return exchange([value], [like(value.shape, value.dtype)], plan, call_id)[0]


def shards(
    byte_states,
    enc_gain,
    enc_qkv,
    enc_proj_out,
    starts,
    counts,
    lift,
    cross_kv,
    latent_gain,
    lat_qkv,
    lat_proj_out,
):
    size, tp_size = lax.axis_size("seq"), lax.axis_size("tp")
    s, t = lax.axis_index("seq"), lax.axis_index("tp")
    pairs = size // 2
    p, c = s // 2, lax.rem(s, 2)
    byte_rows = byte_states.shape[0]
    anchor = s * byte_rows
    both = [(i, i ^ 1) for i in range(size)]
    lat_qkv_other = lax.ppermute(lat_qkv, "seq", both)
    lat_proj_other = lax.ppermute(lat_proj_out, "seq", both)
    states = byte_states.astype(jnp.float32)
    normed = rms_scale(states, enc_gain.astype(jnp.float32)).astype(jnp.bfloat16)
    projected = jnp.einsum(
        "bd,idc->ibc", normed, enc_qkv, preferred_element_type=jnp.float32
    ).astype(jnp.bfloat16)
    patch_count = counts[0]
    local_starts = starts[0]
    lanes = lax.broadcasted_iota(jnp.int32, (8, 128), 1)
    info = jnp.where(lanes == 0, patch_count, jnp.where(lanes == 1, local_starts[0], 0))
    behind, edge, edge_states, infos = halo(projected, byte_states, info)
    reach = WIN // byte_rows
    key_rows = jnp.concatenate(
        [behind[k, 0] for k in range(reach - 1, -1, -1)] + [projected[1], edge[1]], axis=0
    )
    value_rows = jnp.concatenate(
        [behind[k, 1] for k in range(reach - 1, -1, -1)] + [projected[2], edge[2]], axis=0
    )
    query_rows = jnp.concatenate([projected[0], edge[0]], axis=0)
    total_rows = byte_rows + EDGE
    head_count = projected.shape[2] // EH
    scores = jnp.einsum(
        "qhd,khd->hqk",
        query_rows.reshape(total_rows, head_count, EH),
        key_rows.reshape(-1, head_count, EH),
        preferred_element_type=jnp.float32,
    ) * (1.0 / math.sqrt(EH))
    query_pos = anchor + jnp.arange(total_rows, dtype=jnp.int32)
    key_pos = anchor - WIN + jnp.arange(WIN + total_rows, dtype=jnp.int32)
    allowed = (
        (key_pos[None, :] <= query_pos[:, None])
        & (key_pos[None, :] > query_pos[:, None] - WIN)
        & (key_pos[None, :] >= 0)
    )
    weights = masked_softmax(scores, allowed[None]).astype(jnp.bfloat16)
    attended = jnp.einsum(
        "hqk,khd->qhd",
        weights,
        value_rows.reshape(-1, head_count, EH),
        preferred_element_type=jnp.float32,
    )
    attended = attended.reshape(total_rows, head_count * EH).astype(jnp.bfloat16)
    blend = jnp.dot(attended, enc_proj_out, preferred_element_type=jnp.float32).astype(
        jnp.bfloat16
    )
    width = blend.shape[1]
    share = byte_rows // tp_size
    tail = jnp.broadcast_to(blend[byte_rows:][None], (tp_size, EDGE, width))
    blend = jnp.concatenate([blend[:byte_rows].reshape(tp_size, share, width), tail], axis=1)
    (blends,) = turn(
        [blend],
        "tp",
        [lambda ref, target: ref.at[target]],
        [like((tp_size - 1, share + EDGE, width))],
        2,
        tp_size,
    )
    mine = lax.dynamic_index_in_dim(blend, t, 0, keepdims=False).astype(jnp.float32)
    mine = mine + jnp.sum(blends.astype(jnp.float32), axis=0)
    my_states = jnp.concatenate(
        [lax.dynamic_slice_in_dim(byte_states, t * share, share, 0), edge_states], axis=0
    )
    mine = (mine + my_states.astype(jnp.float32)).astype(jnp.bfloat16)
    my_encoded = mine[:share]
    (encodeds,) = turn(
        [my_encoded],
        "tp",
        [lambda ref, target: ref],
        [like((tp_size, share, width))],
        3,
        tp_size,
        by_source=True,
    )
    tp_ids = jnp.arange(tp_size, dtype=jnp.int32)[:, None, None]
    encoded = jnp.where(tp_ids == t, my_encoded[None], encodeds).reshape(byte_rows, width)
    extended = jnp.concatenate([encoded, mine[share : share + SPILL]], axis=0)

    recent = jnp.concatenate([info[None], infos], axis=0)
    ring = jnp.arange(size, dtype=jnp.int32)
    from_ring = lax.rem(s - ring + size, size)
    placed = from_ring[None, :] == ring[:, None]
    count_list = jnp.sum(jnp.where(placed, recent[None, :, 0, 0], 0), axis=1)
    offsets = jnp.sum(jnp.where(ring[None, :] < ring[:, None], count_list[None, :], 0), axis=1)
    next_first = jnp.where(s + 1 < size, recent[size - 1, 0, 1], size * byte_rows)

    slot_total = local_starts.shape[0]
    slot_ids = jnp.arange(slot_total, dtype=jnp.int32)
    in_use = slot_ids < patch_count
    following = jnp.concatenate([local_starts[1:], jnp.zeros((1,), jnp.int32)])
    patch_end = jnp.where(slot_ids + 1 < patch_count, following, next_first)
    patches = patch_block(extended, local_starts, patch_end, in_use, anchor, lift, cross_kv)

    def slots_of(core):
        members = 2 * jnp.arange(pairs, dtype=jnp.int32) + core
        hit = members[:, None] == ring[None, :]
        begin = jnp.sum(jnp.where(hit, offsets[None, :], 0), axis=1)
        used = jnp.sum(jnp.where(hit, count_list[None, :], 0), axis=1)
        position = (begin[:, None] + slot_ids[None, :]).reshape(-1)
        return position, (slot_ids[None, :] < used[:, None]).reshape(-1)

    position, rows_used = slots_of(c)
    other_position, other_used = slots_of(1 - c)

    rows = relay(patches, pairs, False, False, 4).reshape(pairs * slot_total, -1)
    half = rows.shape[1] // 2
    full_width = half * size
    values = rows.astype(jnp.float32)
    squares = jnp.sum(values * values, axis=-1)
    gain = lax.dynamic_slice_in_dim(latent_gain, p * 2 * half, 2 * half, 0)
    geared = (values * gain.astype(jnp.float32)[None]).astype(jnp.bfloat16)
    low, high = geared[:, :half], geared[:, half:]
    partial = (
        jnp.einsum(
            "pd,idc->ipc", jnp.where(c == 0, low, high), lat_qkv, preferred_element_type=jnp.float32
        )
        + jnp.einsum(
            "pd,idc->ipc",
            jnp.where(c == 0, high, low),
            lat_qkv_other,
            preferred_element_type=jnp.float32,
        )
    ).astype(jnp.bfloat16)
    row_total = rows.shape[0]
    square_block = jnp.pad(
        squares.reshape(row_total // 128, 128), ((0, 8 - row_total // 128), (0, 0))
    )
    parts, square_parts = turn(
        [partial, square_block],
        "pair",
        [lambda ref, target: ref.at[:, :, pl.ds(pl.multiple_of(target * HD, HD), HD)], lambda ref, target: ref],
        [like((pairs - 1, 3, row_total, HD)), like((pairs - 1, 8, 128), jnp.float32)],
        5,
        pairs,
    )
    projected = lax.dynamic_slice_in_dim(partial, p * HD, HD, 2).astype(jnp.float32) + jnp.sum(
        parts.astype(jnp.float32), axis=0
    )
    square_sum = (square_block + jnp.sum(square_parts, axis=0)).reshape(-1)[:row_total]
    projected = projected * lax.rsqrt(square_sum / full_width + epsilon)[None, :, None]
    queries = rotate(projected[0][:, None], position)[:, 0].astype(jnp.bfloat16)
    keys = rotate(projected[1][:, None], position)[:, 0].astype(jnp.bfloat16)
    key_value = jnp.stack([keys, projected[2].astype(jnp.bfloat16)])
    key_value_other = swap_cores(key_value, 6)
    all_keys = jnp.concatenate([key_value[0], key_value_other[0]], axis=0)
    all_values = jnp.concatenate([key_value[1], key_value_other[1]], axis=0)
    key_position = jnp.concatenate(
        [
            jnp.where(rows_used, position, far_position),
            jnp.where(other_used, other_position, far_position),
        ]
    )
    scores = jnp.dot(queries, all_keys.T, preferred_element_type=jnp.float32) * (
        1.0 / math.sqrt(HD)
    )
    permitted = key_position[None, :] <= position[:, None]
    weights = masked_softmax(scores, permitted).astype(jnp.bfloat16)
    attended = jnp.dot(weights, all_values, preferred_element_type=jnp.float32).astype(
        jnp.bfloat16
    )
    (heads,) = turn(
        [attended],
        "pair",
        [lambda ref, target: ref],
        [like((pairs, row_total, HD))],
        7,
        pairs,
        by_source=True,
    )
    attended = jnp.concatenate(
        [jnp.where(p == q, attended, heads[q]) for q in range(pairs)], axis=1
    )
    own_out = jnp.dot(attended, lat_proj_out, preferred_element_type=jnp.float32)
    other_out = jnp.dot(attended, lat_proj_other, preferred_element_type=jnp.float32)
    partials = jnp.concatenate(
        [jnp.where(c == 0, own_out, other_out), jnp.where(c == 0, other_out, own_out)], axis=1
    ).astype(jnp.bfloat16)
    reduced = relay(partials.reshape(pairs, slot_total, -1), pairs, True, True, 8)
    latent = patches.astype(jnp.float32) + jnp.sum(reduced.astype(jnp.float32), axis=0)
    latent = jnp.where(in_use[:, None], latent, 0.0).astype(jnp.bfloat16)
    return (encoded, latent)


def fits_pairs(mesh, byte_states, enc_qkv, starts, lat_qkv):
    size, tp_size = mesh.shape["seq"], mesh.shape["tp"]
    byte_rows = byte_states.shape[0] // size
    return (
        size == 2 * tp_size
        and WIN % byte_rows == 0
        and WIN // byte_rows < size
        and byte_rows % (16 * tp_size) == 0
        and lat_qkv.shape[2] // tp_size == HD * tp_size
        and lat_qkv.shape[1] % (128 * size) == 0
        and starts.shape[1] * tp_size % 128 == 0
        and starts.shape[1] * tp_size <= 1024
        and starts.shape[1] % 16 == 0
        and enc_qkv.shape[2] % (128 * tp_size) == 0
    )


def solution(mesh):
    specs = dict(
        mesh=mesh,
        in_specs=(
            P("seq", None),
            P(),
            P(None, None, "tp"),
            P("tp", None),
            P("seq", None),
            P("seq"),
            P(None, "tp"),
            P(None, None, "tp"),
            P(),
            P(None, "seq", "tp"),
            P("tp", "seq"),
        ),
        out_specs=(P("seq", None), P("seq", "tp")),
        check_vma=False,
    )

    def run(*arrays):
        paired = fits_pairs(mesh, arrays[0], arrays[2], arrays[4], arrays[9])
        return jax.shard_map(shards if paired else gathered_shards, **specs)(*arrays)

    return run
```

```python
import math

import jax
import jax.numpy as jnp
from jax import lax
from jax.experimental import pallas as pl
from jax.experimental.pallas import tpu as pltpu
from jax.sharding import PartitionSpec as P

EH = 64
HD = 128
WIN = 512
SPILL = 8


epsilon = 1e-05
rope_base = 500000.0
far_position = 1 << 30


def from_behind(value, axis, steps):
    count = lax.axis_size(axis)
    leading, last = (max(0, -steps), min(count, count - steps))
    return lax.ppermute(value, axis, [(source, source + steps) for source in range(leading, last)])


def prefix(value, axis, join, neutral):
    count, mine = (lax.axis_size(axis), lax.axis_index(axis))
    pieces = lax.all_gather(value, axis)
    subtotal = jnp.full_like(value, 0) + jnp.asarray(neutral, value.dtype)

    def hop(position, subtotal):
        longer = join(subtotal, pieces[position])
        return jnp.where(position < mine, longer, subtotal)

    return lax.fori_loop(0, count - 1, hop, subtotal)


def shortened(value):

    def short(part):
        return part.astype(jnp.bfloat16) if part.dtype == jnp.float32 else part

    return jax.tree.map(short, value)


def rms_scale(values, gain_row):
    mean_square = jnp.mean(values * values, axis=-1, keepdims=True)
    return values * lax.rsqrt(mean_square + epsilon) * gain_row


def masked_softmax(scores, allowed):
    scores = jnp.where(allowed, scores, -1e30)
    largest = jnp.max(scores, axis=-1, keepdims=True)
    raised = jnp.where(allowed, jnp.exp(scores - largest), 0.0)
    return raised / jnp.sum(raised, axis=-1, keepdims=True)


def rotate(values, position):
    halfway = values.shape[-1] // 2
    frequency = jnp.power(
        rope_base, -2.0 * jnp.arange(halfway, dtype=jnp.float32) / values.shape[-1]
    )
    angles = position.astype(jnp.float32)[:, None] * frequency[None, :]
    cosine = jnp.cos(angles)[:, None, :]
    sine_rows = jnp.sin(angles)[:, None, :]
    lower_half = values[..., :halfway]
    upper_half = values[..., halfway:]
    return jnp.concatenate(
        [
            lower_half * cosine - upper_half * sine_rows,
            upper_half * cosine + lower_half * sine_rows,
        ],
        axis=-1,
    )


def patch_block(extended, first_byte, end_byte, in_use, anchor, lift, cross_kv):
    columns = anchor + jnp.arange(extended.shape[0], dtype=jnp.int32)
    inside = (
        (columns[None, :] >= first_byte[:, None])
        & (columns[None, :] < end_byte[:, None])
        & in_use[:, None]
    )
    member = inside.astype(jnp.bfloat16)
    totals = jnp.dot(member, extended, preferred_element_type=jnp.float32)
    lengths = jnp.maximum(jnp.sum(inside.astype(jnp.float32), axis=1), 1.0)
    pooled = (totals / lengths[:, None]).astype(jnp.bfloat16)
    lifted = jnp.dot(pooled, lift, preferred_element_type=jnp.float32)
    key_rows = jnp.dot(extended, cross_kv[0], preferred_element_type=jnp.float32).astype(
        jnp.bfloat16
    )
    value_rows = jnp.dot(extended, cross_kv[1], preferred_element_type=jnp.float32).astype(
        jnp.bfloat16
    )
    slot_total = first_byte.shape[0]
    head_count = lifted.shape[1] // HD
    queries = lifted.astype(jnp.bfloat16).reshape(slot_total, head_count, HD)
    scores = jnp.einsum(
        "phd,khd->hpk",
        queries,
        key_rows.reshape(-1, head_count, HD),
        preferred_element_type=jnp.float32,
    ) * (1.0 / math.sqrt(HD))
    allowed = inside | (~in_use)[:, None] & (columns[None, :] == anchor)
    weights = masked_softmax(scores, allowed[None]).astype(jnp.bfloat16)
    crossed = jnp.einsum(
        "hpk,khd->phd",
        weights,
        value_rows.reshape(-1, head_count, HD),
        preferred_element_type=jnp.float32,
    )
    crossed = crossed.reshape(slot_total, head_count * HD)
    return jnp.where(in_use[:, None], lifted + crossed, 0.0).astype(jnp.bfloat16)


def add_counts(earlier, later):
    return earlier + later


def gathered_shards(
    byte_states,
    enc_gain,
    enc_qkv,
    enc_proj_out,
    starts,
    counts,
    lift,
    cross_kv,
    latent_gain,
    lat_qkv,
    lat_proj_out,
):
    byte_rows = byte_states.shape[0]
    anchor = lax.axis_index("seq") * byte_rows
    states = byte_states.astype(jnp.float32)
    normed = rms_scale(states, enc_gain.astype(jnp.float32)).astype(jnp.bfloat16)
    projected = jnp.einsum(
        "bd,idc->ibc", normed, enc_qkv, preferred_element_type=jnp.float32
    ).astype(jnp.bfloat16)
    reach_blocks = max(WIN // byte_rows, 1)
    tail_rows = min(WIN, byte_rows)
    key_parts = []
    value_parts = []
    for distance in range(reach_blocks, 0, -1):
        moved_keys, moved_values = from_behind(
            (projected[1, byte_rows - tail_rows :], projected[2, byte_rows - tail_rows :]),
            "seq",
            distance,
        )
        key_parts.append(moved_keys)
        value_parts.append(moved_values)
    key_rows = jnp.concatenate(key_parts + [projected[1]], axis=0)
    value_rows = jnp.concatenate(value_parts + [projected[2]], axis=0)
    head_count = projected.shape[2] // EH
    scores = jnp.einsum(
        "qhd,khd->hqk",
        projected[0].reshape(byte_rows, head_count, EH),
        key_rows.reshape(-1, head_count, EH),
        preferred_element_type=jnp.float32,
    ) * (1.0 / math.sqrt(EH))
    query_pos = anchor + jnp.arange(byte_rows, dtype=jnp.int32)
    key_pos = anchor - WIN + jnp.arange(WIN + byte_rows, dtype=jnp.int32)
    allowed = (
        (key_pos[None, :] <= query_pos[:, None])
        & (key_pos[None, :] > query_pos[:, None] - WIN)
        & (key_pos[None, :] >= 0)
    )
    weights = masked_softmax(scores, allowed[None]).astype(jnp.bfloat16)
    attended = jnp.einsum(
        "hqk,khd->qhd",
        weights,
        value_rows.reshape(-1, head_count, EH),
        preferred_element_type=jnp.float32,
    )
    attended = attended.reshape(byte_rows, head_count * EH).astype(jnp.bfloat16)
    blended = lax.psum(jnp.dot(attended, enc_proj_out, preferred_element_type=jnp.float32), "tp")
    encoded = (states + blended).astype(jnp.bfloat16)
    patch_count = counts[0]
    local_starts = starts[0]
    first_local = (local_starts[0:1] - anchor).astype(jnp.bfloat16)
    next_rows, next_first = from_behind((encoded[:SPILL], first_local), "seq", -1)
    next_first = next_first.astype(jnp.int32)[0]
    extended = jnp.concatenate([encoded, next_rows], axis=0)
    slot_ids = jnp.arange(local_starts.shape[0], dtype=jnp.int32)
    in_use = slot_ids < patch_count
    following = jnp.concatenate([local_starts[1:], jnp.zeros((1,), jnp.int32)])
    patch_end = jnp.where(slot_ids + 1 < patch_count, following, anchor + byte_rows + next_first)
    patches = patch_block(extended, local_starts, patch_end, in_use, anchor, lift, cross_kv)
    offset = prefix(counts, "seq", add_counts, jnp.zeros((1,), jnp.int32))[0]
    position = offset + slot_ids
    slot_total = patches.shape[0]
    full_rows = lax.all_gather(patches, "tp", axis=1, tiled=True)
    normed_rows = rms_scale(full_rows.astype(jnp.float32), latent_gain.astype(jnp.float32)).astype(
        jnp.bfloat16
    )
    inner_width = lat_qkv.shape[2]
    projected = jnp.einsum(
        "pd,idc->ipc",
        normed_rows,
        lax.all_gather(lat_qkv, "seq", axis=1, tiled=True),
        preferred_element_type=jnp.float32,
    )
    heads_here = inner_width // HD
    queries = rotate(projected[0].reshape(slot_total, heads_here, HD), position).astype(
        jnp.bfloat16
    )
    latent_keys = (
        rotate(projected[1].reshape(slot_total, heads_here, HD), position)
        .astype(jnp.bfloat16)
        .reshape(slot_total, inner_width)
    )
    latent_values = projected[2].astype(jnp.bfloat16)
    latent_pos = jnp.where(in_use, position, far_position)
    largest = jnp.full((heads_here, slot_total), -1e30, jnp.float32)
    piece_keys = lax.all_gather(latent_keys, "seq", axis=0, tiled=True)
    piece_values = lax.all_gather(latent_values, "seq", axis=0, tiled=True)
    piece_pos = lax.all_gather(shortened(latent_pos), "seq", axis=0, tiled=True)
    rows_here = piece_keys.shape[0]
    piece_scores = jnp.einsum(
        "qhd,khd->hqk",
        queries,
        piece_keys.reshape(rows_here, heads_here, HD),
        preferred_element_type=jnp.float32,
    ) * (1.0 / math.sqrt(HD))
    permitted = (piece_pos[None, :] <= position[:, None])[None]
    piece_scores = jnp.where(permitted, piece_scores, -1e30)
    renewed = jnp.maximum(largest, jnp.max(piece_scores, axis=-1))
    raised = jnp.where(permitted, jnp.exp(piece_scores - renewed[..., None]), 0.0)
    weight_sum = jnp.sum(raised, axis=-1)
    weighted = jnp.einsum(
        "hqk,khd->hqd",
        raised.astype(jnp.bfloat16),
        piece_values.reshape(rows_here, heads_here, HD),
        preferred_element_type=jnp.float32,
    )
    largest, weight_sum, weighted = (renewed, weight_sum, weighted)
    latent_heads = (
        (weighted / weight_sum[..., None])
        .transpose(1, 0, 2)
        .reshape(slot_total, inner_width)
        .astype(jnp.bfloat16)
    )
    partials = jnp.dot(
        latent_heads,
        lax.all_gather(lat_proj_out, "seq", axis=1, tiled=True),
        preferred_element_type=jnp.float32,
    )
    reduced = lax.psum_scatter(partials, "tp", scatter_dimension=1, tiled=True)
    latent = jnp.where(in_use[:, None], patches.astype(jnp.float32) + reduced, 0.0).astype(
        jnp.bfloat16
    )
    return (encoded, latent)


MESH = pl.DeviceIdType.MESH
EDGE = 16


def greet(peers):
    barrier = pltpu.get_barrier_semaphore()
    for peer in peers:
        pl.semaphore_signal(barrier, inc=1, device_id=peer, device_id_type=MESH)
    pl.semaphore_wait(barrier, len(peers))


def exchange(values, out_shapes, plan, call_id):
    n_in, n_out = len(values), len(out_shapes)
    n_copies = 16

    def kernel(*refs):
        ins, outs = refs[:n_in], refs[n_in : n_in + n_out]
        send_sems, recv_sems = refs[n_in + n_out :]
        rounds = plan()
        greet([source for source, _, _ in rounds])
        copies = []
        for _, target, items in rounds:
            for in_id, in_view, out_id, out_view in items:
                copy = pltpu.make_async_remote_copy(
                    src_ref=in_view(ins[in_id]),
                    dst_ref=out_view(outs[out_id]),
                    send_sem=send_sems.at[len(copies)],
                    recv_sem=recv_sems.at[len(copies)],
                    device_id=target,
                    device_id_type=MESH,
                )
                copy.start()
                copies.append(copy)
        for copy in copies:
            copy.wait()

    return pl.pallas_call(
        kernel,
        out_shape=out_shapes,
        in_specs=[pl.BlockSpec(memory_space=pl.ANY)] * n_in,
        out_specs=[pl.BlockSpec(memory_space=pl.ANY)] * n_out,
        scratch_shapes=[
            pltpu.SemaphoreType.DMA((n_copies,)),
            pltpu.SemaphoreType.DMA((n_copies,)),
        ],
        compiler_params=pltpu.CompilerParams(collective_id=call_id, has_side_effects=True),
    )(*values)


def whole(ref):
    return ref


def slot(index):
    return lambda ref: ref.at[index]


def seq_peer(index):
    return {"seq": index}


def tp_peer(index):
    return {"tp": index}


def relay(value, count, spread, plane_first, call_id):
    block = value.shape[1:] if spread else value.shape

    def kernel(value_ref, out_ref, land, send_a, recv_a, send_b, recv_b, own_sem):
        s, t = lax.axis_index("seq"), lax.axis_index("tp")
        p, c = s // 2, lax.rem(s, 2)

        def plane(index):
            return {"seq": 2 * index + c}

        if plane_first:
            a, b, first, second = p, t, plane, tp_peer
        else:
            a, b, first, second = t, p, tp_peer, plane
        others_a = [lax.rem(a + k, count) for k in range(1, count)]
        others_b = [lax.rem(b + k, count) for k in range(1, count)]
        greet([first(i) for i in others_a] + [second(i) for i in others_b])
        hops = []
        for k in range(1, count):
            target = lax.rem(a + k, count)
            hop = pltpu.make_async_remote_copy(
                src_ref=value_ref.at[target] if spread else value_ref,
                dst_ref=land.at[k - 1],
                send_sem=send_a.at[k - 1],
                recv_sem=recv_a.at[k - 1],
                device_id=first(target),
                device_id_type=MESH,
            )
            hop.start()
            hops.append(hop)
        onward = []
        for k in range(count):
            origin = lax.rem(a + count - k, count)
            if k == 0:
                here = value_ref.at[a] if spread else value_ref
            else:
                hops[k - 1].wait_recv()
                here = land.at[k - 1]
            away = pltpu.make_async_remote_copy(
                src_ref=here,
                dst_ref=out_ref.at[b],
                send_sem=send_b.at[k],
                recv_sem=recv_b.at[b],
                device_id=second(origin),
                device_id_type=MESH,
            )
            stay = pltpu.make_async_copy(here, out_ref.at[b], own_sem)
            onward.append((origin, away, stay))

            @pl.when(origin != b)
            def _():
                away.start()

            @pl.when(origin == b)
            def _():
                stay.start()

        for q in range(count):

            @pl.when(b != q)
            def _():
                pltpu.make_async_remote_copy(
                    src_ref=land.at[0],
                    dst_ref=out_ref.at[q],
                    send_sem=send_b.at[q],
                    recv_sem=recv_b.at[q],
                    device_id=second(b),
                    device_id_type=MESH,
                ).wait_recv()

        for hop in hops:
            hop.wait_send()
        for origin, away, stay in onward:

            @pl.when(origin != b)
            def _():
                away.wait_send()

            @pl.when(origin == b)
            def _():
                stay.wait()

    return pl.pallas_call(
        kernel,
        out_shape=jax.ShapeDtypeStruct((count, *block), value.dtype),
        in_specs=[pl.BlockSpec(memory_space=pltpu.VMEM)],
        out_specs=pl.BlockSpec(memory_space=pl.ANY),
        scratch_shapes=[
            pltpu.VMEM((count - 1, *block), value.dtype),
            pltpu.SemaphoreType.DMA((count - 1,)),
            pltpu.SemaphoreType.DMA((count - 1,)),
            pltpu.SemaphoreType.DMA((count,)),
            pltpu.SemaphoreType.DMA((count,)),
            pltpu.SemaphoreType.DMA,
        ],
        compiler_params=pltpu.CompilerParams(collective_id=call_id, has_side_effects=True),
    )(value)


def like(shape, dtype=jnp.bfloat16):
    return jax.ShapeDtypeStruct(shape, dtype)


def halo(projected, byte_states, info):
    size = lax.axis_size("seq")
    rows, width = projected.shape[1:]
    reach = WIN // rows

    def plan():
        s = lax.axis_index("seq")
        rounds = []
        for k in range(1, size):
            items = []
            if k <= reach:
                items.append((0, lambda ref: ref.at[pl.ds(1, 2)], 0, slot(k - 1)))
            if k == size - 1:
                items.append((0, lambda ref: ref.at[:, pl.ds(0, EDGE)], 1, whole))
                items.append((1, lambda ref: ref.at[pl.ds(0, EDGE)], 2, whole))
            items.append((2, whole, 3, slot(k - 1)))
            rounds.append(
                (seq_peer(lax.rem(s + size - k, size)), seq_peer(lax.rem(s + k, size)), items)
            )
        return rounds

    return exchange(
        [projected, byte_states, info],
        [
            like((reach, 2, rows, width)),
            like((3, EDGE, width)),
            like((EDGE, byte_states.shape[1])),
            like((size - 1, 8, 128), jnp.int32),
        ],
        plan,
        1,
    )


def turn(values, axis_kind, send_views, out_shapes, call_id, count, by_source=False):
    def plan():
        s, t = lax.axis_index("seq"), lax.axis_index("tp")
        p, c = s // 2, lax.rem(s, 2)
        rounds = []
        for k in range(1, count):
            if axis_kind == "tp":
                me = t
                peer = tp_peer
            else:
                me = p
                peer = lambda i: {"seq": 2 * i + c}
            target = lax.rem(me + k, count)
            source = lax.rem(me + count - k, count)
            items = [
                (i, (lambda ref, v=view, to=target: v(ref, to)), i, slot(me if by_source else k - 1))
                for i, view in enumerate(send_views)
            ]
            rounds.append((peer(source), peer(target), items))
        return rounds

    return exchange(values, out_shapes, plan, call_id)


def blend_and_patch(attended, proj, byte_states, edge_states, bounds, used, lift, cross_kv, call_id):
    count = lax.axis_size("tp")
    byte_rows, width = byte_states.shape
    share = byte_rows // count
    chunks = 2
    piece = share // chunks
    slots = bounds[0].shape[0]
    columns = lift.shape[1]
    total_rows = byte_rows + EDGE

    def kernel(
        att_ref, proj_ref, states_ref, edge_ref, lo_ref, hi_ref, used_ref, lift_hbm, cross_hbm,
        full_ref, patch_ref,
        sends, lands, tail_send, tail_land, blocks, lift_ref, cross_ref, pooled_ref,
        load_sems, rs_send, rs_recv, tail_s, tail_r, up_send, down_send, ag_recv,
    ):
        t = lax.axis_index("tp")
        loads = [
            pltpu.make_async_copy(lift_hbm, lift_ref, load_sems.at[0]),
            pltpu.make_async_copy(cross_hbm, cross_ref, load_sems.at[1]),
        ]
        for load in loads:
            load.start()
        blend = jnp.dot(att_ref[...], proj_ref[...], preferred_element_type=jnp.float32).astype(
            jnp.bfloat16
        )
        for q in range(count):
            for h in range(chunks):
                begin = q * share + h * piece
                sends[q, h] = blend[begin : begin + piece]
        tail_send[...] = blend[byte_rows:]
        greet([tp_peer(lax.rem(t + k, count)) for k in range(1, count)])
        scatter = [[], []]
        for h in range(chunks):
            for k in range(1, count):
                target = lax.rem(t + k, count)
                copy = pltpu.make_async_remote_copy(
                    src_ref=sends.at[target, h],
                    dst_ref=lands.at[h, k - 1],
                    send_sem=rs_send.at[h, k - 1],
                    recv_sem=rs_recv.at[h, k - 1],
                    device_id=tp_peer(target),
                    device_id_type=MESH,
                )
                copy.start()
                scatter[h].append(copy)
        tails = []
        for k in range(1, count):
            copy = pltpu.make_async_remote_copy(
                src_ref=tail_send,
                dst_ref=tail_land.at[k - 1],
                send_sem=tail_s.at[k - 1],
                recv_sem=tail_r.at[k - 1],
                device_id=tp_peer(lax.rem(t + k, count)),
                device_id_type=MESH,
            )
            copy.start()
            tails.append(copy)

        def pass_on(origin, h, up):
            step = 1 if up else -1
            return pltpu.make_async_remote_copy(
                src_ref=blocks.at[origin, h],
                dst_ref=blocks.at[origin, h],
                send_sem=(up_send if up else down_send).at[origin, h],
                recv_sem=ag_recv.at[origin, h],
                device_id=tp_peer(lax.rem(t + step + count, count)),
                device_id_type=MESH,
            )

        for h in range(chunks):
            for copy in scatter[h]:
                copy.wait_recv()
            total = sends[t, h].astype(jnp.float32)
            for k in range(count - 1):
                total = total + lands[h, k].astype(jnp.float32)
            rows = pl.ds(pl.multiple_of(t * share + h * piece, piece), piece)
            blocks[t, h] = (states_ref[rows].astype(jnp.float32) + total).astype(jnp.bfloat16)

            @pl.when(t < count - 1)
            def _():
                pass_on(t, h, True).start()

            @pl.when(t > 0)
            def _():
                pass_on(t, h, False).start()

        for copy in tails:
            copy.wait_recv()
        total = tail_send[...].astype(jnp.float32)
        for k in range(count - 1):
            total = total + tail_land[k].astype(jnp.float32)
        full_ref[byte_rows:] = (edge_ref[...].astype(jnp.float32) + total).astype(jnp.bfloat16)

        for d in range(1, count):
            for h in range(chunks):

                @pl.when(t - d >= 0)
                def _():
                    pass_on(t - d, h, True).wait_recv()

                    @pl.when(t < count - 1)
                    def _():
                        pass_on(t - d, h, True).start()

                @pl.when(t + d < count)
                def _():
                    pass_on(t + d, h, False).wait_recv()

                    @pl.when(t > 0)
                    def _():
                        pass_on(t + d, h, False).start()

        for q in range(count):
            for h in range(chunks):
                begin = q * share + h * piece
                full_ref[begin : begin + piece] = blocks[q, h]
        for load in loads:
            load.wait()

        where_at = lax.broadcasted_iota(jnp.int32, (slots, total_rows), 1)
        allowed = (where_at >= lo_ref[...]) & (where_at < hi_ref[...])
        in_use = used_ref[...] > 0.0
        member = jnp.where(allowed & in_use, 1.0, 0.0)
        lengths = jnp.maximum(jnp.sum(member, axis=1, keepdims=True), 1.0)
        totals = jnp.dot(
            member.astype(jnp.bfloat16), full_ref[...], preferred_element_type=jnp.float32
        )
        pooled_ref[...] = (totals / lengths).astype(jnp.bfloat16)
        group = 2 * HD

        def heads(i, carry):
            cols = pl.ds(pl.multiple_of(i * group, group), group)
            rows = full_ref[...]
            lifted = jnp.dot(pooled_ref[...], lift_ref[:, cols], preferred_element_type=jnp.float32)
            keys = jnp.dot(rows, cross_ref[0, :, cols], preferred_element_type=jnp.float32).astype(
                jnp.bfloat16
            )
            values = jnp.dot(
                rows, cross_ref[1, :, cols], preferred_element_type=jnp.float32
            ).astype(jnp.bfloat16)
            queries = lifted.astype(jnp.bfloat16)
            crossed = []
            for j in range(2):
                lanes = slice(j * HD, (j + 1) * HD)
                scores = lax.dot_general(
                    queries[:, lanes],
                    keys[:, lanes],
                    (((1,), (1,)), ((), ())),
                    preferred_element_type=jnp.float32,
                ) * (1.0 / math.sqrt(HD))
                weights = masked_softmax(scores, allowed).astype(jnp.bfloat16)
                crossed.append(
                    jnp.dot(weights, values[:, lanes], preferred_element_type=jnp.float32)
                )
            patch = lifted + jnp.concatenate(crossed, axis=1)
            patch_ref[:, cols] = jnp.where(in_use, patch, 0.0).astype(jnp.bfloat16)
            return carry

        lax.fori_loop(0, columns // group, heads, 0)

        for h in range(chunks):
            for copy in scatter[h]:
                copy.wait_send()
        for copy in tails:
            copy.wait_send()
        for q in range(count):
            for h in range(chunks):

                @pl.when((q <= t) & (t < count - 1))
                def _():
                    pass_on(q, h, True).wait_send()

                @pl.when((q >= t) & (t > 0))
                def _():
                    pass_on(q, h, False).wait_send()

    vmem = pl.BlockSpec(memory_space=pltpu.VMEM)
    hbm = pl.BlockSpec(memory_space=pl.ANY)
    dma = pltpu.SemaphoreType.DMA
    return pl.pallas_call(
        kernel,
        out_shape=[like((total_rows, width)), like((slots, columns))],
        in_specs=[vmem] * 7 + [hbm] * 2,
        out_specs=[vmem, vmem],
        scratch_shapes=[
            pltpu.VMEM((count, chunks, piece, width), jnp.bfloat16),
            pltpu.VMEM((chunks, count - 1, piece, width), jnp.bfloat16),
            pltpu.VMEM((EDGE, width), jnp.bfloat16),
            pltpu.VMEM((count - 1, EDGE, width), jnp.bfloat16),
            pltpu.VMEM((count, chunks, piece, width), jnp.bfloat16),
            pltpu.VMEM(lift.shape, lift.dtype),
            pltpu.VMEM(cross_kv.shape, cross_kv.dtype),
            pltpu.VMEM((slots, width), jnp.bfloat16),
            dma((2,)),
            dma((chunks, count - 1)),
            dma((chunks, count - 1)),
            dma((count - 1,)),
            dma((count - 1,)),
            dma((count, chunks)),
            dma((count, chunks)),
            dma((count, chunks)),
        ],
        compiler_params=pltpu.CompilerParams(collective_id=call_id, has_side_effects=True),
    )(attended, proj, byte_states, edge_states, *bounds, used, lift, cross_kv)


def swap_cores(value, call_id):
    def plan():
        s = lax.axis_index("seq")
        other = seq_peer(s + 1 - 2 * lax.rem(s, 2))
        return [(other, other, [(0, whole, 0, whole)])]

    return exchange([value], [like(value.shape, value.dtype)], plan, call_id)[0]


def shards(
    byte_states,
    enc_gain,
    enc_qkv,
    enc_proj_out,
    starts,
    counts,
    lift,
    cross_kv,
    latent_gain,
    lat_qkv,
    lat_proj_out,
):
    size, tp_size = lax.axis_size("seq"), lax.axis_size("tp")
    s, t = lax.axis_index("seq"), lax.axis_index("tp")
    pairs = size // 2
    p, c = s // 2, lax.rem(s, 2)
    byte_rows = byte_states.shape[0]
    anchor = s * byte_rows
    both = [(i, i ^ 1) for i in range(size)]
    lat_qkv_other = lax.ppermute(lat_qkv, "seq", both)
    lat_proj_other = lax.ppermute(lat_proj_out, "seq", both)
    states = byte_states.astype(jnp.float32)
    normed = rms_scale(states, enc_gain.astype(jnp.float32)).astype(jnp.bfloat16)
    projected = jnp.einsum(
        "bd,idc->ibc", normed, enc_qkv, preferred_element_type=jnp.float32
    ).astype(jnp.bfloat16)
    patch_count = counts[0]
    local_starts = starts[0]
    lanes = lax.broadcasted_iota(jnp.int32, (8, 128), 1)
    info = jnp.where(lanes == 0, patch_count, jnp.where(lanes == 1, local_starts[0], 0))
    behind, edge, edge_states, infos = halo(projected, byte_states, info)
    reach = WIN // byte_rows
    key_rows = jnp.concatenate(
        [behind[k, 0] for k in range(reach - 1, -1, -1)] + [projected[1], edge[1]], axis=0
    )
    value_rows = jnp.concatenate(
        [behind[k, 1] for k in range(reach - 1, -1, -1)] + [projected[2], edge[2]], axis=0
    )
    query_rows = jnp.concatenate([projected[0], edge[0]], axis=0)
    total_rows = byte_rows + EDGE
    head_count = projected.shape[2] // EH
    scores = jnp.einsum(
        "qhd,khd->hqk",
        query_rows.reshape(total_rows, head_count, EH),
        key_rows.reshape(-1, head_count, EH),
        preferred_element_type=jnp.float32,
    ) * (1.0 / math.sqrt(EH))
    query_pos = anchor + jnp.arange(total_rows, dtype=jnp.int32)
    key_pos = anchor - WIN + jnp.arange(WIN + total_rows, dtype=jnp.int32)
    allowed = (
        (key_pos[None, :] <= query_pos[:, None])
        & (key_pos[None, :] > query_pos[:, None] - WIN)
        & (key_pos[None, :] >= 0)
    )
    weights = masked_softmax(scores, allowed[None]).astype(jnp.bfloat16)
    attended = jnp.einsum(
        "hqk,khd->qhd",
        weights,
        value_rows.reshape(-1, head_count, EH),
        preferred_element_type=jnp.float32,
    )
    attended = attended.reshape(total_rows, head_count * EH).astype(jnp.bfloat16)
    recent = jnp.concatenate([info[None], infos], axis=0)
    ring = jnp.arange(size, dtype=jnp.int32)
    from_ring = lax.rem(s - ring + size, size)
    placed = from_ring[None, :] == ring[:, None]
    count_list = jnp.sum(jnp.where(placed, recent[None, :, 0, 0], 0), axis=1)
    offsets = jnp.sum(jnp.where(ring[None, :] < ring[:, None], count_list[None, :], 0), axis=1)
    next_first = jnp.where(s + 1 < size, recent[size - 1, 0, 1], size * byte_rows)

    slot_total = local_starts.shape[0]
    slot_ids = jnp.arange(slot_total, dtype=jnp.int32)
    in_use = slot_ids < patch_count
    following = jnp.concatenate([local_starts[1:], jnp.zeros((1,), jnp.int32)])
    patch_end = jnp.where(slot_ids + 1 < patch_count, following, next_first)
    lower = jnp.where(in_use, local_starts - anchor, 0)[:, None]
    upper = jnp.where(in_use, patch_end - anchor, 1)[:, None]
    used_rows = in_use.astype(jnp.float32)[:, None]
    extended, patches = blend_and_patch(
        attended,
        enc_proj_out,
        byte_states,
        edge_states,
        (lower, upper),
        used_rows,
        lift,
        cross_kv,
        2,
    )
    encoded = extended[:byte_rows]

    def slots_of(core):
        members = 2 * jnp.arange(pairs, dtype=jnp.int32) + core
        hit = members[:, None] == ring[None, :]
        begin = jnp.sum(jnp.where(hit, offsets[None, :], 0), axis=1)
        used = jnp.sum(jnp.where(hit, count_list[None, :], 0), axis=1)
        position = (begin[:, None] + slot_ids[None, :]).reshape(-1)
        return position, (slot_ids[None, :] < used[:, None]).reshape(-1)

    position, rows_used = slots_of(c)
    other_position, other_used = slots_of(1 - c)

    rows = relay(patches, pairs, False, False, 4).reshape(pairs * slot_total, -1)
    half = rows.shape[1] // 2
    full_width = half * size
    values = rows.astype(jnp.float32)
    squares = jnp.sum(values * values, axis=-1)
    gain = lax.dynamic_slice_in_dim(latent_gain, p * 2 * half, 2 * half, 0)
    geared = (values * gain.astype(jnp.float32)[None]).astype(jnp.bfloat16)
    low, high = geared[:, :half], geared[:, half:]
    partial = (
        jnp.einsum(
            "pd,idc->ipc", jnp.where(c == 0, low, high), lat_qkv, preferred_element_type=jnp.float32
        )
        + jnp.einsum(
            "pd,idc->ipc",
            jnp.where(c == 0, high, low),
            lat_qkv_other,
            preferred_element_type=jnp.float32,
        )
    ).astype(jnp.bfloat16)
    row_total = rows.shape[0]
    square_block = jnp.pad(
        squares.reshape(row_total // 128, 128), ((0, 8 - row_total // 128), (0, 0))
    )
    parts, square_parts = turn(
        [partial, square_block],
        "pair",
        [lambda ref, target: ref.at[:, :, pl.ds(pl.multiple_of(target * HD, HD), HD)], lambda ref, target: ref],
        [like((pairs - 1, 3, row_total, HD)), like((pairs - 1, 8, 128), jnp.float32)],
        5,
        pairs,
    )
    projected = lax.dynamic_slice_in_dim(partial, p * HD, HD, 2).astype(jnp.float32) + jnp.sum(
        parts.astype(jnp.float32), axis=0
    )
    square_sum = (square_block + jnp.sum(square_parts, axis=0)).reshape(-1)[:row_total]
    projected = projected * lax.rsqrt(square_sum / full_width + epsilon)[None, :, None]
    queries = rotate(projected[0][:, None], position)[:, 0].astype(jnp.bfloat16)
    keys = rotate(projected[1][:, None], position)[:, 0].astype(jnp.bfloat16)
    key_value = jnp.stack([keys, projected[2].astype(jnp.bfloat16)])
    key_value_other = swap_cores(key_value, 6)
    all_keys = jnp.concatenate([key_value[0], key_value_other[0]], axis=0)
    all_values = jnp.concatenate([key_value[1], key_value_other[1]], axis=0)
    key_position = jnp.concatenate(
        [
            jnp.where(rows_used, position, far_position),
            jnp.where(other_used, other_position, far_position),
        ]
    )
    scores = jnp.dot(queries, all_keys.T, preferred_element_type=jnp.float32) * (
        1.0 / math.sqrt(HD)
    )
    permitted = key_position[None, :] <= position[:, None]
    weights = masked_softmax(scores, permitted).astype(jnp.bfloat16)
    attended = jnp.dot(weights, all_values, preferred_element_type=jnp.float32).astype(
        jnp.bfloat16
    )
    (heads,) = turn(
        [attended],
        "pair",
        [lambda ref, target: ref],
        [like((pairs, row_total, HD))],
        7,
        pairs,
        by_source=True,
    )
    attended = jnp.concatenate(
        [jnp.where(p == q, attended, heads[q]) for q in range(pairs)], axis=1
    )
    own_out = jnp.dot(attended, lat_proj_out, preferred_element_type=jnp.float32)
    other_out = jnp.dot(attended, lat_proj_other, preferred_element_type=jnp.float32)
    partials = jnp.concatenate(
        [jnp.where(c == 0, own_out, other_out), jnp.where(c == 0, other_out, own_out)], axis=1
    ).astype(jnp.bfloat16)
    reduced = relay(partials.reshape(pairs, slot_total, -1), pairs, True, True, 8)
    latent = patches.astype(jnp.float32) + jnp.sum(reduced.astype(jnp.float32), axis=0)
    latent = jnp.where(in_use[:, None], latent, 0.0).astype(jnp.bfloat16)
    return (encoded, latent)


def fits_pairs(mesh, byte_states, enc_qkv, starts, lat_qkv):
    size, tp_size = mesh.shape["seq"], mesh.shape["tp"]
    byte_rows = byte_states.shape[0] // size
    return (
        size == 2 * tp_size
        and WIN % byte_rows == 0
        and WIN // byte_rows < size
        and byte_rows % (32 * tp_size) == 0
        and lat_qkv.shape[2] // tp_size == HD * tp_size
        and lat_qkv.shape[1] % (128 * size) == 0
        and starts.shape[1] * tp_size % 128 == 0
        and starts.shape[1] * tp_size <= 1024
        and starts.shape[1] % 16 == 0
        and enc_qkv.shape[2] % (128 * tp_size) == 0
    )


def solution(mesh):
    specs = dict(
        mesh=mesh,
        in_specs=(
            P("seq", None),
            P(),
            P(None, None, "tp"),
            P("tp", None),
            P("seq", None),
            P("seq"),
            P(None, "tp"),
            P(None, None, "tp"),
            P(),
            P(None, "seq", "tp"),
            P("tp", "seq"),
        ),
        out_specs=(P("seq", None), P("seq", "tp")),
        check_vma=False,
    )

    def run(*arrays):
        paired = fits_pairs(mesh, arrays[0], arrays[2], arrays[4], arrays[9])
        return jax.shard_map(shards if paired else gathered_shards, **specs)(*arrays)

    return run
```

```python
import math

import jax
import jax.numpy as jnp
from jax import lax
from jax.experimental import pallas as pl
from jax.experimental.pallas import tpu as pltpu
from jax.sharding import PartitionSpec as P

EH = 64
HD = 128
WIN = 512
SPILL = 8


epsilon = 1e-05
rope_base = 500000.0
far_position = 1 << 30


def from_behind(value, axis, steps):
    count = lax.axis_size(axis)
    leading, last = (max(0, -steps), min(count, count - steps))
    return lax.ppermute(value, axis, [(source, source + steps) for source in range(leading, last)])


def prefix(value, axis, join, neutral):
    count, mine = (lax.axis_size(axis), lax.axis_index(axis))
    pieces = lax.all_gather(value, axis)
    subtotal = jnp.full_like(value, 0) + jnp.asarray(neutral, value.dtype)

    def hop(position, subtotal):
        longer = join(subtotal, pieces[position])
        return jnp.where(position < mine, longer, subtotal)

    return lax.fori_loop(0, count - 1, hop, subtotal)


def shortened(value):

    def short(part):
        return part.astype(jnp.bfloat16) if part.dtype == jnp.float32 else part

    return jax.tree.map(short, value)


def rms_scale(values, gain_row):
    mean_square = jnp.mean(values * values, axis=-1, keepdims=True)
    return values * lax.rsqrt(mean_square + epsilon) * gain_row


def masked_softmax(scores, allowed):
    scores = jnp.where(allowed, scores, -1e30)
    largest = jnp.max(scores, axis=-1, keepdims=True)
    raised = jnp.where(allowed, jnp.exp(scores - largest), 0.0)
    return raised / jnp.sum(raised, axis=-1, keepdims=True)


def rotate(values, position):
    halfway = values.shape[-1] // 2
    frequency = jnp.power(
        rope_base, -2.0 * jnp.arange(halfway, dtype=jnp.float32) / values.shape[-1]
    )
    angles = position.astype(jnp.float32)[:, None] * frequency[None, :]
    cosine = jnp.cos(angles)[:, None, :]
    sine_rows = jnp.sin(angles)[:, None, :]
    lower_half = values[..., :halfway]
    upper_half = values[..., halfway:]
    return jnp.concatenate(
        [
            lower_half * cosine - upper_half * sine_rows,
            upper_half * cosine + lower_half * sine_rows,
        ],
        axis=-1,
    )


def patch_block(extended, first_byte, end_byte, in_use, anchor, lift, cross_kv):
    columns = anchor + jnp.arange(extended.shape[0], dtype=jnp.int32)
    inside = (
        (columns[None, :] >= first_byte[:, None])
        & (columns[None, :] < end_byte[:, None])
        & in_use[:, None]
    )
    member = inside.astype(jnp.bfloat16)
    totals = jnp.dot(member, extended, preferred_element_type=jnp.float32)
    lengths = jnp.maximum(jnp.sum(inside.astype(jnp.float32), axis=1), 1.0)
    pooled = (totals / lengths[:, None]).astype(jnp.bfloat16)
    lifted = jnp.dot(pooled, lift, preferred_element_type=jnp.float32)
    key_rows = jnp.dot(extended, cross_kv[0], preferred_element_type=jnp.float32).astype(
        jnp.bfloat16
    )
    value_rows = jnp.dot(extended, cross_kv[1], preferred_element_type=jnp.float32).astype(
        jnp.bfloat16
    )
    slot_total = first_byte.shape[0]
    head_count = lifted.shape[1] // HD
    queries = lifted.astype(jnp.bfloat16).reshape(slot_total, head_count, HD)
    scores = jnp.einsum(
        "phd,khd->hpk",
        queries,
        key_rows.reshape(-1, head_count, HD),
        preferred_element_type=jnp.float32,
    ) * (1.0 / math.sqrt(HD))
    allowed = inside | (~in_use)[:, None] & (columns[None, :] == anchor)
    weights = masked_softmax(scores, allowed[None]).astype(jnp.bfloat16)
    crossed = jnp.einsum(
        "hpk,khd->phd",
        weights,
        value_rows.reshape(-1, head_count, HD),
        preferred_element_type=jnp.float32,
    )
    crossed = crossed.reshape(slot_total, head_count * HD)
    return jnp.where(in_use[:, None], lifted + crossed, 0.0).astype(jnp.bfloat16)


def add_counts(earlier, later):
    return earlier + later


def gathered_shards(
    byte_states,
    enc_gain,
    enc_qkv,
    enc_proj_out,
    starts,
    counts,
    lift,
    cross_kv,
    latent_gain,
    lat_qkv,
    lat_proj_out,
):
    byte_rows = byte_states.shape[0]
    anchor = lax.axis_index("seq") * byte_rows
    states = byte_states.astype(jnp.float32)
    normed = rms_scale(states, enc_gain.astype(jnp.float32)).astype(jnp.bfloat16)
    projected = jnp.einsum(
        "bd,idc->ibc", normed, enc_qkv, preferred_element_type=jnp.float32
    ).astype(jnp.bfloat16)
    reach_blocks = max(WIN // byte_rows, 1)
    tail_rows = min(WIN, byte_rows)
    key_parts = []
    value_parts = []
    for distance in range(reach_blocks, 0, -1):
        moved_keys, moved_values = from_behind(
            (projected[1, byte_rows - tail_rows :], projected[2, byte_rows - tail_rows :]),
            "seq",
            distance,
        )
        key_parts.append(moved_keys)
        value_parts.append(moved_values)
    key_rows = jnp.concatenate(key_parts + [projected[1]], axis=0)
    value_rows = jnp.concatenate(value_parts + [projected[2]], axis=0)
    head_count = projected.shape[2] // EH
    scores = jnp.einsum(
        "qhd,khd->hqk",
        projected[0].reshape(byte_rows, head_count, EH),
        key_rows.reshape(-1, head_count, EH),
        preferred_element_type=jnp.float32,
    ) * (1.0 / math.sqrt(EH))
    query_pos = anchor + jnp.arange(byte_rows, dtype=jnp.int32)
    key_pos = anchor - WIN + jnp.arange(WIN + byte_rows, dtype=jnp.int32)
    allowed = (
        (key_pos[None, :] <= query_pos[:, None])
        & (key_pos[None, :] > query_pos[:, None] - WIN)
        & (key_pos[None, :] >= 0)
    )
    weights = masked_softmax(scores, allowed[None]).astype(jnp.bfloat16)
    attended = jnp.einsum(
        "hqk,khd->qhd",
        weights,
        value_rows.reshape(-1, head_count, EH),
        preferred_element_type=jnp.float32,
    )
    attended = attended.reshape(byte_rows, head_count * EH).astype(jnp.bfloat16)
    blended = lax.psum(jnp.dot(attended, enc_proj_out, preferred_element_type=jnp.float32), "tp")
    encoded = (states + blended).astype(jnp.bfloat16)
    patch_count = counts[0]
    local_starts = starts[0]
    first_local = (local_starts[0:1] - anchor).astype(jnp.bfloat16)
    next_rows, next_first = from_behind((encoded[:SPILL], first_local), "seq", -1)
    next_first = next_first.astype(jnp.int32)[0]
    extended = jnp.concatenate([encoded, next_rows], axis=0)
    slot_ids = jnp.arange(local_starts.shape[0], dtype=jnp.int32)
    in_use = slot_ids < patch_count
    following = jnp.concatenate([local_starts[1:], jnp.zeros((1,), jnp.int32)])
    patch_end = jnp.where(slot_ids + 1 < patch_count, following, anchor + byte_rows + next_first)
    patches = patch_block(extended, local_starts, patch_end, in_use, anchor, lift, cross_kv)
    offset = prefix(counts, "seq", add_counts, jnp.zeros((1,), jnp.int32))[0]
    position = offset + slot_ids
    slot_total = patches.shape[0]
    full_rows = lax.all_gather(patches, "tp", axis=1, tiled=True)
    normed_rows = rms_scale(full_rows.astype(jnp.float32), latent_gain.astype(jnp.float32)).astype(
        jnp.bfloat16
    )
    inner_width = lat_qkv.shape[2]
    projected = jnp.einsum(
        "pd,idc->ipc",
        normed_rows,
        lax.all_gather(lat_qkv, "seq", axis=1, tiled=True),
        preferred_element_type=jnp.float32,
    )
    heads_here = inner_width // HD
    queries = rotate(projected[0].reshape(slot_total, heads_here, HD), position).astype(
        jnp.bfloat16
    )
    latent_keys = (
        rotate(projected[1].reshape(slot_total, heads_here, HD), position)
        .astype(jnp.bfloat16)
        .reshape(slot_total, inner_width)
    )
    latent_values = projected[2].astype(jnp.bfloat16)
    latent_pos = jnp.where(in_use, position, far_position)
    largest = jnp.full((heads_here, slot_total), -1e30, jnp.float32)
    piece_keys = lax.all_gather(latent_keys, "seq", axis=0, tiled=True)
    piece_values = lax.all_gather(latent_values, "seq", axis=0, tiled=True)
    piece_pos = lax.all_gather(shortened(latent_pos), "seq", axis=0, tiled=True)
    rows_here = piece_keys.shape[0]
    piece_scores = jnp.einsum(
        "qhd,khd->hqk",
        queries,
        piece_keys.reshape(rows_here, heads_here, HD),
        preferred_element_type=jnp.float32,
    ) * (1.0 / math.sqrt(HD))
    permitted = (piece_pos[None, :] <= position[:, None])[None]
    piece_scores = jnp.where(permitted, piece_scores, -1e30)
    renewed = jnp.maximum(largest, jnp.max(piece_scores, axis=-1))
    raised = jnp.where(permitted, jnp.exp(piece_scores - renewed[..., None]), 0.0)
    weight_sum = jnp.sum(raised, axis=-1)
    weighted = jnp.einsum(
        "hqk,khd->hqd",
        raised.astype(jnp.bfloat16),
        piece_values.reshape(rows_here, heads_here, HD),
        preferred_element_type=jnp.float32,
    )
    largest, weight_sum, weighted = (renewed, weight_sum, weighted)
    latent_heads = (
        (weighted / weight_sum[..., None])
        .transpose(1, 0, 2)
        .reshape(slot_total, inner_width)
        .astype(jnp.bfloat16)
    )
    partials = jnp.dot(
        latent_heads,
        lax.all_gather(lat_proj_out, "seq", axis=1, tiled=True),
        preferred_element_type=jnp.float32,
    )
    reduced = lax.psum_scatter(partials, "tp", scatter_dimension=1, tiled=True)
    latent = jnp.where(in_use[:, None], patches.astype(jnp.float32) + reduced, 0.0).astype(
        jnp.bfloat16
    )
    return (encoded, latent)


MESH = pl.DeviceIdType.MESH
EDGE = 16


def greet(peers):
    barrier = pltpu.get_barrier_semaphore()
    for peer in peers:
        pl.semaphore_signal(barrier, inc=1, device_id=peer, device_id_type=MESH)
    pl.semaphore_wait(barrier, len(peers))


def exchange(values, out_shapes, plan, call_id):
    n_in, n_out = len(values), len(out_shapes)
    n_copies = 16

    def kernel(*refs):
        ins, outs = refs[:n_in], refs[n_in : n_in + n_out]
        send_sems, recv_sems = refs[n_in + n_out :]
        rounds = plan()
        greet([source for source, _, _ in rounds])
        copies = []
        for _, target, items in rounds:
            for in_id, in_view, out_id, out_view in items:
                copy = pltpu.make_async_remote_copy(
                    src_ref=in_view(ins[in_id]),
                    dst_ref=out_view(outs[out_id]),
                    send_sem=send_sems.at[len(copies)],
                    recv_sem=recv_sems.at[len(copies)],
                    device_id=target,
                    device_id_type=MESH,
                )
                copy.start()
                copies.append(copy)
        for copy in copies:
            copy.wait()

    return pl.pallas_call(
        kernel,
        out_shape=out_shapes,
        in_specs=[pl.BlockSpec(memory_space=pl.ANY)] * n_in,
        out_specs=[pl.BlockSpec(memory_space=pl.ANY)] * n_out,
        scratch_shapes=[
            pltpu.SemaphoreType.DMA((n_copies,)),
            pltpu.SemaphoreType.DMA((n_copies,)),
        ],
        compiler_params=pltpu.CompilerParams(collective_id=call_id, has_side_effects=True),
    )(*values)


def whole(ref):
    return ref


def slot(index):
    return lambda ref: ref.at[index]


def seq_peer(index):
    return {"seq": index}


def tp_peer(index):
    return {"tp": index}


def relay(value, count, spread, plane_first, call_id):
    block = value.shape[1:] if spread else value.shape

    def kernel(value_ref, out_ref, land, send_a, recv_a, send_b, recv_b, own_sem):
        s, t = lax.axis_index("seq"), lax.axis_index("tp")
        p, c = s // 2, lax.rem(s, 2)

        def plane(index):
            return {"seq": 2 * index + c}

        if plane_first:
            a, b, first, second = p, t, plane, tp_peer
        else:
            a, b, first, second = t, p, tp_peer, plane
        others_a = [lax.rem(a + k, count) for k in range(1, count)]
        others_b = [lax.rem(b + k, count) for k in range(1, count)]
        greet([first(i) for i in others_a] + [second(i) for i in others_b])
        hops = []
        for k in range(1, count):
            target = lax.rem(a + k, count)
            hop = pltpu.make_async_remote_copy(
                src_ref=value_ref.at[target] if spread else value_ref,
                dst_ref=land.at[k - 1],
                send_sem=send_a.at[k - 1],
                recv_sem=recv_a.at[k - 1],
                device_id=first(target),
                device_id_type=MESH,
            )
            hop.start()
            hops.append(hop)
        onward = []
        for k in range(count):
            origin = lax.rem(a + count - k, count)
            if k == 0:
                here = value_ref.at[a] if spread else value_ref
            else:
                hops[k - 1].wait_recv()
                here = land.at[k - 1]
            away = pltpu.make_async_remote_copy(
                src_ref=here,
                dst_ref=out_ref.at[b],
                send_sem=send_b.at[k],
                recv_sem=recv_b.at[b],
                device_id=second(origin),
                device_id_type=MESH,
            )
            stay = pltpu.make_async_copy(here, out_ref.at[b], own_sem)
            onward.append((origin, away, stay))

            @pl.when(origin != b)
            def _():
                away.start()

            @pl.when(origin == b)
            def _():
                stay.start()

        for q in range(count):

            @pl.when(b != q)
            def _():
                pltpu.make_async_remote_copy(
                    src_ref=land.at[0],
                    dst_ref=out_ref.at[q],
                    send_sem=send_b.at[q],
                    recv_sem=recv_b.at[q],
                    device_id=second(b),
                    device_id_type=MESH,
                ).wait_recv()

        for hop in hops:
            hop.wait_send()
        for origin, away, stay in onward:

            @pl.when(origin != b)
            def _():
                away.wait_send()

            @pl.when(origin == b)
            def _():
                stay.wait()

    return pl.pallas_call(
        kernel,
        out_shape=jax.ShapeDtypeStruct((count, *block), value.dtype),
        in_specs=[pl.BlockSpec(memory_space=pltpu.VMEM)],
        out_specs=pl.BlockSpec(memory_space=pl.ANY),
        scratch_shapes=[
            pltpu.VMEM((count - 1, *block), value.dtype),
            pltpu.SemaphoreType.DMA((count - 1,)),
            pltpu.SemaphoreType.DMA((count - 1,)),
            pltpu.SemaphoreType.DMA((count,)),
            pltpu.SemaphoreType.DMA((count,)),
            pltpu.SemaphoreType.DMA,
        ],
        compiler_params=pltpu.CompilerParams(collective_id=call_id, has_side_effects=True),
    )(value)


def like(shape, dtype=jnp.bfloat16):
    return jax.ShapeDtypeStruct(shape, dtype)


def halo(projected, byte_states, info):
    size = lax.axis_size("seq")
    rows, width = projected.shape[1:]
    reach = WIN // rows

    def plan():
        s = lax.axis_index("seq")
        rounds = []
        for k in range(1, size):
            items = []
            if k <= reach:
                items.append((0, lambda ref: ref.at[pl.ds(1, 2)], 0, slot(k - 1)))
            if k == size - 1:
                items.append((0, lambda ref: ref.at[:, pl.ds(0, EDGE)], 1, whole))
                items.append((1, lambda ref: ref.at[pl.ds(0, EDGE)], 2, whole))
            items.append((2, whole, 3, slot(k - 1)))
            rounds.append(
                (seq_peer(lax.rem(s + size - k, size)), seq_peer(lax.rem(s + k, size)), items)
            )
        return rounds

    return exchange(
        [projected, byte_states, info],
        [
            like((reach, 2, rows, width)),
            like((3, EDGE, width)),
            like((EDGE, byte_states.shape[1])),
            like((size - 1, 8, 128), jnp.int32),
        ],
        plan,
        1,
    )


def blend_and_patch(attended, proj, byte_states, edge_states, bounds, used, lift, cross_kv, call_id):
    count = lax.axis_size("tp")
    byte_rows, width = byte_states.shape
    share = byte_rows // count
    chunks = 2
    piece = share // chunks
    slots = bounds[0].shape[0]
    columns = lift.shape[1]
    total_rows = byte_rows + EDGE

    def kernel(
        att_ref, proj_ref, states_ref, edge_ref, lo_ref, hi_ref, used_ref, lift_hbm, cross_hbm,
        full_ref, patch_ref,
        sends, lands, tail_send, tail_land, blocks, lift_ref, cross_ref, pooled_ref,
        load_sems, rs_send, rs_recv, tail_s, tail_r, up_send, down_send, ag_recv,
    ):
        t = lax.axis_index("tp")
        loads = [
            pltpu.make_async_copy(lift_hbm, lift_ref, load_sems.at[0]),
            pltpu.make_async_copy(cross_hbm, cross_ref, load_sems.at[1]),
        ]
        for load in loads:
            load.start()
        blend = jnp.dot(att_ref[...], proj_ref[...], preferred_element_type=jnp.float32).astype(
            jnp.bfloat16
        )
        for q in range(count):
            for h in range(chunks):
                begin = q * share + h * piece
                sends[q, h] = blend[begin : begin + piece]
        tail_send[...] = blend[byte_rows:]
        greet([tp_peer(lax.rem(t + k, count)) for k in range(1, count)])
        scatter = [[], []]
        for h in range(chunks):
            for k in range(1, count):
                target = lax.rem(t + k, count)
                copy = pltpu.make_async_remote_copy(
                    src_ref=sends.at[target, h],
                    dst_ref=lands.at[h, k - 1],
                    send_sem=rs_send.at[h, k - 1],
                    recv_sem=rs_recv.at[h, k - 1],
                    device_id=tp_peer(target),
                    device_id_type=MESH,
                )
                copy.start()
                scatter[h].append(copy)
        tails = []
        for k in range(1, count):
            copy = pltpu.make_async_remote_copy(
                src_ref=tail_send,
                dst_ref=tail_land.at[k - 1],
                send_sem=tail_s.at[k - 1],
                recv_sem=tail_r.at[k - 1],
                device_id=tp_peer(lax.rem(t + k, count)),
                device_id_type=MESH,
            )
            copy.start()
            tails.append(copy)

        def pass_on(origin, h, up):
            step = 1 if up else -1
            return pltpu.make_async_remote_copy(
                src_ref=blocks.at[origin, h],
                dst_ref=blocks.at[origin, h],
                send_sem=(up_send if up else down_send).at[origin, h],
                recv_sem=ag_recv.at[origin, h],
                device_id=tp_peer(lax.rem(t + step + count, count)),
                device_id_type=MESH,
            )

        for h in range(chunks):
            for copy in scatter[h]:
                copy.wait_recv()
            total = sends[t, h].astype(jnp.float32)
            for k in range(count - 1):
                total = total + lands[h, k].astype(jnp.float32)
            rows = pl.ds(pl.multiple_of(t * share + h * piece, piece), piece)
            blocks[t, h] = (states_ref[rows].astype(jnp.float32) + total).astype(jnp.bfloat16)

            @pl.when(t < count - 1)
            def _():
                pass_on(t, h, True).start()

            @pl.when(t > 0)
            def _():
                pass_on(t, h, False).start()

        for copy in tails:
            copy.wait_recv()
        total = tail_send[...].astype(jnp.float32)
        for k in range(count - 1):
            total = total + tail_land[k].astype(jnp.float32)
        full_ref[byte_rows:] = (edge_ref[...].astype(jnp.float32) + total).astype(jnp.bfloat16)

        for d in range(1, count):
            for h in range(chunks):

                @pl.when(t - d >= 0)
                def _():
                    pass_on(t - d, h, True).wait_recv()

                    @pl.when(t < count - 1)
                    def _():
                        pass_on(t - d, h, True).start()

                @pl.when(t + d < count)
                def _():
                    pass_on(t + d, h, False).wait_recv()

                    @pl.when(t > 0)
                    def _():
                        pass_on(t + d, h, False).start()

        for q in range(count):
            for h in range(chunks):
                begin = q * share + h * piece
                full_ref[begin : begin + piece] = blocks[q, h]
        for load in loads:
            load.wait()

        where_at = lax.broadcasted_iota(jnp.int32, (slots, total_rows), 1)
        allowed = (where_at >= lo_ref[...]) & (where_at < hi_ref[...])
        in_use = used_ref[...] > 0.0
        member = jnp.where(allowed & in_use, 1.0, 0.0)
        lengths = jnp.maximum(jnp.sum(member, axis=1, keepdims=True), 1.0)
        totals = jnp.dot(
            member.astype(jnp.bfloat16), full_ref[...], preferred_element_type=jnp.float32
        )
        pooled_ref[...] = (totals / lengths).astype(jnp.bfloat16)
        group = 2 * HD

        def heads(i, carry):
            cols = pl.ds(pl.multiple_of(i * group, group), group)
            rows = full_ref[...]
            lifted = jnp.dot(pooled_ref[...], lift_ref[:, cols], preferred_element_type=jnp.float32)
            keys = jnp.dot(rows, cross_ref[0, :, cols], preferred_element_type=jnp.float32).astype(
                jnp.bfloat16
            )
            values = jnp.dot(
                rows, cross_ref[1, :, cols], preferred_element_type=jnp.float32
            ).astype(jnp.bfloat16)
            queries = lifted.astype(jnp.bfloat16)
            crossed = []
            for j in range(2):
                lanes = slice(j * HD, (j + 1) * HD)
                scores = lax.dot_general(
                    queries[:, lanes],
                    keys[:, lanes],
                    (((1,), (1,)), ((), ())),
                    preferred_element_type=jnp.float32,
                ) * (1.0 / math.sqrt(HD))
                weights = masked_softmax(scores, allowed).astype(jnp.bfloat16)
                crossed.append(
                    jnp.dot(weights, values[:, lanes], preferred_element_type=jnp.float32)
                )
            patch = lifted + jnp.concatenate(crossed, axis=1)
            patch_ref[:, cols] = jnp.where(in_use, patch, 0.0).astype(jnp.bfloat16)
            return carry

        lax.fori_loop(0, columns // group, heads, 0)

        for h in range(chunks):
            for copy in scatter[h]:
                copy.wait_send()
        for copy in tails:
            copy.wait_send()
        for q in range(count):
            for h in range(chunks):

                @pl.when((q <= t) & (t < count - 1))
                def _():
                    pass_on(q, h, True).wait_send()

                @pl.when((q >= t) & (t > 0))
                def _():
                    pass_on(q, h, False).wait_send()

    vmem = pl.BlockSpec(memory_space=pltpu.VMEM)
    hbm = pl.BlockSpec(memory_space=pl.ANY)
    dma = pltpu.SemaphoreType.DMA
    return pl.pallas_call(
        kernel,
        out_shape=[like((total_rows, width)), like((slots, columns))],
        in_specs=[vmem] * 7 + [hbm] * 2,
        out_specs=[vmem, vmem],
        scratch_shapes=[
            pltpu.VMEM((count, chunks, piece, width), jnp.bfloat16),
            pltpu.VMEM((chunks, count - 1, piece, width), jnp.bfloat16),
            pltpu.VMEM((EDGE, width), jnp.bfloat16),
            pltpu.VMEM((count - 1, EDGE, width), jnp.bfloat16),
            pltpu.VMEM((count, chunks, piece, width), jnp.bfloat16),
            pltpu.VMEM(lift.shape, lift.dtype),
            pltpu.VMEM(cross_kv.shape, cross_kv.dtype),
            pltpu.VMEM((slots, width), jnp.bfloat16),
            dma((2,)),
            dma((chunks, count - 1)),
            dma((chunks, count - 1)),
            dma((count - 1,)),
            dma((count - 1,)),
            dma((count, chunks)),
            dma((count, chunks)),
            dma((count, chunks)),
        ],
        compiler_params=pltpu.CompilerParams(collective_id=call_id, has_side_effects=True),
    )(attended, proj, byte_states, edge_states, *bounds, used, lift, cross_kv)


def latent_stage(rows, patches, used, gain, weights, projs, cosine, sine, query_pos, key_pos, call_id):
    count = lax.axis_size("tp")
    row_total, chip_width = rows.shape
    half = chip_width // 2
    slots, columns = patches.shape
    full_width = columns * count

    def kernel(
        rows_ref, patch_ref, used_ref, gain_ref, cos_ref, sin_ref, qpos_ref, kpos_ref,
        w_own_hbm, w_other_hbm, o_own_hbm, o_other_hbm,
        out_ref,
        w_own, w_other, o_own, o_other, geared, qkv_send, qkv_land, sq_send, sq_land,
        kv_own, kv_other, att_all, parts, land, final,
        load_sems, qkv_s, qkv_r, sq_s, sq_r, kv_sems, att_s, att_r, a_s, a_r, b_s, b_r,
    ):
        s, t = lax.axis_index("seq"), lax.axis_index("tp")
        p, c = s // 2, lax.rem(s, 2)
        pair_refs = ((w_own_hbm, w_own), (w_other_hbm, w_other), (o_own_hbm, o_own), (o_other_hbm, o_other))
        loads = [
            pltpu.make_async_copy(source, target, load_sems.at[i])
            for i, (source, target) in enumerate(pair_refs)
        ]
        for load in loads:
            load.start()

        def plane(index):
            return {"seq": 2 * index + c}

        partner = seq_peer(s + 1 - 2 * c)
        greet(
            [plane(lax.rem(p + k, count)) for k in range(1, count)]
            + [tp_peer(lax.rem(t + k, count)) for k in range(1, count)]
            + [partner]
        )

        def send(source, target, send_sem, recv_sem, device):
            return pltpu.make_async_remote_copy(
                src_ref=source,
                dst_ref=target,
                send_sem=send_sem,
                recv_sem=recv_sem,
                device_id=device,
                device_id_type=MESH,
            )

        values = rows_ref[...].astype(jnp.float32)
        squares = jnp.sum(values * values, axis=1, keepdims=True)
        eye = lax.broadcasted_iota(jnp.int32, (row_total, row_total), 0) == lax.broadcasted_iota(
            jnp.int32, (row_total, row_total), 1
        )
        flat = jnp.sum(jnp.where(eye, squares, 0.0), axis=0, keepdims=True)
        sq_send[...] = jnp.broadcast_to(flat, sq_send.shape)
        geared[...] = (values * gain_ref[...]).astype(jnp.bfloat16)
        sent = []
        for k in range(1, count):
            copy = send(
                sq_send, sq_land.at[k - 1], sq_s.at[k - 1], sq_r.at[k - 1], plane(lax.rem(p + k, count))
            )
            copy.start()
            sent.append(copy)
        loads[0].wait()
        loads[1].wait()
        mine = geared[:, pl.ds(pl.multiple_of(c * half, half), half)]
        theirs = geared[:, pl.ds(pl.multiple_of((1 - c) * half, half), half)]
        total = []
        for k in list(range(1, count)) + [0]:
            target = lax.rem(p + k, count)
            lanes = pl.ds(pl.multiple_of(target * HD, HD), HD)
            for i in range(3):
                part = jnp.dot(
                    mine, w_own[i, :, lanes], preferred_element_type=jnp.float32
                ) + jnp.dot(theirs, w_other[i, :, lanes], preferred_element_type=jnp.float32)
                if k:
                    qkv_send[k - 1, i] = part.astype(jnp.bfloat16)
                else:
                    total.append(part)
            if k:
                copy = send(
                    qkv_send.at[k - 1], qkv_land.at[k - 1], qkv_s.at[k - 1], qkv_r.at[k - 1], plane(target)
                )
                copy.start()
                sent.append(copy)
        for copy in sent:
            copy.wait_recv()
        flat = flat + jnp.sum(sq_land[:, 0:1, :], axis=0)
        square_sum = jnp.sum(jnp.where(eye, flat, 0.0), axis=1, keepdims=True)
        scale = lax.rsqrt(square_sum / full_width + epsilon)
        for i in range(3):
            for k in range(count - 1):
                total[i] = total[i] + qkv_land[k, i].astype(jnp.float32)
            total[i] = total[i] * scale

        def turned(vectors):
            return (
                vectors * cos_ref[...] + pltpu.roll(vectors, HD // 2, 1) * sin_ref[...]
            ).astype(jnp.bfloat16)

        queries = turned(total[0])
        kv_own[0] = turned(total[1])
        kv_own[1] = total[2].astype(jnp.bfloat16)
        swap = send(kv_own, kv_other, kv_sems.at[0], kv_sems.at[1], partner)
        swap.start()

        def scored(keys, first):
            scores = lax.dot_general(
                queries, keys, (((1,), (1,)), ((), ())), preferred_element_type=jnp.float32
            ) * (1.0 / math.sqrt(HD))
            permitted = kpos_ref[:, first : first + row_total] <= qpos_ref[...]
            return jnp.where(permitted, scores, -1e30), permitted

        scores_a, permitted_a = scored(kv_own[0], 0)
        swap.wait_recv()
        scores_b, permitted_b = scored(kv_other[0], row_total)
        largest = jnp.maximum(
            jnp.max(scores_a, axis=1, keepdims=True), jnp.max(scores_b, axis=1, keepdims=True)
        )
        raised_a = jnp.where(permitted_a, jnp.exp(scores_a - largest), 0.0)
        raised_b = jnp.where(permitted_b, jnp.exp(scores_b - largest), 0.0)
        weight_sum = jnp.sum(raised_a, axis=1, keepdims=True) + jnp.sum(
            raised_b, axis=1, keepdims=True
        )
        weighted = jnp.dot(
            raised_a.astype(jnp.bfloat16), kv_own[1], preferred_element_type=jnp.float32
        ) + jnp.dot(raised_b.astype(jnp.bfloat16), kv_other[1], preferred_element_type=jnp.float32)
        att_all[p] = (weighted / weight_sum).astype(jnp.bfloat16)
        heads = []
        for k in range(1, count):
            copy = send(
                att_all.at[p], att_all.at[p], att_s.at[k - 1], att_r.at[p], plane(lax.rem(p + k, count))
            )
            copy.start()
            heads.append(copy)
        for k in range(1, count):
            source = lax.rem(p + k, count)
            send(
                att_all.at[source], att_all.at[source], att_s.at[k - 1], att_r.at[source], plane(source)
            ).wait_recv()
        loads[2].wait()
        loads[3].wait()
        hops = []
        for k in list(range(1, count)) + [0]:
            target = lax.rem(p + k, count)
            take = pl.ds(pl.multiple_of(target * slots, slots), slots)
            attended = jnp.concatenate([att_all[j, take, :] for j in range(count)], axis=1)
            for output, core in ((o_own, c), (o_other, 1 - c)):
                parts[target, :, pl.ds(pl.multiple_of(core * half, half), half)] = jnp.dot(
                    attended, output[...], preferred_element_type=jnp.float32
                ).astype(jnp.bfloat16)
            if k:
                hop = send(
                    parts.at[target], land.at[k - 1], a_s.at[k - 1], a_r.at[k - 1], plane(target)
                )
                hop.start()
                hops.append(hop)
        onward = []
        for k in range(count):
            origin = lax.rem(p + count - k, count)
            if k == 0:
                here = parts.at[p]
            else:
                hops[k - 1].wait_recv()
                here = land.at[k - 1]
            away = send(here, final.at[t], b_s.at[k], b_r.at[t], tp_peer(origin))
            onward.append((origin, away))

            @pl.when(origin != t)
            def _():
                away.start()

            @pl.when(origin == t)
            def _():
                final[t] = here[...]

        summed = patch_ref[...].astype(jnp.float32)
        for q in range(count):

            @pl.when(t != q)
            def _():
                send(land.at[0], final.at[q], b_s.at[q], b_r.at[q], tp_peer(t)).wait_recv()

            summed = summed + final[q].astype(jnp.float32)
        out_ref[...] = jnp.where(used_ref[...] > 0.0, summed, 0.0).astype(jnp.bfloat16)
        for copy in sent + heads + hops + [swap]:
            copy.wait_send()
        for origin, away in onward:

            @pl.when(origin != t)
            def _():
                away.wait_send()

    vmem = pl.BlockSpec(memory_space=pltpu.VMEM)
    hbm = pl.BlockSpec(memory_space=pl.ANY)
    dma = pltpu.SemaphoreType.DMA
    near = count - 1
    return pl.pallas_call(
        kernel,
        out_shape=like((slots, columns)),
        in_specs=[vmem] * 8 + [hbm] * 4,
        out_specs=vmem,
        scratch_shapes=[
            pltpu.VMEM(weights[0].shape, jnp.bfloat16),
            pltpu.VMEM(weights[1].shape, jnp.bfloat16),
            pltpu.VMEM(projs[0].shape, jnp.bfloat16),
            pltpu.VMEM(projs[1].shape, jnp.bfloat16),
            pltpu.VMEM((row_total, chip_width), jnp.bfloat16),
            pltpu.VMEM((near, 3, row_total, HD), jnp.bfloat16),
            pltpu.VMEM((near, 3, row_total, HD), jnp.bfloat16),
            pltpu.VMEM((8, row_total), jnp.float32),
            pltpu.VMEM((near, 8, row_total), jnp.float32),
            pltpu.VMEM((2, row_total, HD), jnp.bfloat16),
            pltpu.VMEM((2, row_total, HD), jnp.bfloat16),
            pltpu.VMEM((count, row_total, HD), jnp.bfloat16),
            pltpu.VMEM((count, slots, columns), jnp.bfloat16),
            pltpu.VMEM((near, slots, columns), jnp.bfloat16),
            pltpu.VMEM((count, slots, columns), jnp.bfloat16),
            dma((4,)),
            dma((near,)),
            dma((near,)),
            dma((near,)),
            dma((near,)),
            dma((2,)),
            dma((near,)),
            dma((count,)),
            dma((near,)),
            dma((near,)),
            dma((count,)),
            dma((count,)),
        ],
        compiler_params=pltpu.CompilerParams(collective_id=call_id, has_side_effects=True),
    )(rows, patches, used, gain, cosine, sine, query_pos, key_pos, *weights, *projs)


def shards(
    byte_states,
    enc_gain,
    enc_qkv,
    enc_proj_out,
    starts,
    counts,
    lift,
    cross_kv,
    latent_gain,
    lat_qkv,
    lat_proj_out,
):
    size, tp_size = lax.axis_size("seq"), lax.axis_size("tp")
    s, t = lax.axis_index("seq"), lax.axis_index("tp")
    pairs = size // 2
    p, c = s // 2, lax.rem(s, 2)
    byte_rows = byte_states.shape[0]
    anchor = s * byte_rows
    both = [(i, i ^ 1) for i in range(size)]
    lat_qkv_other = lax.ppermute(lat_qkv, "seq", both)
    lat_proj_other = lax.ppermute(lat_proj_out, "seq", both)
    states = byte_states.astype(jnp.float32)
    normed = rms_scale(states, enc_gain.astype(jnp.float32)).astype(jnp.bfloat16)
    projected = jnp.einsum(
        "bd,idc->ibc", normed, enc_qkv, preferred_element_type=jnp.float32
    ).astype(jnp.bfloat16)
    patch_count = counts[0]
    local_starts = starts[0]
    lanes = lax.broadcasted_iota(jnp.int32, (8, 128), 1)
    info = jnp.where(lanes == 0, patch_count, jnp.where(lanes == 1, local_starts[0], 0))
    behind, edge, edge_states, infos = halo(projected, byte_states, info)
    reach = WIN // byte_rows
    key_rows = jnp.concatenate(
        [behind[k, 0] for k in range(reach - 1, -1, -1)] + [projected[1], edge[1]], axis=0
    )
    value_rows = jnp.concatenate(
        [behind[k, 1] for k in range(reach - 1, -1, -1)] + [projected[2], edge[2]], axis=0
    )
    query_rows = jnp.concatenate([projected[0], edge[0]], axis=0)
    total_rows = byte_rows + EDGE
    head_count = projected.shape[2] // EH
    scores = jnp.einsum(
        "qhd,khd->hqk",
        query_rows.reshape(total_rows, head_count, EH),
        key_rows.reshape(-1, head_count, EH),
        preferred_element_type=jnp.float32,
    ) * (1.0 / math.sqrt(EH))
    query_pos = anchor + jnp.arange(total_rows, dtype=jnp.int32)
    key_pos = anchor - WIN + jnp.arange(WIN + total_rows, dtype=jnp.int32)
    allowed = (
        (key_pos[None, :] <= query_pos[:, None])
        & (key_pos[None, :] > query_pos[:, None] - WIN)
        & (key_pos[None, :] >= 0)
    )
    weights = masked_softmax(scores, allowed[None]).astype(jnp.bfloat16)
    attended = jnp.einsum(
        "hqk,khd->qhd",
        weights,
        value_rows.reshape(-1, head_count, EH),
        preferred_element_type=jnp.float32,
    )
    attended = attended.reshape(total_rows, head_count * EH).astype(jnp.bfloat16)
    recent = jnp.concatenate([info[None], infos], axis=0)
    ring = jnp.arange(size, dtype=jnp.int32)
    from_ring = lax.rem(s - ring + size, size)
    placed = from_ring[None, :] == ring[:, None]
    count_list = jnp.sum(jnp.where(placed, recent[None, :, 0, 0], 0), axis=1)
    offsets = jnp.sum(jnp.where(ring[None, :] < ring[:, None], count_list[None, :], 0), axis=1)
    next_first = jnp.where(s + 1 < size, recent[size - 1, 0, 1], size * byte_rows)

    slot_total = local_starts.shape[0]
    slot_ids = jnp.arange(slot_total, dtype=jnp.int32)
    in_use = slot_ids < patch_count
    following = jnp.concatenate([local_starts[1:], jnp.zeros((1,), jnp.int32)])
    patch_end = jnp.where(slot_ids + 1 < patch_count, following, next_first)
    lower = jnp.where(in_use, local_starts - anchor, 0)[:, None]
    upper = jnp.where(in_use, patch_end - anchor, 1)[:, None]
    used_rows = in_use.astype(jnp.float32)[:, None]
    extended, patches = blend_and_patch(
        attended,
        enc_proj_out,
        byte_states,
        edge_states,
        (lower, upper),
        used_rows,
        lift,
        cross_kv,
        2,
    )
    encoded = extended[:byte_rows]

    def slots_of(core):
        members = 2 * jnp.arange(pairs, dtype=jnp.int32) + core
        hit = members[:, None] == ring[None, :]
        begin = jnp.sum(jnp.where(hit, offsets[None, :], 0), axis=1)
        used = jnp.sum(jnp.where(hit, count_list[None, :], 0), axis=1)
        position = (begin[:, None] + slot_ids[None, :]).reshape(-1)
        return position, (slot_ids[None, :] < used[:, None]).reshape(-1)

    position, rows_used = slots_of(c)
    other_position, other_used = slots_of(1 - c)

    rows = relay(patches, pairs, False, False, 4).reshape(pairs * slot_total, -1)
    half = rows.shape[1] // 2
    gain = lax.dynamic_slice_in_dim(latent_gain, p * 2 * half, 2 * half, 0).astype(jnp.float32)
    frequency = jnp.power(
        rope_base, -2.0 * jnp.arange(HD // 2, dtype=jnp.float32) / HD
    )
    angles = position.astype(jnp.float32)[:, None] * frequency[None, :]
    sine = jnp.sin(angles)
    cosine = jnp.cos(angles)
    key_position = jnp.concatenate(
        [
            jnp.where(rows_used, position, far_position),
            jnp.where(other_used, other_position, far_position),
        ]
    )
    latent = latent_stage(
        rows,
        patches,
        used_rows,
        gain[None],
        (lat_qkv, lat_qkv_other),
        (lat_proj_out, lat_proj_other),
        jnp.concatenate([cosine, cosine], axis=1),
        jnp.concatenate([-sine, sine], axis=1),
        position[:, None],
        key_position[None, :],
        5,
    )
    return (encoded, latent)


def fits_pairs(mesh, byte_states, enc_qkv, starts, lat_qkv):
    size, tp_size = mesh.shape["seq"], mesh.shape["tp"]
    byte_rows = byte_states.shape[0] // size
    return (
        size == 2 * tp_size
        and WIN % byte_rows == 0
        and WIN // byte_rows < size
        and byte_rows % (32 * tp_size) == 0
        and lat_qkv.shape[2] // tp_size == HD * tp_size
        and lat_qkv.shape[1] % (128 * size) == 0
        and starts.shape[1] * tp_size % 128 == 0
        and starts.shape[1] * tp_size <= 1024
        and starts.shape[1] % 16 == 0
        and enc_qkv.shape[2] % (128 * tp_size) == 0
    )


def solution(mesh):
    specs = dict(
        mesh=mesh,
        in_specs=(
            P("seq", None),
            P(),
            P(None, None, "tp"),
            P("tp", None),
            P("seq", None),
            P("seq"),
            P(None, "tp"),
            P(None, None, "tp"),
            P(),
            P(None, "seq", "tp"),
            P("tp", "seq"),
        ),
        out_specs=(P("seq", None), P("seq", "tp")),
        check_vma=False,
    )

    def run(*arrays):
        paired = fits_pairs(mesh, arrays[0], arrays[2], arrays[4], arrays[9])
        return jax.shard_map(shards if paired else gathered_shards, **specs)(*arrays)

    return run
```

```python
import math

import jax
import jax.numpy as jnp
from jax import lax
from jax.experimental import pallas as pl
from jax.experimental.pallas import tpu as pltpu
from jax.sharding import PartitionSpec as P

EH = 64
HD = 128
WIN = 512
SPILL = 8


epsilon = 1e-05
rope_base = 500000.0
far_position = 1 << 30


def from_behind(value, axis, steps):
    count = lax.axis_size(axis)
    leading, last = (max(0, -steps), min(count, count - steps))
    return lax.ppermute(value, axis, [(source, source + steps) for source in range(leading, last)])


def prefix(value, axis, join, neutral):
    count, mine = (lax.axis_size(axis), lax.axis_index(axis))
    pieces = lax.all_gather(value, axis)
    subtotal = jnp.full_like(value, 0) + jnp.asarray(neutral, value.dtype)

    def hop(position, subtotal):
        longer = join(subtotal, pieces[position])
        return jnp.where(position < mine, longer, subtotal)

    return lax.fori_loop(0, count - 1, hop, subtotal)


def shortened(value):

    def short(part):
        return part.astype(jnp.bfloat16) if part.dtype == jnp.float32 else part

    return jax.tree.map(short, value)


def rms_scale(values, gain_row):
    mean_square = jnp.mean(values * values, axis=-1, keepdims=True)
    return values * lax.rsqrt(mean_square + epsilon) * gain_row


def masked_softmax(scores, allowed):
    scores = jnp.where(allowed, scores, -1e30)
    largest = jnp.max(scores, axis=-1, keepdims=True)
    raised = jnp.where(allowed, jnp.exp(scores - largest), 0.0)
    return raised / jnp.sum(raised, axis=-1, keepdims=True)


def rotate(values, position):
    halfway = values.shape[-1] // 2
    frequency = jnp.power(
        rope_base, -2.0 * jnp.arange(halfway, dtype=jnp.float32) / values.shape[-1]
    )
    angles = position.astype(jnp.float32)[:, None] * frequency[None, :]
    cosine = jnp.cos(angles)[:, None, :]
    sine_rows = jnp.sin(angles)[:, None, :]
    lower_half = values[..., :halfway]
    upper_half = values[..., halfway:]
    return jnp.concatenate(
        [
            lower_half * cosine - upper_half * sine_rows,
            upper_half * cosine + lower_half * sine_rows,
        ],
        axis=-1,
    )


def patch_block(extended, first_byte, end_byte, in_use, anchor, lift, cross_kv):
    columns = anchor + jnp.arange(extended.shape[0], dtype=jnp.int32)
    inside = (
        (columns[None, :] >= first_byte[:, None])
        & (columns[None, :] < end_byte[:, None])
        & in_use[:, None]
    )
    member = inside.astype(jnp.bfloat16)
    totals = jnp.dot(member, extended, preferred_element_type=jnp.float32)
    lengths = jnp.maximum(jnp.sum(inside.astype(jnp.float32), axis=1), 1.0)
    pooled = (totals / lengths[:, None]).astype(jnp.bfloat16)
    lifted = jnp.dot(pooled, lift, preferred_element_type=jnp.float32)
    key_rows = jnp.dot(extended, cross_kv[0], preferred_element_type=jnp.float32).astype(
        jnp.bfloat16
    )
    value_rows = jnp.dot(extended, cross_kv[1], preferred_element_type=jnp.float32).astype(
        jnp.bfloat16
    )
    slot_total = first_byte.shape[0]
    head_count = lifted.shape[1] // HD
    queries = lifted.astype(jnp.bfloat16).reshape(slot_total, head_count, HD)
    scores = jnp.einsum(
        "phd,khd->hpk",
        queries,
        key_rows.reshape(-1, head_count, HD),
        preferred_element_type=jnp.float32,
    ) * (1.0 / math.sqrt(HD))
    allowed = inside | (~in_use)[:, None] & (columns[None, :] == anchor)
    weights = masked_softmax(scores, allowed[None]).astype(jnp.bfloat16)
    crossed = jnp.einsum(
        "hpk,khd->phd",
        weights,
        value_rows.reshape(-1, head_count, HD),
        preferred_element_type=jnp.float32,
    )
    crossed = crossed.reshape(slot_total, head_count * HD)
    return jnp.where(in_use[:, None], lifted + crossed, 0.0).astype(jnp.bfloat16)


def add_counts(earlier, later):
    return earlier + later


def gathered_shards(
    byte_states,
    enc_gain,
    enc_qkv,
    enc_proj_out,
    starts,
    counts,
    lift,
    cross_kv,
    latent_gain,
    lat_qkv,
    lat_proj_out,
):
    byte_rows = byte_states.shape[0]
    anchor = lax.axis_index("seq") * byte_rows
    states = byte_states.astype(jnp.float32)
    normed = rms_scale(states, enc_gain.astype(jnp.float32)).astype(jnp.bfloat16)
    projected = jnp.einsum(
        "bd,idc->ibc", normed, enc_qkv, preferred_element_type=jnp.float32
    ).astype(jnp.bfloat16)
    reach_blocks = max(WIN // byte_rows, 1)
    tail_rows = min(WIN, byte_rows)
    key_parts = []
    value_parts = []
    for distance in range(reach_blocks, 0, -1):
        moved_keys, moved_values = from_behind(
            (projected[1, byte_rows - tail_rows :], projected[2, byte_rows - tail_rows :]),
            "seq",
            distance,
        )
        key_parts.append(moved_keys)
        value_parts.append(moved_values)
    key_rows = jnp.concatenate(key_parts + [projected[1]], axis=0)
    value_rows = jnp.concatenate(value_parts + [projected[2]], axis=0)
    head_count = projected.shape[2] // EH
    scores = jnp.einsum(
        "qhd,khd->hqk",
        projected[0].reshape(byte_rows, head_count, EH),
        key_rows.reshape(-1, head_count, EH),
        preferred_element_type=jnp.float32,
    ) * (1.0 / math.sqrt(EH))
    query_pos = anchor + jnp.arange(byte_rows, dtype=jnp.int32)
    key_pos = anchor - WIN + jnp.arange(WIN + byte_rows, dtype=jnp.int32)
    allowed = (
        (key_pos[None, :] <= query_pos[:, None])
        & (key_pos[None, :] > query_pos[:, None] - WIN)
        & (key_pos[None, :] >= 0)
    )
    weights = masked_softmax(scores, allowed[None]).astype(jnp.bfloat16)
    attended = jnp.einsum(
        "hqk,khd->qhd",
        weights,
        value_rows.reshape(-1, head_count, EH),
        preferred_element_type=jnp.float32,
    )
    attended = attended.reshape(byte_rows, head_count * EH).astype(jnp.bfloat16)
    blended = lax.psum(jnp.dot(attended, enc_proj_out, preferred_element_type=jnp.float32), "tp")
    encoded = (states + blended).astype(jnp.bfloat16)
    patch_count = counts[0]
    local_starts = starts[0]
    first_local = (local_starts[0:1] - anchor).astype(jnp.bfloat16)
    next_rows, next_first = from_behind((encoded[:SPILL], first_local), "seq", -1)
    next_first = next_first.astype(jnp.int32)[0]
    extended = jnp.concatenate([encoded, next_rows], axis=0)
    slot_ids = jnp.arange(local_starts.shape[0], dtype=jnp.int32)
    in_use = slot_ids < patch_count
    following = jnp.concatenate([local_starts[1:], jnp.zeros((1,), jnp.int32)])
    patch_end = jnp.where(slot_ids + 1 < patch_count, following, anchor + byte_rows + next_first)
    patches = patch_block(extended, local_starts, patch_end, in_use, anchor, lift, cross_kv)
    offset = prefix(counts, "seq", add_counts, jnp.zeros((1,), jnp.int32))[0]
    position = offset + slot_ids
    slot_total = patches.shape[0]
    full_rows = lax.all_gather(patches, "tp", axis=1, tiled=True)
    normed_rows = rms_scale(full_rows.astype(jnp.float32), latent_gain.astype(jnp.float32)).astype(
        jnp.bfloat16
    )
    inner_width = lat_qkv.shape[2]
    projected = jnp.einsum(
        "pd,idc->ipc",
        normed_rows,
        lax.all_gather(lat_qkv, "seq", axis=1, tiled=True),
        preferred_element_type=jnp.float32,
    )
    heads_here = inner_width // HD
    queries = rotate(projected[0].reshape(slot_total, heads_here, HD), position).astype(
        jnp.bfloat16
    )
    latent_keys = (
        rotate(projected[1].reshape(slot_total, heads_here, HD), position)
        .astype(jnp.bfloat16)
        .reshape(slot_total, inner_width)
    )
    latent_values = projected[2].astype(jnp.bfloat16)
    latent_pos = jnp.where(in_use, position, far_position)
    largest = jnp.full((heads_here, slot_total), -1e30, jnp.float32)
    piece_keys = lax.all_gather(latent_keys, "seq", axis=0, tiled=True)
    piece_values = lax.all_gather(latent_values, "seq", axis=0, tiled=True)
    piece_pos = lax.all_gather(shortened(latent_pos), "seq", axis=0, tiled=True)
    rows_here = piece_keys.shape[0]
    piece_scores = jnp.einsum(
        "qhd,khd->hqk",
        queries,
        piece_keys.reshape(rows_here, heads_here, HD),
        preferred_element_type=jnp.float32,
    ) * (1.0 / math.sqrt(HD))
    permitted = (piece_pos[None, :] <= position[:, None])[None]
    piece_scores = jnp.where(permitted, piece_scores, -1e30)
    renewed = jnp.maximum(largest, jnp.max(piece_scores, axis=-1))
    raised = jnp.where(permitted, jnp.exp(piece_scores - renewed[..., None]), 0.0)
    weight_sum = jnp.sum(raised, axis=-1)
    weighted = jnp.einsum(
        "hqk,khd->hqd",
        raised.astype(jnp.bfloat16),
        piece_values.reshape(rows_here, heads_here, HD),
        preferred_element_type=jnp.float32,
    )
    largest, weight_sum, weighted = (renewed, weight_sum, weighted)
    latent_heads = (
        (weighted / weight_sum[..., None])
        .transpose(1, 0, 2)
        .reshape(slot_total, inner_width)
        .astype(jnp.bfloat16)
    )
    partials = jnp.dot(
        latent_heads,
        lax.all_gather(lat_proj_out, "seq", axis=1, tiled=True),
        preferred_element_type=jnp.float32,
    )
    reduced = lax.psum_scatter(partials, "tp", scatter_dimension=1, tiled=True)
    latent = jnp.where(in_use[:, None], patches.astype(jnp.float32) + reduced, 0.0).astype(
        jnp.bfloat16
    )
    return (encoded, latent)


MESH = pl.DeviceIdType.MESH
EDGE = 16


def greet(peers):
    barrier = pltpu.get_barrier_semaphore()
    for peer in peers:
        pl.semaphore_signal(barrier, inc=1, device_id=peer, device_id_type=MESH)
    pl.semaphore_wait(barrier, len(peers))


def exchange(values, out_shapes, plan, call_id):
    n_in, n_out = len(values), len(out_shapes)
    n_copies = 16

    def kernel(*refs):
        ins, outs = refs[:n_in], refs[n_in : n_in + n_out]
        send_sems, recv_sems = refs[n_in + n_out :]
        rounds = plan()
        greet([source for source, _, _ in rounds])
        copies = []
        for _, target, items in rounds:
            for in_id, in_view, out_id, out_view in items:
                copy = pltpu.make_async_remote_copy(
                    src_ref=in_view(ins[in_id]),
                    dst_ref=out_view(outs[out_id]),
                    send_sem=send_sems.at[len(copies)],
                    recv_sem=recv_sems.at[len(copies)],
                    device_id=target,
                    device_id_type=MESH,
                )
                copy.start()
                copies.append(copy)
        for copy in copies:
            copy.wait()

    return pl.pallas_call(
        kernel,
        out_shape=out_shapes,
        in_specs=[pl.BlockSpec(memory_space=pl.ANY)] * n_in,
        out_specs=[pl.BlockSpec(memory_space=pl.ANY)] * n_out,
        scratch_shapes=[
            pltpu.SemaphoreType.DMA((n_copies,)),
            pltpu.SemaphoreType.DMA((n_copies,)),
        ],
        compiler_params=pltpu.CompilerParams(collective_id=call_id, has_side_effects=True),
    )(*values)


def whole(ref):
    return ref


def slot(index):
    return lambda ref: ref.at[index]


def seq_peer(index):
    return {"seq": index}


def tp_peer(index):
    return {"tp": index}


def relay(value, count, spread, plane_first, call_id):
    block = value.shape[1:] if spread else value.shape

    def kernel(value_ref, out_ref, land, send_a, recv_a, send_b, recv_b, own_sem):
        s, t = lax.axis_index("seq"), lax.axis_index("tp")
        p, c = s // 2, lax.rem(s, 2)

        def plane(index):
            return {"seq": 2 * index + c}

        if plane_first:
            a, b, first, second = p, t, plane, tp_peer
        else:
            a, b, first, second = t, p, tp_peer, plane
        others_a = [lax.rem(a + k, count) for k in range(1, count)]
        others_b = [lax.rem(b + k, count) for k in range(1, count)]
        greet([first(i) for i in others_a] + [second(i) for i in others_b])
        hops = []
        for k in range(1, count):
            target = lax.rem(a + k, count)
            hop = pltpu.make_async_remote_copy(
                src_ref=value_ref.at[target] if spread else value_ref,
                dst_ref=land.at[k - 1],
                send_sem=send_a.at[k - 1],
                recv_sem=recv_a.at[k - 1],
                device_id=first(target),
                device_id_type=MESH,
            )
            hop.start()
            hops.append(hop)
        onward = []
        for k in range(count):
            origin = lax.rem(a + count - k, count)
            if k == 0:
                here = value_ref.at[a] if spread else value_ref
            else:
                hops[k - 1].wait_recv()
                here = land.at[k - 1]
            away = pltpu.make_async_remote_copy(
                src_ref=here,
                dst_ref=out_ref.at[b],
                send_sem=send_b.at[k],
                recv_sem=recv_b.at[b],
                device_id=second(origin),
                device_id_type=MESH,
            )
            stay = pltpu.make_async_copy(here, out_ref.at[b], own_sem)
            onward.append((origin, away, stay))

            @pl.when(origin != b)
            def _():
                away.start()

            @pl.when(origin == b)
            def _():
                stay.start()

        for q in range(count):

            @pl.when(b != q)
            def _():
                pltpu.make_async_remote_copy(
                    src_ref=land.at[0],
                    dst_ref=out_ref.at[q],
                    send_sem=send_b.at[q],
                    recv_sem=recv_b.at[q],
                    device_id=second(b),
                    device_id_type=MESH,
                ).wait_recv()

        for hop in hops:
            hop.wait_send()
        for origin, away, stay in onward:

            @pl.when(origin != b)
            def _():
                away.wait_send()

            @pl.when(origin == b)
            def _():
                stay.wait()

    return pl.pallas_call(
        kernel,
        out_shape=jax.ShapeDtypeStruct((count, *block), value.dtype),
        in_specs=[pl.BlockSpec(memory_space=pltpu.VMEM)],
        out_specs=pl.BlockSpec(memory_space=pl.ANY),
        scratch_shapes=[
            pltpu.VMEM((count - 1, *block), value.dtype),
            pltpu.SemaphoreType.DMA((count - 1,)),
            pltpu.SemaphoreType.DMA((count - 1,)),
            pltpu.SemaphoreType.DMA((count,)),
            pltpu.SemaphoreType.DMA((count,)),
            pltpu.SemaphoreType.DMA,
        ],
        compiler_params=pltpu.CompilerParams(collective_id=call_id, has_side_effects=True),
    )(value)


def like(shape, dtype=jnp.bfloat16):
    return jax.ShapeDtypeStruct(shape, dtype)


def halo(projected, byte_states, info):
    size = lax.axis_size("seq")
    rows, width = projected.shape[1:]
    reach = WIN // rows

    def plan():
        s = lax.axis_index("seq")
        rounds = []
        for k in range(1, size):
            items = []
            if k <= reach:
                items.append((0, lambda ref: ref.at[pl.ds(1, 2)], 0, slot(k - 1)))
            if k == size - 1:
                items.append((0, lambda ref: ref.at[:, pl.ds(0, EDGE)], 1, whole))
                items.append((1, lambda ref: ref.at[pl.ds(0, EDGE)], 2, whole))
            items.append((2, whole, 3, slot(k - 1)))
            rounds.append(
                (seq_peer(lax.rem(s + size - k, size)), seq_peer(lax.rem(s + k, size)), items)
            )
        return rounds

    return exchange(
        [projected, byte_states, info],
        [
            like((reach, 2, rows, width)),
            like((3, EDGE, width)),
            like((EDGE, byte_states.shape[1])),
            like((size - 1, 8, 128), jnp.int32),
        ],
        plan,
        1,
    )


def encode_and_patch(
    projected, behind, edge, proj, byte_states, edge_states, bounds, used, lift, cross_kv, call_id
):
    count = lax.axis_size("tp")
    byte_rows, width = byte_states.shape
    share = byte_rows // count
    chunks = 2
    piece = share // chunks
    slots = bounds[0].shape[0]
    columns = lift.shape[1]
    total_rows = byte_rows + EDGE
    reach = behind.shape[0]

    def kernel(
        own_ref, behind_ref, next_ref, proj_ref, states_ref, edge_ref, lo_ref, hi_ref, used_ref,
        lift_hbm, cross_hbm,
        enc_ref, patch_ref,
        sends, lands, tail_send, tail_land, blocks, lift_ref, cross_ref, pooled_ref, full_ref,
        load_sems, rs_send, rs_recv, tail_s, tail_r, up_send, down_send, ag_recv,
    ):
        t = lax.axis_index("tp")
        loads = [
            pltpu.make_async_copy(lift_hbm, lift_ref, load_sems.at[0]),
            pltpu.make_async_copy(cross_hbm, cross_ref, load_sems.at[1]),
        ]
        for load in loads:
            load.start()
        key_rows, value_rows = (
            jnp.concatenate(
                [behind_ref[k, i] for k in range(reach - 1, -1, -1)]
                + [own_ref[i + 1], next_ref[i + 1]],
                axis=0,
            )
            for i in range(2)
        )
        query_rows = jnp.concatenate([own_ref[0], next_ref[0]], axis=0)
        reach_shape = (total_rows, WIN + total_rows)
        query_at = lax.broadcasted_iota(jnp.int32, reach_shape, 0)
        key_at = lax.broadcasted_iota(jnp.int32, reach_shape, 1) - WIN
        near = (
            (key_at <= query_at)
            & (key_at > query_at - WIN)
            & (key_at >= -lax.axis_index("seq") * byte_rows)
        )
        head_of = lax.broadcasted_iota(jnp.int32, query_rows.shape, 1) // EH
        attended = jnp.zeros(query_rows.shape, jnp.float32)
        for head in range(query_rows.shape[1] // EH):
            scores = lax.dot_general(
                jnp.where(head_of == head, query_rows, jnp.zeros_like(query_rows)),
                key_rows,
                (((1,), (1,)), ((), ())),
                preferred_element_type=jnp.float32,
            ) * (1.0 / math.sqrt(EH))
            weights = masked_softmax(scores, near).astype(jnp.bfloat16)
            seen = jnp.dot(weights, value_rows, preferred_element_type=jnp.float32)
            attended = jnp.where(head_of == head, seen, attended)
        blend = jnp.dot(
            attended.astype(jnp.bfloat16), proj_ref[...], preferred_element_type=jnp.float32
        ).astype(jnp.bfloat16)
        for q in range(count):
            for h in range(chunks):
                begin = q * share + h * piece
                sends[q, h] = blend[begin : begin + piece]
        tail_send[...] = blend[byte_rows:]
        greet([tp_peer(lax.rem(t + k, count)) for k in range(1, count)])
        scatter = [[], []]
        for h in range(chunks):
            for k in range(1, count):
                target = lax.rem(t + k, count)
                copy = pltpu.make_async_remote_copy(
                    src_ref=sends.at[target, h],
                    dst_ref=lands.at[h, k - 1],
                    send_sem=rs_send.at[h, k - 1],
                    recv_sem=rs_recv.at[h, k - 1],
                    device_id=tp_peer(target),
                    device_id_type=MESH,
                )
                copy.start()
                scatter[h].append(copy)
        tails = []
        for k in range(1, count):
            copy = pltpu.make_async_remote_copy(
                src_ref=tail_send,
                dst_ref=tail_land.at[k - 1],
                send_sem=tail_s.at[k - 1],
                recv_sem=tail_r.at[k - 1],
                device_id=tp_peer(lax.rem(t + k, count)),
                device_id_type=MESH,
            )
            copy.start()
            tails.append(copy)

        def pass_on(origin, h, up):
            step = 1 if up else -1
            return pltpu.make_async_remote_copy(
                src_ref=blocks.at[origin, h],
                dst_ref=blocks.at[origin, h],
                send_sem=(up_send if up else down_send).at[origin, h],
                recv_sem=ag_recv.at[origin, h],
                device_id=tp_peer(lax.rem(t + step + count, count)),
                device_id_type=MESH,
            )

        for h in range(chunks):
            for copy in scatter[h]:
                copy.wait_recv()
            total = sends[t, h].astype(jnp.float32)
            for k in range(count - 1):
                total = total + lands[h, k].astype(jnp.float32)
            rows = pl.ds(pl.multiple_of(t * share + h * piece, piece), piece)
            blocks[t, h] = (states_ref[rows].astype(jnp.float32) + total).astype(jnp.bfloat16)

            @pl.when(t < count - 1)
            def _():
                pass_on(t, h, True).start()

            @pl.when(t > 0)
            def _():
                pass_on(t, h, False).start()

        for copy in tails:
            copy.wait_recv()
        total = tail_send[...].astype(jnp.float32)
        for k in range(count - 1):
            total = total + tail_land[k].astype(jnp.float32)
        full_ref[byte_rows:] = (edge_ref[...].astype(jnp.float32) + total).astype(jnp.bfloat16)

        for d in range(1, count):
            for h in range(chunks):

                @pl.when(t - d >= 0)
                def _():
                    pass_on(t - d, h, True).wait_recv()

                    @pl.when(t < count - 1)
                    def _():
                        pass_on(t - d, h, True).start()

                @pl.when(t + d < count)
                def _():
                    pass_on(t + d, h, False).wait_recv()

                    @pl.when(t > 0)
                    def _():
                        pass_on(t + d, h, False).start()

        for q in range(count):
            for h in range(chunks):
                begin = q * share + h * piece
                full_ref[begin : begin + piece] = blocks[q, h]
                enc_ref[begin : begin + piece] = blocks[q, h]
        for load in loads:
            load.wait()

        where_at = lax.broadcasted_iota(jnp.int32, (slots, total_rows), 1)
        allowed = (where_at >= lo_ref[...]) & (where_at < hi_ref[...])
        in_use = used_ref[...] > 0.0
        member = jnp.where(allowed & in_use, 1.0, 0.0)
        lengths = jnp.maximum(jnp.sum(member, axis=1, keepdims=True), 1.0)
        totals = jnp.dot(
            member.astype(jnp.bfloat16), full_ref[...], preferred_element_type=jnp.float32
        )
        pooled_ref[...] = (totals / lengths).astype(jnp.bfloat16)
        group = 2 * HD

        def heads(i, carry):
            cols = pl.ds(pl.multiple_of(i * group, group), group)
            rows = full_ref[...]
            lifted = jnp.dot(pooled_ref[...], lift_ref[:, cols], preferred_element_type=jnp.float32)
            keys = jnp.dot(rows, cross_ref[0, :, cols], preferred_element_type=jnp.float32).astype(
                jnp.bfloat16
            )
            values = jnp.dot(
                rows, cross_ref[1, :, cols], preferred_element_type=jnp.float32
            ).astype(jnp.bfloat16)
            queries = lifted.astype(jnp.bfloat16)
            crossed = []
            for j in range(2):
                lanes = slice(j * HD, (j + 1) * HD)
                scores = lax.dot_general(
                    queries[:, lanes],
                    keys[:, lanes],
                    (((1,), (1,)), ((), ())),
                    preferred_element_type=jnp.float32,
                ) * (1.0 / math.sqrt(HD))
                weights = masked_softmax(scores, allowed).astype(jnp.bfloat16)
                crossed.append(
                    jnp.dot(weights, values[:, lanes], preferred_element_type=jnp.float32)
                )
            patch = lifted + jnp.concatenate(crossed, axis=1)
            patch_ref[:, cols] = jnp.where(in_use, patch, 0.0).astype(jnp.bfloat16)
            return carry

        lax.fori_loop(0, columns // group, heads, 0)

        for h in range(chunks):
            for copy in scatter[h]:
                copy.wait_send()
        for copy in tails:
            copy.wait_send()
        for q in range(count):
            for h in range(chunks):

                @pl.when((q <= t) & (t < count - 1))
                def _():
                    pass_on(q, h, True).wait_send()

                @pl.when((q >= t) & (t > 0))
                def _():
                    pass_on(q, h, False).wait_send()

    vmem = pl.BlockSpec(memory_space=pltpu.VMEM)
    hbm = pl.BlockSpec(memory_space=pl.ANY)
    dma = pltpu.SemaphoreType.DMA
    return pl.pallas_call(
        kernel,
        out_shape=[like((byte_rows, width)), like((slots, columns))],
        in_specs=[vmem] * 9 + [hbm] * 2,
        out_specs=[vmem, vmem],
        scratch_shapes=[
            pltpu.VMEM((count, chunks, piece, width), jnp.bfloat16),
            pltpu.VMEM((chunks, count - 1, piece, width), jnp.bfloat16),
            pltpu.VMEM((EDGE, width), jnp.bfloat16),
            pltpu.VMEM((count - 1, EDGE, width), jnp.bfloat16),
            pltpu.VMEM((count, chunks, piece, width), jnp.bfloat16),
            pltpu.VMEM(lift.shape, lift.dtype),
            pltpu.VMEM(cross_kv.shape, cross_kv.dtype),
            pltpu.VMEM((slots, width), jnp.bfloat16),
            pltpu.VMEM((total_rows, width), jnp.bfloat16),
            dma((2,)),
            dma((chunks, count - 1)),
            dma((chunks, count - 1)),
            dma((count - 1,)),
            dma((count - 1,)),
            dma((count, chunks)),
            dma((count, chunks)),
            dma((count, chunks)),
        ],
        compiler_params=pltpu.CompilerParams(collective_id=call_id, has_side_effects=True),
    )(projected, behind, edge, proj, byte_states, edge_states, *bounds, used, lift, cross_kv)


def latent_stage(rows, patches, used, gain, weights, projs, cosine, sine, query_pos, key_pos, call_id):
    count = lax.axis_size("tp")
    row_total, chip_width = rows.shape
    half = chip_width // 2
    slots, columns = patches.shape
    full_width = columns * count

    def kernel(
        rows_ref, patch_ref, used_ref, gain_ref, cos_ref, sin_ref, qpos_ref, kpos_ref,
        w_own_hbm, w_other_hbm, o_own_hbm, o_other_hbm,
        out_ref,
        w_own, w_other, o_own, o_other, geared, qkv_send, qkv_land, sq_send, sq_land,
        kv_own, kv_other, att_all, parts, land, final,
        load_sems, qkv_s, qkv_r, sq_s, sq_r, kv_sems, att_s, att_r, a_s, a_r, b_s, b_r,
    ):
        s, t = lax.axis_index("seq"), lax.axis_index("tp")
        p, c = s // 2, lax.rem(s, 2)
        pair_refs = ((w_own_hbm, w_own), (w_other_hbm, w_other), (o_own_hbm, o_own), (o_other_hbm, o_other))
        loads = [
            pltpu.make_async_copy(source, target, load_sems.at[i])
            for i, (source, target) in enumerate(pair_refs)
        ]
        for load in loads:
            load.start()

        def plane(index):
            return {"seq": 2 * index + c}

        partner = seq_peer(s + 1 - 2 * c)
        greet(
            [plane(lax.rem(p + k, count)) for k in range(1, count)]
            + [tp_peer(lax.rem(t + k, count)) for k in range(1, count)]
            + [partner]
        )

        def send(source, target, send_sem, recv_sem, device):
            return pltpu.make_async_remote_copy(
                src_ref=source,
                dst_ref=target,
                send_sem=send_sem,
                recv_sem=recv_sem,
                device_id=device,
                device_id_type=MESH,
            )

        values = rows_ref[...].astype(jnp.float32)
        squares = jnp.sum(values * values, axis=1, keepdims=True)
        eye = lax.broadcasted_iota(jnp.int32, (row_total, row_total), 0) == lax.broadcasted_iota(
            jnp.int32, (row_total, row_total), 1
        )
        flat = jnp.sum(jnp.where(eye, squares, 0.0), axis=0, keepdims=True)
        sq_send[...] = jnp.broadcast_to(flat, sq_send.shape)
        geared[...] = (values * gain_ref[...]).astype(jnp.bfloat16)
        sent = []
        for k in range(1, count):
            copy = send(
                sq_send, sq_land.at[k - 1], sq_s.at[k - 1], sq_r.at[k - 1], plane(lax.rem(p + k, count))
            )
            copy.start()
            sent.append(copy)
        loads[0].wait()
        loads[1].wait()
        mine = geared[:, pl.ds(pl.multiple_of(c * half, half), half)]
        theirs = geared[:, pl.ds(pl.multiple_of((1 - c) * half, half), half)]
        total = []
        for k in list(range(1, count)) + [0]:
            target = lax.rem(p + k, count)
            lanes = pl.ds(pl.multiple_of(target * HD, HD), HD)
            for i in range(3):
                part = jnp.dot(
                    mine, w_own[i, :, lanes], preferred_element_type=jnp.float32
                ) + jnp.dot(theirs, w_other[i, :, lanes], preferred_element_type=jnp.float32)
                if k:
                    qkv_send[k - 1, i] = part.astype(jnp.bfloat16)
                else:
                    total.append(part)
            if k:
                copy = send(
                    qkv_send.at[k - 1], qkv_land.at[k - 1], qkv_s.at[k - 1], qkv_r.at[k - 1], plane(target)
                )
                copy.start()
                sent.append(copy)
        for copy in sent:
            copy.wait_recv()
        flat = flat + jnp.sum(sq_land[:, 0:1, :], axis=0)
        square_sum = jnp.sum(jnp.where(eye, flat, 0.0), axis=1, keepdims=True)
        scale = lax.rsqrt(square_sum / full_width + epsilon)
        for i in range(3):
            for k in range(count - 1):
                total[i] = total[i] + qkv_land[k, i].astype(jnp.float32)
            total[i] = total[i] * scale

        def turned(vectors):
            return (
                vectors * cos_ref[...] + pltpu.roll(vectors, HD // 2, 1) * sin_ref[...]
            ).astype(jnp.bfloat16)

        queries = turned(total[0])
        kv_own[0] = turned(total[1])
        kv_own[1] = total[2].astype(jnp.bfloat16)
        swap = send(kv_own, kv_other, kv_sems.at[0], kv_sems.at[1], partner)
        swap.start()

        def scored(keys, first):
            scores = lax.dot_general(
                queries, keys, (((1,), (1,)), ((), ())), preferred_element_type=jnp.float32
            ) * (1.0 / math.sqrt(HD))
            permitted = kpos_ref[:, first : first + row_total] <= qpos_ref[...]
            return jnp.where(permitted, scores, -1e30), permitted

        scores_a, permitted_a = scored(kv_own[0], 0)
        swap.wait_recv()
        scores_b, permitted_b = scored(kv_other[0], row_total)
        largest = jnp.maximum(
            jnp.max(scores_a, axis=1, keepdims=True), jnp.max(scores_b, axis=1, keepdims=True)
        )
        raised_a = jnp.where(permitted_a, jnp.exp(scores_a - largest), 0.0)
        raised_b = jnp.where(permitted_b, jnp.exp(scores_b - largest), 0.0)
        weight_sum = jnp.sum(raised_a, axis=1, keepdims=True) + jnp.sum(
            raised_b, axis=1, keepdims=True
        )
        weighted = jnp.dot(
            raised_a.astype(jnp.bfloat16), kv_own[1], preferred_element_type=jnp.float32
        ) + jnp.dot(raised_b.astype(jnp.bfloat16), kv_other[1], preferred_element_type=jnp.float32)
        att_all[p] = (weighted / weight_sum).astype(jnp.bfloat16)
        heads = []
        for k in range(1, count):
            copy = send(
                att_all.at[p], att_all.at[p], att_s.at[k - 1], att_r.at[p], plane(lax.rem(p + k, count))
            )
            copy.start()
            heads.append(copy)
        for k in range(1, count):
            source = lax.rem(p + k, count)
            send(
                att_all.at[source], att_all.at[source], att_s.at[k - 1], att_r.at[source], plane(source)
            ).wait_recv()
        loads[2].wait()
        loads[3].wait()
        hops = []
        for k in list(range(1, count)) + [0]:
            target = lax.rem(p + k, count)
            take = pl.ds(pl.multiple_of(target * slots, slots), slots)
            attended = jnp.concatenate([att_all[j, take, :] for j in range(count)], axis=1)
            for output, core in ((o_own, c), (o_other, 1 - c)):
                parts[target, :, pl.ds(pl.multiple_of(core * half, half), half)] = jnp.dot(
                    attended, output[...], preferred_element_type=jnp.float32
                ).astype(jnp.bfloat16)
            if k:
                hop = send(
                    parts.at[target], land.at[k - 1], a_s.at[k - 1], a_r.at[k - 1], plane(target)
                )
                hop.start()
                hops.append(hop)
        onward = []
        for k in range(count):
            origin = lax.rem(p + count - k, count)
            if k == 0:
                here = parts.at[p]
            else:
                hops[k - 1].wait_recv()
                here = land.at[k - 1]
            away = send(here, final.at[t], b_s.at[k], b_r.at[t], tp_peer(origin))
            onward.append((origin, away))

            @pl.when(origin != t)
            def _():
                away.start()

            @pl.when(origin == t)
            def _():
                final[t] = here[...]

        summed = patch_ref[...].astype(jnp.float32)
        for q in range(count):

            @pl.when(t != q)
            def _():
                send(land.at[0], final.at[q], b_s.at[q], b_r.at[q], tp_peer(t)).wait_recv()

            summed = summed + final[q].astype(jnp.float32)
        out_ref[...] = jnp.where(used_ref[...] > 0.0, summed, 0.0).astype(jnp.bfloat16)
        for copy in sent + heads + hops + [swap]:
            copy.wait_send()
        for origin, away in onward:

            @pl.when(origin != t)
            def _():
                away.wait_send()

    vmem = pl.BlockSpec(memory_space=pltpu.VMEM)
    hbm = pl.BlockSpec(memory_space=pl.ANY)
    dma = pltpu.SemaphoreType.DMA
    near = count - 1
    return pl.pallas_call(
        kernel,
        out_shape=like((slots, columns)),
        in_specs=[vmem] * 8 + [hbm] * 4,
        out_specs=vmem,
        scratch_shapes=[
            pltpu.VMEM(weights[0].shape, jnp.bfloat16),
            pltpu.VMEM(weights[1].shape, jnp.bfloat16),
            pltpu.VMEM(projs[0].shape, jnp.bfloat16),
            pltpu.VMEM(projs[1].shape, jnp.bfloat16),
            pltpu.VMEM((row_total, chip_width), jnp.bfloat16),
            pltpu.VMEM((near, 3, row_total, HD), jnp.bfloat16),
            pltpu.VMEM((near, 3, row_total, HD), jnp.bfloat16),
            pltpu.VMEM((8, row_total), jnp.float32),
            pltpu.VMEM((near, 8, row_total), jnp.float32),
            pltpu.VMEM((2, row_total, HD), jnp.bfloat16),
            pltpu.VMEM((2, row_total, HD), jnp.bfloat16),
            pltpu.VMEM((count, row_total, HD), jnp.bfloat16),
            pltpu.VMEM((count, slots, columns), jnp.bfloat16),
            pltpu.VMEM((near, slots, columns), jnp.bfloat16),
            pltpu.VMEM((count, slots, columns), jnp.bfloat16),
            dma((4,)),
            dma((near,)),
            dma((near,)),
            dma((near,)),
            dma((near,)),
            dma((2,)),
            dma((near,)),
            dma((count,)),
            dma((near,)),
            dma((near,)),
            dma((count,)),
            dma((count,)),
        ],
        compiler_params=pltpu.CompilerParams(collective_id=call_id, has_side_effects=True),
    )(rows, patches, used, gain, cosine, sine, query_pos, key_pos, *weights, *projs)


def shards(
    byte_states,
    enc_gain,
    enc_qkv,
    enc_proj_out,
    starts,
    counts,
    lift,
    cross_kv,
    latent_gain,
    lat_qkv,
    lat_proj_out,
):
    size, tp_size = lax.axis_size("seq"), lax.axis_size("tp")
    s, t = lax.axis_index("seq"), lax.axis_index("tp")
    pairs = size // 2
    p, c = s // 2, lax.rem(s, 2)
    byte_rows = byte_states.shape[0]
    anchor = s * byte_rows
    both = [(i, i ^ 1) for i in range(size)]
    lat_qkv_other = lax.ppermute(lat_qkv, "seq", both)
    lat_proj_other = lax.ppermute(lat_proj_out, "seq", both)
    states = byte_states.astype(jnp.float32)
    normed = rms_scale(states, enc_gain.astype(jnp.float32)).astype(jnp.bfloat16)
    projected = jnp.einsum(
        "bd,idc->ibc", normed, enc_qkv, preferred_element_type=jnp.float32
    ).astype(jnp.bfloat16)
    patch_count = counts[0]
    local_starts = starts[0]
    lanes = lax.broadcasted_iota(jnp.int32, (8, 128), 1)
    info = jnp.where(lanes == 0, patch_count, jnp.where(lanes == 1, local_starts[0], 0))
    behind, edge, edge_states, infos = halo(projected, byte_states, info)
    recent = jnp.concatenate([info[None], infos], axis=0)
    ring = jnp.arange(size, dtype=jnp.int32)
    from_ring = lax.rem(s - ring + size, size)
    placed = from_ring[None, :] == ring[:, None]
    count_list = jnp.sum(jnp.where(placed, recent[None, :, 0, 0], 0), axis=1)
    offsets = jnp.sum(jnp.where(ring[None, :] < ring[:, None], count_list[None, :], 0), axis=1)
    next_first = jnp.where(s + 1 < size, recent[size - 1, 0, 1], size * byte_rows)

    slot_total = local_starts.shape[0]
    slot_ids = jnp.arange(slot_total, dtype=jnp.int32)
    in_use = slot_ids < patch_count
    following = jnp.concatenate([local_starts[1:], jnp.zeros((1,), jnp.int32)])
    patch_end = jnp.where(slot_ids + 1 < patch_count, following, next_first)
    lower = jnp.where(in_use, local_starts - anchor, 0)[:, None]
    upper = jnp.where(in_use, patch_end - anchor, 1)[:, None]
    used_rows = in_use.astype(jnp.float32)[:, None]
    encoded, patches = encode_and_patch(
        projected,
        behind,
        edge,
        enc_proj_out,
        byte_states,
        edge_states,
        (lower, upper),
        used_rows,
        lift,
        cross_kv,
        2,
    )

    def slots_of(core):
        members = 2 * jnp.arange(pairs, dtype=jnp.int32) + core
        hit = members[:, None] == ring[None, :]
        begin = jnp.sum(jnp.where(hit, offsets[None, :], 0), axis=1)
        used = jnp.sum(jnp.where(hit, count_list[None, :], 0), axis=1)
        position = (begin[:, None] + slot_ids[None, :]).reshape(-1)
        return position, (slot_ids[None, :] < used[:, None]).reshape(-1)

    position, rows_used = slots_of(c)
    other_position, other_used = slots_of(1 - c)

    rows = relay(patches, pairs, False, False, 4).reshape(pairs * slot_total, -1)
    half = rows.shape[1] // 2
    gain = lax.dynamic_slice_in_dim(latent_gain, p * 2 * half, 2 * half, 0).astype(jnp.float32)
    frequency = jnp.power(
        rope_base, -2.0 * jnp.arange(HD // 2, dtype=jnp.float32) / HD
    )
    angles = position.astype(jnp.float32)[:, None] * frequency[None, :]
    sine = jnp.sin(angles)
    cosine = jnp.cos(angles)
    key_position = jnp.concatenate(
        [
            jnp.where(rows_used, position, far_position),
            jnp.where(other_used, other_position, far_position),
        ]
    )
    latent = latent_stage(
        rows,
        patches,
        used_rows,
        gain[None],
        (lat_qkv, lat_qkv_other),
        (lat_proj_out, lat_proj_other),
        jnp.concatenate([cosine, cosine], axis=1),
        jnp.concatenate([-sine, sine], axis=1),
        position[:, None],
        key_position[None, :],
        5,
    )
    return (encoded, latent)


def fits_pairs(mesh, byte_states, enc_qkv, starts, lat_qkv):
    size, tp_size = mesh.shape["seq"], mesh.shape["tp"]
    byte_rows = byte_states.shape[0] // size
    return (
        size == 2 * tp_size
        and WIN % byte_rows == 0
        and WIN // byte_rows < size
        and byte_rows % (32 * tp_size) == 0
        and lat_qkv.shape[2] // tp_size == HD * tp_size
        and lat_qkv.shape[1] % (128 * size) == 0
        and starts.shape[1] * tp_size % 128 == 0
        and starts.shape[1] * tp_size <= 1024
        and starts.shape[1] % 16 == 0
        and enc_qkv.shape[2] % (128 * tp_size) == 0
    )


def solution(mesh):
    specs = dict(
        mesh=mesh,
        in_specs=(
            P("seq", None),
            P(),
            P(None, None, "tp"),
            P("tp", None),
            P("seq", None),
            P("seq"),
            P(None, "tp"),
            P(None, None, "tp"),
            P(),
            P(None, "seq", "tp"),
            P("tp", "seq"),
        ),
        out_specs=(P("seq", None), P("seq", "tp")),
        check_vma=False,
    )

    def run(*arrays):
        paired = fits_pairs(mesh, arrays[0], arrays[2], arrays[4], arrays[9])
        return jax.shard_map(shards if paired else gathered_shards, **specs)(*arrays)

    return run
```

```python
import math

import jax
import jax.numpy as jnp
from jax import lax
from jax.experimental import pallas as pl
from jax.experimental.pallas import tpu as pltpu
from jax.sharding import PartitionSpec as P

EH = 64
HD = 128
WIN = 512
SPILL = 8


epsilon = 1e-05
rope_base = 500000.0
far_position = 1 << 30


def from_behind(value, axis, steps):
    count = lax.axis_size(axis)
    leading, last = (max(0, -steps), min(count, count - steps))
    return lax.ppermute(value, axis, [(source, source + steps) for source in range(leading, last)])


def prefix(value, axis, join, neutral):
    count, mine = (lax.axis_size(axis), lax.axis_index(axis))
    pieces = lax.all_gather(value, axis)
    subtotal = jnp.full_like(value, 0) + jnp.asarray(neutral, value.dtype)

    def hop(position, subtotal):
        longer = join(subtotal, pieces[position])
        return jnp.where(position < mine, longer, subtotal)

    return lax.fori_loop(0, count - 1, hop, subtotal)


def shortened(value):

    def short(part):
        return part.astype(jnp.bfloat16) if part.dtype == jnp.float32 else part

    return jax.tree.map(short, value)


def rms_scale(values, gain_row):
    mean_square = jnp.mean(values * values, axis=-1, keepdims=True)
    return values * lax.rsqrt(mean_square + epsilon) * gain_row


def masked_softmax(scores, allowed):
    scores = jnp.where(allowed, scores, -1e30)
    largest = jnp.max(scores, axis=-1, keepdims=True)
    raised = jnp.where(allowed, jnp.exp(scores - largest), 0.0)
    return raised / jnp.sum(raised, axis=-1, keepdims=True)


def rotate(values, position):
    halfway = values.shape[-1] // 2
    frequency = jnp.power(
        rope_base, -2.0 * jnp.arange(halfway, dtype=jnp.float32) / values.shape[-1]
    )
    angles = position.astype(jnp.float32)[:, None] * frequency[None, :]
    cosine = jnp.cos(angles)[:, None, :]
    sine_rows = jnp.sin(angles)[:, None, :]
    lower_half = values[..., :halfway]
    upper_half = values[..., halfway:]
    return jnp.concatenate(
        [
            lower_half * cosine - upper_half * sine_rows,
            upper_half * cosine + lower_half * sine_rows,
        ],
        axis=-1,
    )


def patch_block(extended, first_byte, end_byte, in_use, anchor, lift, cross_kv):
    columns = anchor + jnp.arange(extended.shape[0], dtype=jnp.int32)
    inside = (
        (columns[None, :] >= first_byte[:, None])
        & (columns[None, :] < end_byte[:, None])
        & in_use[:, None]
    )
    member = inside.astype(jnp.bfloat16)
    totals = jnp.dot(member, extended, preferred_element_type=jnp.float32)
    lengths = jnp.maximum(jnp.sum(inside.astype(jnp.float32), axis=1), 1.0)
    pooled = (totals / lengths[:, None]).astype(jnp.bfloat16)
    lifted = jnp.dot(pooled, lift, preferred_element_type=jnp.float32)
    key_rows = jnp.dot(extended, cross_kv[0], preferred_element_type=jnp.float32).astype(
        jnp.bfloat16
    )
    value_rows = jnp.dot(extended, cross_kv[1], preferred_element_type=jnp.float32).astype(
        jnp.bfloat16
    )
    slot_total = first_byte.shape[0]
    head_count = lifted.shape[1] // HD
    queries = lifted.astype(jnp.bfloat16).reshape(slot_total, head_count, HD)
    scores = jnp.einsum(
        "phd,khd->hpk",
        queries,
        key_rows.reshape(-1, head_count, HD),
        preferred_element_type=jnp.float32,
    ) * (1.0 / math.sqrt(HD))
    allowed = inside | (~in_use)[:, None] & (columns[None, :] == anchor)
    weights = masked_softmax(scores, allowed[None]).astype(jnp.bfloat16)
    crossed = jnp.einsum(
        "hpk,khd->phd",
        weights,
        value_rows.reshape(-1, head_count, HD),
        preferred_element_type=jnp.float32,
    )
    crossed = crossed.reshape(slot_total, head_count * HD)
    return jnp.where(in_use[:, None], lifted + crossed, 0.0).astype(jnp.bfloat16)


def add_counts(earlier, later):
    return earlier + later


def gathered_shards(
    byte_states,
    enc_gain,
    enc_qkv,
    enc_proj_out,
    starts,
    counts,
    lift,
    cross_kv,
    latent_gain,
    lat_qkv,
    lat_proj_out,
):
    byte_rows = byte_states.shape[0]
    anchor = lax.axis_index("seq") * byte_rows
    states = byte_states.astype(jnp.float32)
    normed = rms_scale(states, enc_gain.astype(jnp.float32)).astype(jnp.bfloat16)
    projected = jnp.einsum(
        "bd,idc->ibc", normed, enc_qkv, preferred_element_type=jnp.float32
    ).astype(jnp.bfloat16)
    reach_blocks = max(WIN // byte_rows, 1)
    tail_rows = min(WIN, byte_rows)
    key_parts = []
    value_parts = []
    for distance in range(reach_blocks, 0, -1):
        moved_keys, moved_values = from_behind(
            (projected[1, byte_rows - tail_rows :], projected[2, byte_rows - tail_rows :]),
            "seq",
            distance,
        )
        key_parts.append(moved_keys)
        value_parts.append(moved_values)
    key_rows = jnp.concatenate(key_parts + [projected[1]], axis=0)
    value_rows = jnp.concatenate(value_parts + [projected[2]], axis=0)
    head_count = projected.shape[2] // EH
    scores = jnp.einsum(
        "qhd,khd->hqk",
        projected[0].reshape(byte_rows, head_count, EH),
        key_rows.reshape(-1, head_count, EH),
        preferred_element_type=jnp.float32,
    ) * (1.0 / math.sqrt(EH))
    query_pos = anchor + jnp.arange(byte_rows, dtype=jnp.int32)
    key_pos = anchor - WIN + jnp.arange(WIN + byte_rows, dtype=jnp.int32)
    allowed = (
        (key_pos[None, :] <= query_pos[:, None])
        & (key_pos[None, :] > query_pos[:, None] - WIN)
        & (key_pos[None, :] >= 0)
    )
    weights = masked_softmax(scores, allowed[None]).astype(jnp.bfloat16)
    attended = jnp.einsum(
        "hqk,khd->qhd",
        weights,
        value_rows.reshape(-1, head_count, EH),
        preferred_element_type=jnp.float32,
    )
    attended = attended.reshape(byte_rows, head_count * EH).astype(jnp.bfloat16)
    blended = lax.psum(jnp.dot(attended, enc_proj_out, preferred_element_type=jnp.float32), "tp")
    encoded = (states + blended).astype(jnp.bfloat16)
    patch_count = counts[0]
    local_starts = starts[0]
    first_local = (local_starts[0:1] - anchor).astype(jnp.bfloat16)
    next_rows, next_first = from_behind((encoded[:SPILL], first_local), "seq", -1)
    next_first = next_first.astype(jnp.int32)[0]
    extended = jnp.concatenate([encoded, next_rows], axis=0)
    slot_ids = jnp.arange(local_starts.shape[0], dtype=jnp.int32)
    in_use = slot_ids < patch_count
    following = jnp.concatenate([local_starts[1:], jnp.zeros((1,), jnp.int32)])
    patch_end = jnp.where(slot_ids + 1 < patch_count, following, anchor + byte_rows + next_first)
    patches = patch_block(extended, local_starts, patch_end, in_use, anchor, lift, cross_kv)
    offset = prefix(counts, "seq", add_counts, jnp.zeros((1,), jnp.int32))[0]
    position = offset + slot_ids
    slot_total = patches.shape[0]
    full_rows = lax.all_gather(patches, "tp", axis=1, tiled=True)
    normed_rows = rms_scale(full_rows.astype(jnp.float32), latent_gain.astype(jnp.float32)).astype(
        jnp.bfloat16
    )
    inner_width = lat_qkv.shape[2]
    projected = jnp.einsum(
        "pd,idc->ipc",
        normed_rows,
        lax.all_gather(lat_qkv, "seq", axis=1, tiled=True),
        preferred_element_type=jnp.float32,
    )
    heads_here = inner_width // HD
    queries = rotate(projected[0].reshape(slot_total, heads_here, HD), position).astype(
        jnp.bfloat16
    )
    latent_keys = (
        rotate(projected[1].reshape(slot_total, heads_here, HD), position)
        .astype(jnp.bfloat16)
        .reshape(slot_total, inner_width)
    )
    latent_values = projected[2].astype(jnp.bfloat16)
    latent_pos = jnp.where(in_use, position, far_position)
    largest = jnp.full((heads_here, slot_total), -1e30, jnp.float32)
    piece_keys = lax.all_gather(latent_keys, "seq", axis=0, tiled=True)
    piece_values = lax.all_gather(latent_values, "seq", axis=0, tiled=True)
    piece_pos = lax.all_gather(shortened(latent_pos), "seq", axis=0, tiled=True)
    rows_here = piece_keys.shape[0]
    piece_scores = jnp.einsum(
        "qhd,khd->hqk",
        queries,
        piece_keys.reshape(rows_here, heads_here, HD),
        preferred_element_type=jnp.float32,
    ) * (1.0 / math.sqrt(HD))
    permitted = (piece_pos[None, :] <= position[:, None])[None]
    piece_scores = jnp.where(permitted, piece_scores, -1e30)
    renewed = jnp.maximum(largest, jnp.max(piece_scores, axis=-1))
    raised = jnp.where(permitted, jnp.exp(piece_scores - renewed[..., None]), 0.0)
    weight_sum = jnp.sum(raised, axis=-1)
    weighted = jnp.einsum(
        "hqk,khd->hqd",
        raised.astype(jnp.bfloat16),
        piece_values.reshape(rows_here, heads_here, HD),
        preferred_element_type=jnp.float32,
    )
    largest, weight_sum, weighted = (renewed, weight_sum, weighted)
    latent_heads = (
        (weighted / weight_sum[..., None])
        .transpose(1, 0, 2)
        .reshape(slot_total, inner_width)
        .astype(jnp.bfloat16)
    )
    partials = jnp.dot(
        latent_heads,
        lax.all_gather(lat_proj_out, "seq", axis=1, tiled=True),
        preferred_element_type=jnp.float32,
    )
    reduced = lax.psum_scatter(partials, "tp", scatter_dimension=1, tiled=True)
    latent = jnp.where(in_use[:, None], patches.astype(jnp.float32) + reduced, 0.0).astype(
        jnp.bfloat16
    )
    return (encoded, latent)


MESH = pl.DeviceIdType.MESH
EDGE = 16


def greet(peers):
    barrier = pltpu.get_barrier_semaphore()
    for peer in peers:
        pl.semaphore_signal(barrier, inc=1, device_id=peer, device_id_type=MESH)
    pl.semaphore_wait(barrier, len(peers))


def exchange(values, out_shapes, plan, call_id):
    n_in, n_out = len(values), len(out_shapes)
    n_copies = 16

    def kernel(*refs):
        ins, outs = refs[:n_in], refs[n_in : n_in + n_out]
        send_sems, recv_sems = refs[n_in + n_out :]
        rounds = plan()
        greet([source for source, _, _ in rounds])
        copies = []
        for _, target, items in rounds:
            for in_id, in_view, out_id, out_view in items:
                copy = pltpu.make_async_remote_copy(
                    src_ref=in_view(ins[in_id]),
                    dst_ref=out_view(outs[out_id]),
                    send_sem=send_sems.at[len(copies)],
                    recv_sem=recv_sems.at[len(copies)],
                    device_id=target,
                    device_id_type=MESH,
                )
                copy.start()
                copies.append(copy)
        for copy in copies:
            copy.wait()

    return pl.pallas_call(
        kernel,
        out_shape=out_shapes,
        in_specs=[pl.BlockSpec(memory_space=pl.ANY)] * n_in,
        out_specs=[pl.BlockSpec(memory_space=pl.ANY)] * n_out,
        scratch_shapes=[
            pltpu.SemaphoreType.DMA((n_copies,)),
            pltpu.SemaphoreType.DMA((n_copies,)),
        ],
        compiler_params=pltpu.CompilerParams(collective_id=call_id, has_side_effects=True),
    )(*values)


def whole(ref):
    return ref


def slot(index):
    return lambda ref: ref.at[index]


def seq_peer(index):
    return {"seq": index}


def tp_peer(index):
    return {"tp": index}


def like(shape, dtype=jnp.bfloat16):
    return jax.ShapeDtypeStruct(shape, dtype)


def halo(projected, byte_states, info):
    size = lax.axis_size("seq")
    rows, width = projected.shape[1:]
    reach = WIN // rows

    def plan():
        s = lax.axis_index("seq")
        rounds = []
        for k in range(1, size):
            items = []
            if k <= reach:
                items.append((0, lambda ref: ref.at[pl.ds(1, 2)], 0, slot(k - 1)))
            if k == size - 1:
                items.append((0, lambda ref: ref.at[:, pl.ds(0, EDGE)], 1, whole))
                items.append((1, lambda ref: ref.at[pl.ds(0, EDGE)], 2, whole))
            items.append((2, whole, 3, slot(k - 1)))
            rounds.append(
                (seq_peer(lax.rem(s + size - k, size)), seq_peer(lax.rem(s + k, size)), items)
            )
        return rounds

    return exchange(
        [projected, byte_states, info],
        [
            like((reach, 2, rows, width)),
            like((3, EDGE, width)),
            like((EDGE, byte_states.shape[1])),
            like((size - 1, 8, 128), jnp.int32),
        ],
        plan,
        1,
    )


def encode_and_patch(
    projected, behind, edge, proj, byte_states, edge_states, bounds, used, lift, cross_kv, call_id
):
    count = lax.axis_size("tp")
    byte_rows, width = byte_states.shape
    share = byte_rows // count
    chunks = 2
    piece = share // chunks
    slots = bounds[0].shape[0]
    columns = lift.shape[1]
    total_rows = byte_rows + EDGE
    reach = behind.shape[0]
    group = 2 * HD
    panel_count = columns // group

    def kernel(
        own_ref, behind_ref, next_ref, proj_ref, states_ref, edge_ref, lo_ref, hi_ref, used_ref,
        lift_hbm, cross_hbm,
        enc_ref, patch_ref, rows_ref,
        sends, lands, tail_send, tail_land, blocks, lift_ref, cross_ref, pooled_ref, full_ref, panels, z_land,
        load_sems, rs_send, rs_recv, tail_s, tail_r, up_send, down_send, ag_recv,
        z_send, z_recv, plane_send, plane_recv, stay_sems,
    ):
        s, t = lax.axis_index("seq"), lax.axis_index("tp")
        p, c = s // 2, lax.rem(s, 2)

        def plane(index):
            return {"seq": 2 * index + c}

        loads = [
            pltpu.make_async_copy(lift_hbm, lift_ref, load_sems.at[0]),
            pltpu.make_async_copy(cross_hbm, cross_ref, load_sems.at[1]),
        ]
        for load in loads:
            load.start()
        key_rows, value_rows = (
            jnp.concatenate(
                [behind_ref[k, i] for k in range(reach - 1, -1, -1)]
                + [own_ref[i + 1], next_ref[i + 1]],
                axis=0,
            )
            for i in range(2)
        )
        query_rows = jnp.concatenate([own_ref[0], next_ref[0]], axis=0)
        reach_shape = (total_rows, WIN + total_rows)
        query_at = lax.broadcasted_iota(jnp.int32, reach_shape, 0)
        key_at = lax.broadcasted_iota(jnp.int32, reach_shape, 1) - WIN
        near = (
            (key_at <= query_at)
            & (key_at > query_at - WIN)
            & (key_at >= -lax.axis_index("seq") * byte_rows)
        )
        head_of = lax.broadcasted_iota(jnp.int32, query_rows.shape, 1) // EH
        attended = jnp.zeros(query_rows.shape, jnp.float32)
        for head in range(query_rows.shape[1] // EH):
            scores = lax.dot_general(
                jnp.where(head_of == head, query_rows, jnp.zeros_like(query_rows)),
                key_rows,
                (((1,), (1,)), ((), ())),
                preferred_element_type=jnp.float32,
            ) * (1.0 / math.sqrt(EH))
            weights = masked_softmax(scores, near).astype(jnp.bfloat16)
            seen = jnp.dot(weights, value_rows, preferred_element_type=jnp.float32)
            attended = jnp.where(head_of == head, seen, attended)
        blend = jnp.dot(
            attended.astype(jnp.bfloat16), proj_ref[...], preferred_element_type=jnp.float32
        ).astype(jnp.bfloat16)
        for q in range(count):
            for h in range(chunks):
                begin = q * share + h * piece
                sends[q, h] = blend[begin : begin + piece]
        tail_send[...] = blend[byte_rows:]
        greet(
            [tp_peer(lax.rem(t + k, count)) for k in range(1, count)]
            + [plane(lax.rem(p + k, count)) for k in range(1, count)]
        )
        scatter = [[], []]
        for h in range(chunks):
            for k in range(1, count):
                target = lax.rem(t + k, count)
                copy = pltpu.make_async_remote_copy(
                    src_ref=sends.at[target, h],
                    dst_ref=lands.at[h, k - 1],
                    send_sem=rs_send.at[h, k - 1],
                    recv_sem=rs_recv.at[h, k - 1],
                    device_id=tp_peer(target),
                    device_id_type=MESH,
                )
                copy.start()
                scatter[h].append(copy)
        tails = []
        for k in range(1, count):
            copy = pltpu.make_async_remote_copy(
                src_ref=tail_send,
                dst_ref=tail_land.at[k - 1],
                send_sem=tail_s.at[k - 1],
                recv_sem=tail_r.at[k - 1],
                device_id=tp_peer(lax.rem(t + k, count)),
                device_id_type=MESH,
            )
            copy.start()
            tails.append(copy)

        def pass_on(origin, h, up):
            step = 1 if up else -1
            return pltpu.make_async_remote_copy(
                src_ref=blocks.at[origin, h],
                dst_ref=blocks.at[origin, h],
                send_sem=(up_send if up else down_send).at[origin, h],
                recv_sem=ag_recv.at[origin, h],
                device_id=tp_peer(lax.rem(t + step + count, count)),
                device_id_type=MESH,
            )

        for h in range(chunks):
            for copy in scatter[h]:
                copy.wait_recv()
            total = sends[t, h].astype(jnp.float32)
            for k in range(count - 1):
                total = total + lands[h, k].astype(jnp.float32)
            rows = pl.ds(pl.multiple_of(t * share + h * piece, piece), piece)
            blocks[t, h] = (states_ref[rows].astype(jnp.float32) + total).astype(jnp.bfloat16)

            @pl.when(t < count - 1)
            def _():
                pass_on(t, h, True).start()

            @pl.when(t > 0)
            def _():
                pass_on(t, h, False).start()

        for copy in tails:
            copy.wait_recv()
        total = tail_send[...].astype(jnp.float32)
        for k in range(count - 1):
            total = total + tail_land[k].astype(jnp.float32)
        full_ref[byte_rows:] = (edge_ref[...].astype(jnp.float32) + total).astype(jnp.bfloat16)

        for d in range(1, count):
            for h in range(chunks):

                @pl.when(t - d >= 0)
                def _():
                    pass_on(t - d, h, True).wait_recv()

                    @pl.when(t < count - 1)
                    def _():
                        pass_on(t - d, h, True).start()

                @pl.when(t + d < count)
                def _():
                    pass_on(t + d, h, False).wait_recv()

                    @pl.when(t > 0)
                    def _():
                        pass_on(t + d, h, False).start()

        for q in range(count):
            for h in range(chunks):
                begin = q * share + h * piece
                full_ref[begin : begin + piece] = blocks[q, h]
                enc_ref[begin : begin + piece] = blocks[q, h]
        for load in loads:
            load.wait()

        where_at = lax.broadcasted_iota(jnp.int32, (slots, total_rows), 1)
        allowed = (where_at >= lo_ref[...]) & (where_at < hi_ref[...])
        in_use = used_ref[...] > 0.0
        member = jnp.where(allowed & in_use, 1.0, 0.0)
        lengths = jnp.maximum(jnp.sum(member, axis=1, keepdims=True), 1.0)
        totals = jnp.dot(
            member.astype(jnp.bfloat16), full_ref[...], preferred_element_type=jnp.float32
        )
        pooled_ref[...] = (totals / lengths).astype(jnp.bfloat16)

        def across(k, i):
            return pltpu.make_async_remote_copy(
                src_ref=panels.at[i],
                dst_ref=z_land.at[k - 1, i],
                send_sem=z_send.at[k - 1, i],
                recv_sem=z_recv.at[k - 1, i],
                device_id=tp_peer(lax.rem(t + k, count)),
                device_id_type=MESH,
            )

        def heads(i, carry):
            cols = pl.ds(pl.multiple_of(i * group, group), group)
            rows = full_ref[...]
            lifted = jnp.dot(pooled_ref[...], lift_ref[:, cols], preferred_element_type=jnp.float32)
            keys = jnp.dot(rows, cross_ref[0, :, cols], preferred_element_type=jnp.float32).astype(
                jnp.bfloat16
            )
            values = jnp.dot(
                rows, cross_ref[1, :, cols], preferred_element_type=jnp.float32
            ).astype(jnp.bfloat16)
            queries = lifted.astype(jnp.bfloat16)
            crossed = []
            for j in range(2):
                lanes = slice(j * HD, (j + 1) * HD)
                scores = lax.dot_general(
                    queries[:, lanes],
                    keys[:, lanes],
                    (((1,), (1,)), ((), ())),
                    preferred_element_type=jnp.float32,
                ) * (1.0 / math.sqrt(HD))
                weights = masked_softmax(scores, allowed).astype(jnp.bfloat16)
                crossed.append(
                    jnp.dot(weights, values[:, lanes], preferred_element_type=jnp.float32)
                )
            patch = lifted + jnp.concatenate(crossed, axis=1)
            panel = jnp.where(in_use, patch, 0.0).astype(jnp.bfloat16)
            patch_ref[:, cols] = panel
            panels[i] = panel
            for k in range(1, count):
                across(k, i).start()
            return carry

        lax.fori_loop(0, panel_count, heads, 0)
        onward = []
        for i in range(panel_count):
            for k in range(count):
                origin = lax.rem(t + count - k, count)
                if k == 0:
                    here = panels.at[i]
                else:
                    across(k, i).wait_recv()
                    here = z_land.at[k - 1, i]
                away = pltpu.make_async_remote_copy(
                    src_ref=here,
                    dst_ref=rows_ref.at[p, i],
                    send_sem=plane_send.at[k, i],
                    recv_sem=plane_recv.at[p, i],
                    device_id=plane(origin),
                    device_id_type=MESH,
                )
                stay = pltpu.make_async_copy(here, rows_ref.at[p, i], stay_sems.at[i])
                onward.append((origin, away, stay))

                @pl.when(origin != p)
                def _():
                    away.start()

                @pl.when(origin == p)
                def _():
                    stay.start()

        for q in range(count):

            @pl.when(p != q)
            def _():
                for i in range(panel_count):
                    pltpu.make_async_remote_copy(
                        src_ref=panels.at[i],
                        dst_ref=rows_ref.at[q, i],
                        send_sem=plane_send.at[q, i],
                        recv_sem=plane_recv.at[q, i],
                        device_id=plane(p),
                        device_id_type=MESH,
                    ).wait_recv()

        for i in range(panel_count):
            for k in range(1, count):
                across(k, i).wait_send()
        for origin, away, stay in onward:

            @pl.when(origin != p)
            def _():
                away.wait_send()

            @pl.when(origin == p)
            def _():
                stay.wait()

        for h in range(chunks):
            for copy in scatter[h]:
                copy.wait_send()
        for copy in tails:
            copy.wait_send()
        for q in range(count):
            for h in range(chunks):

                @pl.when((q <= t) & (t < count - 1))
                def _():
                    pass_on(q, h, True).wait_send()

                @pl.when((q >= t) & (t > 0))
                def _():
                    pass_on(q, h, False).wait_send()

    vmem = pl.BlockSpec(memory_space=pltpu.VMEM)
    hbm = pl.BlockSpec(memory_space=pl.ANY)
    dma = pltpu.SemaphoreType.DMA
    return pl.pallas_call(
        kernel,
        out_shape=[
            like((byte_rows, width)),
            like((slots, columns)),
            like((count, panel_count, slots, group)),
        ],
        in_specs=[vmem] * 9 + [hbm] * 2,
        out_specs=[vmem, vmem, hbm],
        scratch_shapes=[
            pltpu.VMEM((count, chunks, piece, width), jnp.bfloat16),
            pltpu.VMEM((chunks, count - 1, piece, width), jnp.bfloat16),
            pltpu.VMEM((EDGE, width), jnp.bfloat16),
            pltpu.VMEM((count - 1, EDGE, width), jnp.bfloat16),
            pltpu.VMEM((count, chunks, piece, width), jnp.bfloat16),
            pltpu.VMEM(lift.shape, lift.dtype),
            pltpu.VMEM(cross_kv.shape, cross_kv.dtype),
            pltpu.VMEM((slots, width), jnp.bfloat16),
            pltpu.VMEM((total_rows, width), jnp.bfloat16),
            pltpu.VMEM((panel_count, slots, group), jnp.bfloat16),
            pltpu.VMEM((count - 1, panel_count, slots, group), jnp.bfloat16),
            dma((2,)),
            dma((chunks, count - 1)),
            dma((chunks, count - 1)),
            dma((count - 1,)),
            dma((count - 1,)),
            dma((count, chunks)),
            dma((count, chunks)),
            dma((count, chunks)),
            dma((count - 1, panel_count)),
            dma((count - 1, panel_count)),
            dma((count, panel_count)),
            dma((count, panel_count)),
            dma((panel_count,)),
        ],
        compiler_params=pltpu.CompilerParams(collective_id=call_id, has_side_effects=True),
    )(projected, behind, edge, proj, byte_states, edge_states, *bounds, used, lift, cross_kv)


def latent_stage(rows, patches, used, gain, weights, projs, cosine, sine, query_pos, key_pos, call_id):
    count = lax.axis_size("tp")
    pair_count, panel_count, slot_count, group = rows.shape
    row_total, chip_width = pair_count * slot_count, panel_count * group
    half = chip_width // 2
    slots, columns = patches.shape
    full_width = columns * count

    def kernel(
        rows_ref, patch_ref, used_ref, gain_ref, cos_ref, sin_ref, qpos_ref, kpos_ref,
        w_own_hbm, w_other_hbm, o_own_hbm, o_other_hbm,
        out_ref,
        w_own, w_other, o_own, o_other, geared, qkv_send, qkv_land, sq_send, sq_land,
        kv_own, kv_other, att_all, parts, land, final,
        load_sems, qkv_s, qkv_r, sq_s, sq_r, kv_sems, att_s, att_r, a_s, a_r, b_s, b_r,
    ):
        s, t = lax.axis_index("seq"), lax.axis_index("tp")
        p, c = s // 2, lax.rem(s, 2)
        pair_refs = ((w_own_hbm, w_own), (w_other_hbm, w_other), (o_own_hbm, o_own), (o_other_hbm, o_other))
        loads = [
            pltpu.make_async_copy(source, target, load_sems.at[i])
            for i, (source, target) in enumerate(pair_refs)
        ]
        for load in loads:
            load.start()

        def plane(index):
            return {"seq": 2 * index + c}

        partner = seq_peer(s + 1 - 2 * c)
        greet(
            [plane(lax.rem(p + k, count)) for k in range(1, count)]
            + [tp_peer(lax.rem(t + k, count)) for k in range(1, count)]
            + [partner]
        )

        def send(source, target, send_sem, recv_sem, device):
            return pltpu.make_async_remote_copy(
                src_ref=source,
                dst_ref=target,
                send_sem=send_sem,
                recv_sem=recv_sem,
                device_id=device,
                device_id_type=MESH,
            )

        values = jnp.concatenate(
            [rows_ref[:, i].reshape(row_total, group) for i in range(panel_count)], axis=1
        ).astype(jnp.float32)
        squares = jnp.sum(values * values, axis=1, keepdims=True)
        eye = lax.broadcasted_iota(jnp.int32, (row_total, row_total), 0) == lax.broadcasted_iota(
            jnp.int32, (row_total, row_total), 1
        )
        flat = jnp.sum(jnp.where(eye, squares, 0.0), axis=0, keepdims=True)
        sq_send[...] = jnp.broadcast_to(flat, sq_send.shape)
        geared[...] = (values * gain_ref[...]).astype(jnp.bfloat16)
        sent = []
        for k in range(1, count):
            copy = send(
                sq_send, sq_land.at[k - 1], sq_s.at[k - 1], sq_r.at[k - 1], plane(lax.rem(p + k, count))
            )
            copy.start()
            sent.append(copy)
        loads[0].wait()
        loads[1].wait()
        mine = geared[:, pl.ds(pl.multiple_of(c * half, half), half)]
        theirs = geared[:, pl.ds(pl.multiple_of((1 - c) * half, half), half)]
        total = []
        for k in list(range(1, count)) + [0]:
            target = lax.rem(p + k, count)
            lanes = pl.ds(pl.multiple_of(target * HD, HD), HD)
            for i in range(3):
                part = jnp.dot(
                    mine, w_own[i, :, lanes], preferred_element_type=jnp.float32
                ) + jnp.dot(theirs, w_other[i, :, lanes], preferred_element_type=jnp.float32)
                if k:
                    qkv_send[k - 1, i] = part.astype(jnp.bfloat16)
                else:
                    total.append(part)
            if k:
                copy = send(
                    qkv_send.at[k - 1], qkv_land.at[k - 1], qkv_s.at[k - 1], qkv_r.at[k - 1], plane(target)
                )
                copy.start()
                sent.append(copy)
        for copy in sent:
            copy.wait_recv()
        flat = flat + jnp.sum(sq_land[:, 0:1, :], axis=0)
        square_sum = jnp.sum(jnp.where(eye, flat, 0.0), axis=1, keepdims=True)
        scale = lax.rsqrt(square_sum / full_width + epsilon)
        for i in range(3):
            for k in range(count - 1):
                total[i] = total[i] + qkv_land[k, i].astype(jnp.float32)
            total[i] = total[i] * scale

        def turned(vectors):
            return (
                vectors * cos_ref[...] + pltpu.roll(vectors, HD // 2, 1) * sin_ref[...]
            ).astype(jnp.bfloat16)

        queries = turned(total[0])
        kv_own[0] = turned(total[1])
        kv_own[1] = total[2].astype(jnp.bfloat16)
        swap = send(kv_own, kv_other, kv_sems.at[0], kv_sems.at[1], partner)
        swap.start()

        def scored(keys, first):
            scores = lax.dot_general(
                queries, keys, (((1,), (1,)), ((), ())), preferred_element_type=jnp.float32
            ) * (1.0 / math.sqrt(HD))
            permitted = kpos_ref[:, first : first + row_total] <= qpos_ref[...]
            return jnp.where(permitted, scores, -1e30), permitted

        scores_a, permitted_a = scored(kv_own[0], 0)
        swap.wait_recv()
        scores_b, permitted_b = scored(kv_other[0], row_total)
        largest = jnp.maximum(
            jnp.max(scores_a, axis=1, keepdims=True), jnp.max(scores_b, axis=1, keepdims=True)
        )
        raised_a = jnp.where(permitted_a, jnp.exp(scores_a - largest), 0.0)
        raised_b = jnp.where(permitted_b, jnp.exp(scores_b - largest), 0.0)
        weight_sum = jnp.sum(raised_a, axis=1, keepdims=True) + jnp.sum(
            raised_b, axis=1, keepdims=True
        )
        weighted = jnp.dot(
            raised_a.astype(jnp.bfloat16), kv_own[1], preferred_element_type=jnp.float32
        ) + jnp.dot(raised_b.astype(jnp.bfloat16), kv_other[1], preferred_element_type=jnp.float32)
        att_all[p] = (weighted / weight_sum).astype(jnp.bfloat16)
        heads = []
        for k in range(1, count):
            copy = send(
                att_all.at[p], att_all.at[p], att_s.at[k - 1], att_r.at[p], plane(lax.rem(p + k, count))
            )
            copy.start()
            heads.append(copy)
        for k in range(1, count):
            source = lax.rem(p + k, count)
            send(
                att_all.at[source], att_all.at[source], att_s.at[k - 1], att_r.at[source], plane(source)
            ).wait_recv()
        loads[2].wait()
        loads[3].wait()
        hops = []
        for k in list(range(1, count)) + [0]:
            target = lax.rem(p + k, count)
            take = pl.ds(pl.multiple_of(target * slots, slots), slots)
            attended = jnp.concatenate([att_all[j, take, :] for j in range(count)], axis=1)
            for output, core in ((o_own, c), (o_other, 1 - c)):
                parts[target, :, pl.ds(pl.multiple_of(core * half, half), half)] = jnp.dot(
                    attended, output[...], preferred_element_type=jnp.float32
                ).astype(jnp.bfloat16)
            if k:
                hop = send(
                    parts.at[target], land.at[k - 1], a_s.at[k - 1], a_r.at[k - 1], plane(target)
                )
                hop.start()
                hops.append(hop)
        onward = []
        for k in range(count):
            origin = lax.rem(p + count - k, count)
            if k == 0:
                here = parts.at[p]
            else:
                hops[k - 1].wait_recv()
                here = land.at[k - 1]
            away = send(here, final.at[t], b_s.at[k], b_r.at[t], tp_peer(origin))
            onward.append((origin, away))

            @pl.when(origin != t)
            def _():
                away.start()

            @pl.when(origin == t)
            def _():
                final[t] = here[...]

        summed = patch_ref[...].astype(jnp.float32)
        for q in range(count):

            @pl.when(t != q)
            def _():
                send(land.at[0], final.at[q], b_s.at[q], b_r.at[q], tp_peer(t)).wait_recv()

            summed = summed + final[q].astype(jnp.float32)
        out_ref[...] = jnp.where(used_ref[...] > 0.0, summed, 0.0).astype(jnp.bfloat16)
        for copy in sent + heads + hops + [swap]:
            copy.wait_send()
        for origin, away in onward:

            @pl.when(origin != t)
            def _():
                away.wait_send()

    vmem = pl.BlockSpec(memory_space=pltpu.VMEM)
    hbm = pl.BlockSpec(memory_space=pl.ANY)
    dma = pltpu.SemaphoreType.DMA
    near = count - 1
    return pl.pallas_call(
        kernel,
        out_shape=like((slots, columns)),
        in_specs=[vmem] * 8 + [hbm] * 4,
        out_specs=vmem,
        scratch_shapes=[
            pltpu.VMEM(weights[0].shape, jnp.bfloat16),
            pltpu.VMEM(weights[1].shape, jnp.bfloat16),
            pltpu.VMEM(projs[0].shape, jnp.bfloat16),
            pltpu.VMEM(projs[1].shape, jnp.bfloat16),
            pltpu.VMEM((row_total, chip_width), jnp.bfloat16),
            pltpu.VMEM((near, 3, row_total, HD), jnp.bfloat16),
            pltpu.VMEM((near, 3, row_total, HD), jnp.bfloat16),
            pltpu.VMEM((8, row_total), jnp.float32),
            pltpu.VMEM((near, 8, row_total), jnp.float32),
            pltpu.VMEM((2, row_total, HD), jnp.bfloat16),
            pltpu.VMEM((2, row_total, HD), jnp.bfloat16),
            pltpu.VMEM((count, row_total, HD), jnp.bfloat16),
            pltpu.VMEM((count, slots, columns), jnp.bfloat16),
            pltpu.VMEM((near, slots, columns), jnp.bfloat16),
            pltpu.VMEM((count, slots, columns), jnp.bfloat16),
            dma((4,)),
            dma((near,)),
            dma((near,)),
            dma((near,)),
            dma((near,)),
            dma((2,)),
            dma((near,)),
            dma((count,)),
            dma((near,)),
            dma((near,)),
            dma((count,)),
            dma((count,)),
        ],
        compiler_params=pltpu.CompilerParams(collective_id=call_id, has_side_effects=True),
    )(rows, patches, used, gain, cosine, sine, query_pos, key_pos, *weights, *projs)


def shards(
    byte_states,
    enc_gain,
    enc_qkv,
    enc_proj_out,
    starts,
    counts,
    lift,
    cross_kv,
    latent_gain,
    lat_qkv,
    lat_proj_out,
):
    size, tp_size = lax.axis_size("seq"), lax.axis_size("tp")
    s, t = lax.axis_index("seq"), lax.axis_index("tp")
    pairs = size // 2
    p, c = s // 2, lax.rem(s, 2)
    byte_rows = byte_states.shape[0]
    anchor = s * byte_rows
    both = [(i, i ^ 1) for i in range(size)]
    lat_qkv_other = lax.ppermute(lat_qkv, "seq", both)
    lat_proj_other = lax.ppermute(lat_proj_out, "seq", both)
    states = byte_states.astype(jnp.float32)
    normed = rms_scale(states, enc_gain.astype(jnp.float32)).astype(jnp.bfloat16)
    projected = jnp.einsum(
        "bd,idc->ibc", normed, enc_qkv, preferred_element_type=jnp.float32
    ).astype(jnp.bfloat16)
    patch_count = counts[0]
    local_starts = starts[0]
    lanes = lax.broadcasted_iota(jnp.int32, (8, 128), 1)
    info = jnp.where(lanes == 0, patch_count, jnp.where(lanes == 1, local_starts[0], 0))
    behind, edge, edge_states, infos = halo(projected, byte_states, info)
    recent = jnp.concatenate([info[None], infos], axis=0)
    ring = jnp.arange(size, dtype=jnp.int32)
    from_ring = lax.rem(s - ring + size, size)
    placed = from_ring[None, :] == ring[:, None]
    count_list = jnp.sum(jnp.where(placed, recent[None, :, 0, 0], 0), axis=1)
    offsets = jnp.sum(jnp.where(ring[None, :] < ring[:, None], count_list[None, :], 0), axis=1)
    next_first = jnp.where(s + 1 < size, recent[size - 1, 0, 1], size * byte_rows)

    slot_total = local_starts.shape[0]
    slot_ids = jnp.arange(slot_total, dtype=jnp.int32)
    in_use = slot_ids < patch_count
    following = jnp.concatenate([local_starts[1:], jnp.zeros((1,), jnp.int32)])
    patch_end = jnp.where(slot_ids + 1 < patch_count, following, next_first)
    lower = jnp.where(in_use, local_starts - anchor, 0)[:, None]
    upper = jnp.where(in_use, patch_end - anchor, 1)[:, None]
    used_rows = in_use.astype(jnp.float32)[:, None]
    encoded, patches, rows = encode_and_patch(
        projected,
        behind,
        edge,
        enc_proj_out,
        byte_states,
        edge_states,
        (lower, upper),
        used_rows,
        lift,
        cross_kv,
        2,
    )

    def slots_of(core):
        members = 2 * jnp.arange(pairs, dtype=jnp.int32) + core
        hit = members[:, None] == ring[None, :]
        begin = jnp.sum(jnp.where(hit, offsets[None, :], 0), axis=1)
        used = jnp.sum(jnp.where(hit, count_list[None, :], 0), axis=1)
        position = (begin[:, None] + slot_ids[None, :]).reshape(-1)
        return position, (slot_ids[None, :] < used[:, None]).reshape(-1)

    position, rows_used = slots_of(c)
    other_position, other_used = slots_of(1 - c)

    half = lat_qkv.shape[1]
    gain = lax.dynamic_slice_in_dim(latent_gain, p * 2 * half, 2 * half, 0).astype(jnp.float32)
    frequency = jnp.power(
        rope_base, -2.0 * jnp.arange(HD // 2, dtype=jnp.float32) / HD
    )
    angles = position.astype(jnp.float32)[:, None] * frequency[None, :]
    sine = jnp.sin(angles)
    cosine = jnp.cos(angles)
    key_position = jnp.concatenate(
        [
            jnp.where(rows_used, position, far_position),
            jnp.where(other_used, other_position, far_position),
        ]
    )
    latent = latent_stage(
        rows,
        patches,
        used_rows,
        gain[None],
        (lat_qkv, lat_qkv_other),
        (lat_proj_out, lat_proj_other),
        jnp.concatenate([cosine, cosine], axis=1),
        jnp.concatenate([-sine, sine], axis=1),
        position[:, None],
        key_position[None, :],
        5,
    )
    return (encoded, latent)


def fits_pairs(mesh, byte_states, enc_qkv, starts, lat_qkv):
    size, tp_size = mesh.shape["seq"], mesh.shape["tp"]
    byte_rows = byte_states.shape[0] // size
    return (
        size == 2 * tp_size
        and WIN % byte_rows == 0
        and WIN // byte_rows < size
        and byte_rows % (32 * tp_size) == 0
        and lat_qkv.shape[2] // tp_size == HD * tp_size
        and lat_qkv.shape[1] % (128 * size) == 0
        and starts.shape[1] * tp_size % 128 == 0
        and starts.shape[1] * tp_size <= 1024
        and starts.shape[1] % 16 == 0
        and enc_qkv.shape[2] % (128 * tp_size) == 0
    )


def solution(mesh):
    specs = dict(
        mesh=mesh,
        in_specs=(
            P("seq", None),
            P(),
            P(None, None, "tp"),
            P("tp", None),
            P("seq", None),
            P("seq"),
            P(None, "tp"),
            P(None, None, "tp"),
            P(),
            P(None, "seq", "tp"),
            P("tp", "seq"),
        ),
        out_specs=(P("seq", None), P("seq", "tp")),
        check_vma=False,
    )

    def run(*arrays):
        paired = fits_pairs(mesh, arrays[0], arrays[2], arrays[4], arrays[9])
        return jax.shard_map(shards if paired else gathered_shards, **specs)(*arrays)

    return run
```
